128 devices in a mesh: grp: 16 (over y, z_lo, core), tile: 8 (over z_hi, x).
Axes of the slice: x: 4, y: 4, z: 4 (z_hi: 2, z_lo: 2; z = z_hi * 2 + z_lo), core: 2. Of those that a mesh axis runs over, the one named last changes fastest.
Arguments:
- parent_so2: float32 [4, 1024, 1024], P(None, 'grp', 'tile'), may hold values from 0.1 to 10
- wind_east: float32 [4, 1024, 1024], P(None, 'grp', 'tile'), may hold values from -0.2 to 0.2
- wind_north: float32 [4, 1024, 1024], P(None, 'grp', 'tile'), may hold values from -0.2 to 0.2
- diffusivity: float32 [4, 1024, 1024], P(None, 'grp', 'tile'), may hold values from 0.01 to 0.25
- nest_so2: float32 [16, 4, 320, 320], P('grp', None, 'tile'), may hold values from 0.1 to 10
- nest_rows: int32 [16], replicated, may hold values from 0 to 15, as said below
- nest_offset: int32 [16], replicated, may hold values from 1 to 31
- nest_left: int32 [16], replicated, may hold values from 1 to 991
- nest_height: int32 [16], replicated, may hold values from 16 to 32
- nest_width: int32 [16], replicated, may hold values from 16 to 32
Outputs:
- parent_next: float32 [4, 1024, 1024], P(None, 'grp', 'tile')
- nest_next: float32 [16, 4, 320, 320], P('grp', None, 'tile')
The draws below stay inside these ranges and needn't reach their ends.
Inputs may be any that keep to these rules, and one draw needn't show every extreme that they name: `nest_rows`: each of 0 to 15 appears once.
All inputs are finite; a program needn't handle non-finite values.
Results may differ from the reference program's by a relative error of at most 0.0001.
Values sent between devices are 32-bit elements; how exact they have to be, the bound alone decides.
No kernel may reach another device: no remote copies, remote signals or barrier semaphores. Data moves between devices by JAX's collectives and lax.ppermute only.
A program may use at most 64 MiB of HBM per device.

```python
import math
import jax
import jax.numpy as jnp
from jax import lax

LEV = 4
RATIO = 10
FRX = 32
FRY = 32
CPX = 64
NESTS = 16
PX = 1024
PY = 1024
NFX = 320
NFY = 320


def ragged_values(key, salt, lowest, highest):
    key_values = jax.random.fold_in(key, salt)
    key_high = jax.random.fold_in(key, salt + 1)
    key_low = jax.random.fold_in(key, salt + 2)
    values = jax.random.randint(key_values, (NESTS,), lowest, highest + 1)
    high_at = jax.random.randint(key_high, (), 0, NESTS)
    low_at = (high_at + 1 + jax.random.randint(key_low, (), 0, NESTS - 1)) % NESTS
    values = values.at[high_at].set(highest)
    values = values.at[low_at].set(lowest)
    return values.astype(jnp.int32)


def draw_nest_rows(key, part):
    key_start = jax.random.fold_in(key, 41)
    key_order = jax.random.fold_in(key, 42)
    start = jax.random.randint(key_start, (), 0, NESTS).astype(jnp.int32)
    fixed = jnp.array([NESTS - 1, 2, (2 + NESTS // 2) % NESTS], dtype=jnp.int32)
    targets = jnp.arange(NESTS, dtype=jnp.int32)
    taken = jnp.any(targets[:, None] == fixed[None, :], axis=1)
    scores = jnp.where(taken, NESTS + targets, targets).astype(jnp.int32)
    rest = jnp.argsort(scores, stable=True).astype(jnp.int32)[:NESTS - 3]
    shuffle = jax.random.permutation(key_order, NESTS - 3).astype(jnp.int32)
    relative = jnp.concatenate([fixed, rest[shuffle]], 0)
    places = (start + jnp.arange(NESTS, dtype=jnp.int32)) % NESTS
    values = (start + relative) % NESTS
    return jnp.zeros((NESTS,), jnp.int32).at[places].set(values).astype(jnp.int32)


def draw_nest_offset(key, part):
    return ragged_values(key, 11, 1, CPX - FRX - 1)


def draw_nest_height(key, part):
    return ragged_values(key, 21, FRX // 2, FRX)


def draw_nest_width(key, part):
    return ragged_values(key, 31, FRY // 2, FRY)


def set_ends(values, rng, smallest, top_value):
    longest = values.shape.index(max(values.shape))
    spots = []
    for shift in (0, 1):
        where = [jax.random.randint(jax.random.fold_in(rng, axis), (), 0, length) for axis, length in enumerate(values.shape)]
        where[longest] = (where[longest] + shift) % values.shape[longest]
        spots.append(tuple(where))
    return values.at[spots[0]].set(smallest).at[spots[1]].set(top_value)


def levels(rng, extent, split, smallest, high):
    factor_of, own = 1.0, jax.random.fold_in(rng, 6)
    for position, blocks in split:
        steps = jnp.exp(jax.random.uniform(jax.random.fold_in(own, position), (blocks,), jnp.float32, smallest / len(split), high / len(split)))
        factor_of = factor_of * jnp.repeat(steps, extent[position] // blocks).reshape([-1 if axis == position else 1 for axis in range(len(extent))])
    return factor_of


def setup_inputs(seed: int = 0) -> dict:
    streams_of = jax.random.split(jax.random.key(seed), 11)
    parent_so2 = jnp.clip(jnp.exp(math.log(10.0) - 4.6051702 * jax.random.uniform(streams_of[0], (LEV, PX, PY), jnp.float32) ** levels(streams_of[0], (LEV, PX, PY), ((1, 16), (2, 8)), -0.2, 0.2)), 0.1, 10.0)
    wind_east = jnp.clip(jax.random.uniform(streams_of[1], (LEV, PX, PY), jnp.float32, -0.2, 0.2) * levels(streams_of[1], (LEV, PX, PY), ((1, 16), (2, 8)), -0.4, 0.0), -0.2, 0.2)
    wind_north = jnp.clip(jax.random.uniform(streams_of[2], (LEV, PX, PY), jnp.float32, -0.2, 0.2) * levels(streams_of[2], (LEV, PX, PY), ((1, 16), (2, 8)), -0.4, 0.0), -0.2, 0.2)
    diffusivity = jnp.clip(jnp.exp(math.log(0.25) - 3.218876 * jax.random.uniform(streams_of[3], (LEV, PX, PY), jnp.float32) ** levels(streams_of[3], (LEV, PX, PY), ((1, 16), (2, 8)), -0.2, 0.2)), 0.01, 0.25)
    nest_so2 = jnp.clip(jnp.exp(math.log(10.0) - 4.6051702 * jax.random.uniform(streams_of[4], (NESTS, LEV, NFX, NFY), jnp.float32) ** levels(streams_of[4], (NESTS, LEV, NFX, NFY), ((0, 16), (2, 8)), -0.2, 0.2)), 0.1, 10.0)
    nest_rows = draw_nest_rows(jax.random.fold_in(streams_of[10], 71), 0)
    nest_offset = draw_nest_offset(jax.random.fold_in(streams_of[10], 71), 0)
    nest_left = set_ends(jax.random.randint(streams_of[7], (NESTS,), 1, PY - FRY), jax.random.fold_in(streams_of[7], 1), 1, (PY - FRY) - 1).astype(jnp.int32)
    nest_height = draw_nest_height(jax.random.fold_in(streams_of[10], 71), 0)
    nest_width = draw_nest_width(jax.random.fold_in(streams_of[10], 71), 0)
    return {"parent_so2": parent_so2, "wind_east": wind_east, "wind_north": wind_north, "diffusivity": diffusivity, "nest_so2": nest_so2, "nest_rows": nest_rows, "nest_offset": nest_offset, "nest_left": nest_left, "nest_height": nest_height, "nest_width": nest_width}


mixing_rate = 0.02


def advance(padded_c, padded_u, padded_v, vertical):
    centre = padded_c[:, 1:-1, 1:-1]
    face_u = 0.5 * (padded_u[:, :-1, 1:-1] + padded_u[:, 1:, 1:-1])
    flux_x = jnp.maximum(face_u, 0.0) * padded_c[:, :-1, 1:-1] + jnp.minimum(face_u, 0.0) * padded_c[:, 1:, 1:-1]
    face_v = 0.5 * (padded_v[:, 1:-1, :-1] + padded_v[:, 1:-1, 1:])
    flux_y = jnp.maximum(face_v, 0.0) * padded_c[:, 1:-1, :-1] + jnp.minimum(face_v, 0.0) * padded_c[:, 1:-1, 1:]
    spread = padded_c[:, :-2, 1:-1] + padded_c[:, 2:, 1:-1] + padded_c[:, 1:-1, :-2] + padded_c[:, 1:-1, 2:] - 4.0 * centre
    coupling = 0.5 * (vertical[:-1] + vertical[1:])
    between = coupling * (centre[1:] - centre[:-1])
    zero_layer = jnp.zeros_like(centre[:1])
    column = jnp.concatenate([between, zero_layer], 0) - jnp.concatenate([zero_layer, between], 0)
    return centre - (flux_x[:, 1:] - flux_x[:, :-1]) - (flux_y[:, :, 1:] - flux_y[:, :, :-1]) + mixing_rate * spread + column


def expand_axis(window, axis):
    first = lax.slice_in_dim(window, 0, 1, axis=axis)
    inner = jnp.repeat(lax.slice_in_dim(window, 1, window.shape[axis] - 1, axis=axis), RATIO, axis=axis)
    last = lax.slice_in_dim(window, window.shape[axis] - 1, window.shape[axis], axis=axis)
    return jnp.concatenate([first, inner, last], axis)


def reference(parent_so2, wind_east, wind_north, diffusivity, nest_so2, nest_rows, nest_offset, nest_left, nest_height, nest_width):
    edge = ((0, 0), (1, 1), (1, 1))
    stepped = advance(jnp.pad(parent_so2, edge), jnp.pad(wind_east, edge), jnp.pad(wind_north, edge), diffusivity)
    fields = jnp.stack([parent_so2, wind_east, wind_north, diffusivity])
    outputs = []
    zero_index = jnp.zeros((), jnp.int32)
    fine_row_ids = jnp.arange(NFX, dtype=jnp.int32)
    fine_col_ids = jnp.arange(NFY, dtype=jnp.int32)
    coarse_row_ids = jnp.arange(FRX, dtype=jnp.int32)
    coarse_col_ids = jnp.arange(FRY, dtype=jnp.int32)
    for nest_index in range(NESTS):
        top_row = (nest_rows[nest_index] * CPX + nest_offset[nest_index]).astype(jnp.int32)
        left_col = nest_left[nest_index].astype(jnp.int32)
        height = nest_height[nest_index]
        width = nest_width[nest_index]
        window = lax.dynamic_slice(fields, (zero_index, zero_index, top_row - 1, left_col - 1), (4, LEV, FRX + 2, FRY + 2))
        full = expand_axis(expand_axis(window, 2), 3)
        active = (fine_row_ids < height * RATIO)[:, None] & (fine_col_ids < width * RATIO)[None, :]
        fine_c = full[0]
        fine_c = fine_c.at[:, 1:-1, 1:-1].set(jnp.where(active, nest_so2[nest_index], fine_c[:, 1:-1, 1:-1]))
        fine_k = 0.1 * full[3][:, 1:-1, 1:-1]
        for sub_step in range(RATIO):
            interior = advance(fine_c, full[1], full[2], fine_k)
            fine_c = fine_c.at[:, 1:-1, 1:-1].set(jnp.where(active, interior, fine_c[:, 1:-1, 1:-1]))
        result = fine_c[:, 1:-1, 1:-1]
        outputs.append(result)
        coarse_band = jnp.mean(result.reshape(LEV, FRX, RATIO, FRY, RATIO), axis=(2, 4))
        current = lax.dynamic_slice(stepped, (zero_index, top_row, left_col), (LEV, FRX, FRY))
        covered = (coarse_row_ids < height)[:, None] & (coarse_col_ids < width)[None, :]
        stepped = lax.dynamic_update_slice(stepped, jnp.where(covered, coarse_band, current), (zero_index, top_row, left_col))
    return stepped, jnp.stack(outputs)
```

```python
import functools
import jax
import jax.numpy as jnp
from jax import lax
from jax.experimental import pallas as pl
from jax.experimental.pallas import tpu as pltpu
from jax.sharding import PartitionSpec as P

RATIO = 10
FR = 32
LEV = 4
ROWS = 64
COLS = 128
OWN = 40
WIDE = 320
GROUPS = 16
TILES = 8
SPAN = FR + 2
WIN = 40
HALO = 120
MIX = 0.02

SMEM = pl.BlockSpec(memory_space=pltpu.SMEM)
ANY = pl.BlockSpec(memory_space=pl.ANY)
VMEM = pl.BlockSpec(memory_space=pltpu.VMEM)


def width_of(chunk):
    return min(128, WIDE - 128 * chunk)


def nest_over(rows, group):
    found = jnp.int32(0)
    for i in range(GROUPS):
        found = jnp.where(rows[i] == group, jnp.int32(i), found)
    return found


def lanes(shape):
    return lax.broadcasted_iota(jnp.int32, shape, 1)


def pack_kernel(rows, offs, left, so2, east, north, diff, nest, send, edges, x, nx, win, halo, sems):
    t = lax.axis_index("tile")
    g = lax.axis_index("grp")
    loads = [
        pltpu.make_async_copy(f, x.at[pl.ds(4 * i, 4), pl.ds(0, ROWS), :], sems.at[i])
        for i, f in enumerate((so2, east, north, diff))
    ]
    loads.append(pltpu.make_async_copy(nest.at[0], nx, sems.at[4]))
    for c in loads:
        c.start()
    n = nest_over(rows, g)
    top = offs[n] - 1
    base = 128 * t + 1 - left[n] + 1024
    x[:, ROWS : ROWS + 8, :] = jnp.zeros((16, 8, 128), jnp.float32)
    lane = lanes((8, 128))
    loads[4].wait()
    for l in range(LEV):
        for m in range(3):
            w = width_of(m)
            at = 10 * (3 * l + m)
            halo[0, at : at + 10, 0:w] = nx[l, 0:10, 128 * m : 128 * m + w]
            halo[1, at : at + 10, 0:w] = nx[l, OWN - 10 : OWN, 128 * m : 128 * m + w]

    up = pltpu.make_async_copy(halo.at[0], send.at[jnp.maximum(t - 1, 0), pl.ds(WIN + 8, HALO), :], sems.at[5])
    down = pltpu.make_async_copy(
        halo.at[1], send.at[jnp.minimum(t + 1, TILES - 1), pl.ds(WIN + 8, HALO), :], sems.at[6]
    )

    @pl.when(t > 0)
    def _():
        up.start()

    @pl.when(t < TILES - 1)
    def _():
        down.start()

    for c in loads[:4]:
        c.wait()
    for l in range(LEV):
        edges[l : l + 1, :] = x[l, 0:1, :]
        edges[4 + l : 5 + l, :] = x[4 + l, 0:1, :]
        edges[8 + l : 9 + l, :] = x[l, ROWS - 1 : ROWS, :]
        edges[12 + l : 13 + l, :] = x[4 + l, ROWS - 1 : ROWS, :]
    first = jnp.zeros((8, 128), jnp.float32)
    last = jnp.zeros((8, 128), jnp.float32)
    for p in range(8):
        plane = p if p < 4 else p + 4
        for b in range(8):
            k = 8 * p + b
            v = x[plane, 8 * b : 8 * b + 8, :]
            first = jnp.where(lane == k, pltpu.roll(v, k, 1), first)
            last = jnp.where(lane == k, pltpu.roll(v, k + 1, 1), last)
    shifts = [lax.rem(base + SPAN * f, 128) for f in range(3)]
    kshifts = [lax.rem(base + 32 * l - 1, 128) for l in range(LEV)]
    for d in range(TILES):
        for l in range(LEV):
            part = [
                pltpu.roll(x[4 * f + l, pl.ds(top + 4 * d, 8), :], shifts[f], 1) for f in range(3)
            ]
            win[d, 8 * l : 8 * l + 8, :] = jnp.where(
                lane < SPAN, part[0], jnp.where(lane < 2 * SPAN, part[1], part[2])
            )
        part = [pltpu.roll(x[12 + l, pl.ds(top + 4 * d, 8), :], kshifts[l], 1) for l in range(LEV)]
        win[d, 32:40, :] = jnp.where(
            lane < 64,
            jnp.where(lane < 32, part[0], part[1]),
            jnp.where(lane < 96, part[2], part[3]),
        )
        win[d, 40:48, :] = jnp.where(d < t, first, last)
    out = pltpu.make_async_copy(win, send.at[:, pl.ds(0, WIN + 8), :], sems.at[7])
    out.start()

    @pl.when(t > 0)
    def _():
        up.wait()

    @pl.when(t < TILES - 1)
    def _():
        down.wait()

    out.wait()


def merge_kernel(rows, left, got, edges, send, a, b, sems):
    g = lax.axis_index("grp")
    n = nest_over(rows, g)
    start = left[n] - 1
    first = lax.div(start, COLS)
    second = jnp.minimum(first + 1, TILES - 1)
    load_a = pltpu.make_async_copy(got.at[first, pl.ds(0, WIN), :], a, sems.at[0])
    load_b = pltpu.make_async_copy(got.at[second, pl.ds(0, WIN), :], b, sems.at[1])
    load_a.start()
    load_b.start()
    up = pltpu.make_async_copy(
        edges.at[pl.ds(0, 8), :], send.at[jnp.maximum(g - 1, 0), pl.ds(WIN, 8), :], sems.at[2]
    )
    down = pltpu.make_async_copy(
        edges.at[pl.ds(8, 8), :], send.at[jnp.minimum(g + 1, GROUPS - 1), pl.ds(WIN, 8), :], sems.at[3]
    )

    @pl.when(g > 0)
    def _():
        up.start()

    @pl.when(g < GROUPS - 1)
    def _():
        down.start()

    room = COLS - (start - COLS * first)
    lane = lanes((32, 128))
    col = (
        lane
        - jnp.where(lane >= SPAN, SPAN, 0)
        - jnp.where(lane >= 2 * SPAN, SPAN, 0)
    )
    klane = lanes((8, 128))
    kcol = (klane & 31) + 1
    load_a.wait()
    load_b.wait()
    a[0:32, :] = jnp.where(col < room, a[0:32, :], b[0:32, :])
    a[32:40, :] = jnp.where(kcol < room, a[32:40, :], b[32:40, :])
    out = pltpu.make_async_copy(a, send.at[n, pl.ds(0, WIN), :], sems.at[4])
    out.start()

    @pl.when(g > 0)
    def _():
        up.wait()

    @pl.when(g < GROUPS - 1)
    def _():
        down.wait()

    out.wait()


def from_left(chunks, lane):
    turned = [pltpu.roll(c, 1, 1) for c in chunks]
    return [jnp.where(lane == 0, turned[m - 1], turned[m]) for m in range(3)]


def from_right(chunks, lane):
    turned = [pltpu.roll(c, 127, 1) for c in chunks]
    return [jnp.where(lane == 127, turned[(m + 1) % 3], turned[m]) for m in range(3)]


def pos(v):
    return jnp.maximum(v, 0.0)


def neg(v):
    return jnp.minimum(v, 0.0)


def fine_kernel(
    rows, left, height, width, got_tile, got_grp, nest, so2, east, north, diff,
    fine_out, back, stepped,
    w, hn, nx, eh, ch, px, vk, e, c, u, v, kz, raw, am, ap, bm, bp, ac, sums, slot, sems,
):
    t = lax.axis_index("tile")
    g = lax.axis_index("grp")
    src = rows[g]
    prev_t = jnp.maximum(t - 1, 0)
    next_t = jnp.minimum(t + 1, TILES - 1)
    prev_g = jnp.maximum(g - 1, 0)
    next_g = jnp.minimum(g + 1, GROUPS - 1)
    copies = [
        (got_grp.at[src, pl.ds(0, WIN), :], w),
        (nest.at[0], nx),
        (got_tile.at[prev_t, pl.ds(WIN + 8, HALO), :], hn.at[0]),
        (got_tile.at[next_t, pl.ds(WIN + 8, HALO), :], hn.at[1]),
        (so2, px.at[pl.ds(0, 4), pl.ds(8, ROWS), :]),
        (east, px.at[pl.ds(4, 4), pl.ds(8, ROWS), :]),
        (north, vk.at[pl.ds(0, 4)]),
        (diff, vk.at[pl.ds(4, 4)]),
        (got_grp.at[prev_g, pl.ds(WIN, 8), :], eh.at[0]),
        (got_grp.at[next_g, pl.ds(WIN, 8), :], eh.at[1]),
        (got_tile.at[prev_t, pl.ds(WIN, 8), :], ch.at[0]),
        (got_tile.at[next_t, pl.ds(WIN, 8), :], ch.at[1]),
    ]
    copies = [pltpu.make_async_copy(s, d, sems.at[i]) for i, (s, d) in enumerate(copies)]
    for copy in copies:
        copy.start()
    lane = lanes((8, 128))
    sub = lax.broadcasted_iota(jnp.int32, (8, 128), 0)
    zero = jnp.zeros((8, 128), jnp.float32)
    for p in range(2):
        for l in range(LEV):
            for m in range(3):
                c[p, l, m, 0:8, :] = zero
                c[p, l, m, 72:80, :] = zero
    copies[0].wait()
    for m in range(3):
        fine_col = 128 * m + lane
        under = (fine_col * 6554) >> 16
        pick = jnp.where(fine_col < WIDE, under + 1, jnp.where(fine_col == WIDE, SPAN - 1, 0))
        kpick = jnp.minimum(under, FR - 1)
        for l in range(LEV):
            block = w[8 * l : 8 * l + 8, :]
            for f in range(3):
                e[4 * f + l, m] = jnp.take_along_axis(block, pick + SPAN * f, axis=1)
            e[12 + l, m] = jnp.take_along_axis(w[32:40, :], kpick + 32 * l, axis=1)
    copies[1].wait()
    copies[2].wait()
    copies[3].wait()
    for l in range(LEV):
        for m in range(3):
            n = width_of(m)
            at = 10 * (3 * l + m)
            raw[l, m, 8:18, :] = hn[0, at : at + 10, :]
            raw[l, m, 18:58, 0:n] = nx[l, :, 128 * m : 128 * m + n]
            raw[l, m, 58:68, :] = hn[1, at : at + 10, :]
    last_row = RATIO * height[g]
    last_col = RATIO * width[g]
    first_row = OWN * t - 10

    def spread(p, m, i):
        lo, hi = (8 * i) // 10, min((8 * i + 7) // 10, 5)
        low = jnp.broadcast_to(e[p, m, lo : lo + 1, :], (8, 128))
        if lo == hi:
            return low
        high = jnp.broadcast_to(e[p, m, hi : hi + 1, :], (8, 128))
        return jnp.where(sub < 10 * hi - 8 * i, low, high)

    for i in range(8):
        r = 8 + 8 * i
        row = first_row + 8 * i + sub
        row_in = (row >= 0) & (row < last_row)
        for m in range(3):
            active = row_in & (128 * m + lane < last_col)
            for l in range(LEV):
                c[0, l, m, r : r + 8, :] = jnp.where(active, raw[l, m, r : r + 8, :], spread(l, m, i))
                u[l, m, r : r + 8, :] = spread(4 + l, m, i)
                v[l, m, r : r + 8, :] = spread(8 + l, m, i)
    for i in range(8):
        r = 8 + 8 * i
        local = 8 * i + sub
        row = first_row + local
        row_in = (row >= 0) & (row < last_row) & (local >= 1) & (local <= 58)
        inside = [row_in & (128 * m + lane < last_col) for m in range(3)]
        faces = []
        for m in range(3):
            ks = [spread(12 + l, m, i) for l in range(LEV)]
            faces.append([(0.05 * (ks[l] + ks[l + 1])) for l in range(LEV - 1)])
            for l in range(LEV - 1):
                kz[l, m, 8 * i : 8 * i + 8, :] = jnp.where(inside[m], faces[m][l], 0.0)
        for l in range(LEV):
            vs = [v[l, m, r : r + 8, :] for m in range(3)]
            before = from_left(vs, lane)
            after = from_right(vs, lane)
            for m in range(3):
                here = u[l, m, r : r + 8, :]
                u_lo = 0.5 * (u[l, m, r - 1 : r + 7, :] + here)
                u_hi = 0.5 * (here + u[l, m, r + 1 : r + 9, :])
                v_lo = 0.5 * (before[m] + vs[m])
                v_hi = 0.5 * (vs[m] + after[m])
                mid = (1.0 - 4.0 * MIX) - pos(u_hi) + neg(u_lo) - pos(v_hi) + neg(v_lo)
                if l > 0:
                    mid = mid - faces[m][l - 1]
                if l < LEV - 1:
                    mid = mid - faces[m][l]
                q = slice(8 * i, 8 * i + 8)
                ac[l, m, q, :] = jnp.where(inside[m], mid, 1.0)
                am[l, m, q, :] = jnp.where(inside[m], MIX + pos(u_lo), 0.0)
                ap[l, m, q, :] = jnp.where(inside[m], MIX - neg(u_hi), 0.0)
                bm[l, m, q, :] = jnp.where(inside[m], MIX + pos(v_lo), 0.0)
                bp[l, m, q, :] = jnp.where(inside[m], MIX - neg(v_hi), 0.0)

    def advance(old, new):
        for i in range(8):
            r = 8 + 8 * i
            q = slice(8 * i, 8 * i + 8)
            now = [[c[old, l, m, r : r + 8, :] for m in range(3)] for l in range(LEV)]
            flow = [[kz[l, m, q, :] for m in range(3)] for l in range(LEV - 1)]
            for l in range(LEV):
                before = from_left(now[l], lane)
                after = from_right(now[l], lane)
                for m in range(3):
                    value = ac[l, m, q, :] * now[l][m]
                    value = value + am[l, m, q, :] * c[old, l, m, r - 1 : r + 7, :]
                    value = value + ap[l, m, q, :] * c[old, l, m, r + 1 : r + 9, :]
                    value = value + bm[l, m, q, :] * before[m]
                    value = value + bp[l, m, q, :] * after[m]
                    if l > 0:
                        value = value + flow[l - 1][m] * now[l - 1][m]
                    if l < LEV - 1:
                        value = value + flow[l][m] * now[l + 1][m]
                    c[new, l, m, r : r + 8, :] = value

    def pair(_, carry):
        advance(0, 1)
        advance(1, 0)
        return carry

    lax.fori_loop(0, RATIO // 2, pair, 0)
    for l in range(LEV):
        for m in range(3):
            n = width_of(m)
            fine_out[0, l, :, 128 * m : 128 * m + n] = c[0, l, m, 18:58, 0:n]
            for a in range(4):
                band = c[0, l, m, 18 + 10 * a : 28 + 10 * a, :]
                sums[m, 4 * l + a : 4 * l + a + 1, :] = jnp.sum(band, axis=0, keepdims=True)
    mean = jnp.zeros((16, 128), jnp.float32)
    for m in range(3):
        k = 128 * m + lax.broadcasted_iota(jnp.int32, (128, 128), 0)
        chosen = ((k * 6554) >> 16) == lanes((128, 128))
        pick = jnp.where(chosen & (k < WIDE), 1.0, 0.0)
        mean = mean + jnp.dot(
            sums[m], pick, precision=lax.Precision.HIGHEST, preferred_element_type=jnp.float32
        )
    mean = mean * (1.0 / (RATIO * RATIO))
    lane4 = lanes((4, 128))
    value = jnp.zeros((4, 128), jnp.float32)
    turned = [mean if l == 0 else pltpu.roll(mean, 32 * l, 1) for l in range(LEV)]
    for l in range(LEV):
        inside = (lane4 >= 32 * l) & (lane4 < 32 * l + 32)
        value = jnp.where(inside, turned[l][4 * l : 4 * l + 4, :], value)
    slot[...] = value
    tile_a = lax.div(left[g], COLS)
    tile_b = jnp.where(tile_a < TILES - 1, tile_a + 1, tile_a - 1)
    send_a = pltpu.make_async_copy(slot, back.at[TILES * src + tile_a], sems.at[12])
    send_b = pltpu.make_async_copy(slot, back.at[TILES * src + tile_b], sems.at[13])
    send_a.start()
    send_b.start()

    for copy in copies[4:]:
        copy.wait()
    for p in range(8):
        px[p, 7:8, :] = jnp.where(g > 0, eh[0, p : p + 1, :], 0.0)
        px[p, 72:73, :] = jnp.where(g < GROUPS - 1, eh[1, p : p + 1, :], 0.0)
    edge_l = jnp.where(t > 0, ch[0], 0.0)
    edge_r = jnp.where(t < TILES - 1, ch[1], 0.0)
    for b in range(8):
        r = 8 + 8 * b
        q = slice(8 * b, 8 * b + 8)
        now = [px[l, r : r + 8, :] for l in range(LEV)]
        ks = [vk[4 + l, q, :] for l in range(LEV)]
        between = [0.5 * (ks[l] + ks[l + 1]) * (now[l + 1] - now[l]) for l in range(LEV - 1)]
        for l in range(LEV):
            here = now[l]
            k, kv = 8 * l + b, 32 + 8 * l + b
            wind = vk[l, q, :]
            c_w = jnp.where(lane == 0, pltpu.roll(edge_l, (128 - k) % 128, 1), pltpu.roll(here, 1, 1))
            c_e = jnp.where(lane == 127, pltpu.roll(edge_r, 127 - k, 1), pltpu.roll(here, 127, 1))
            v_w = jnp.where(lane == 0, pltpu.roll(edge_l, 128 - kv, 1), pltpu.roll(wind, 1, 1))
            v_e = jnp.where(lane == 127, pltpu.roll(edge_r, 127 - kv, 1), pltpu.roll(wind, 127, 1))
            c_n = px[l, r - 1 : r + 7, :]
            c_s = px[l, r + 1 : r + 9, :]
            flow = px[4 + l, r : r + 8, :]
            u_lo = 0.5 * (px[4 + l, r - 1 : r + 7, :] + flow)
            u_hi = 0.5 * (flow + px[4 + l, r + 1 : r + 9, :])
            v_lo = 0.5 * (v_w + wind)
            v_hi = 0.5 * (wind + v_e)
            value = (
                here
                - ((pos(u_hi) * here + neg(u_hi) * c_s) - (pos(u_lo) * c_n + neg(u_lo) * here))
                - ((pos(v_hi) * here + neg(v_hi) * c_e) - (pos(v_lo) * c_w + neg(v_lo) * here))
                + MIX * (c_n + c_s + c_w + c_e - 4.0 * here)
            )
            if l < LEV - 1:
                value = value + between[l]
            if l > 0:
                value = value - between[l - 1]
            stepped[l, q, :] = value
    send_a.wait()
    send_b.wait()


def place_kernel(rows, offs, left, height, width, stepped, got, out, s, r, sems):
    t = lax.axis_index("tile")
    g = lax.axis_index("grp")
    n = nest_over(rows, g)
    lf = left[n]
    wd = width[n]

    @pl.when((lf < COLS * t + COLS) & (lf + wd > COLS * t))
    def _():
        off = offs[n]
        base = pl.multiple_of(lax.div(off, 8) * 8, 8)
        load_s = pltpu.make_async_copy(stepped.at[:, pl.ds(base, 40), :], s, sems.at[0])
        load_r = pltpu.make_async_copy(got.at[n], r, sems.at[1])
        load_s.start()
        load_r.start()
        lane = lanes((FR, 128)) + COLS * t
        row = lax.broadcasted_iota(jnp.int32, (FR, 128), 0)
        covered = (lane >= lf) & (lane < lf + wd) & (row < height[n])
        load_s.wait()
        load_r.wait()
        for l in range(LEV):
            turned = pltpu.roll(r[...], lax.rem(lf - COLS * t - 32 * l + 2048, 128), 1)
            at = pl.ds(off - base, FR)
            s[l, at, :] = jnp.where(covered, turned, s[l, at, :])
        store = pltpu.make_async_copy(s, out.at[:, pl.ds(base, 40), :], sems.at[2])
        store.start()
        store.wait()


def shards(so2, east, north, diff, nest, rows, offs, left, height, width):
    f32 = jnp.float32
    shape = jax.ShapeDtypeStruct
    dma = pltpu.SemaphoreType.DMA
    send, edges = pl.pallas_call(
        pack_kernel,
        out_shape=(shape((TILES, WIN + 8 + HALO, 128), f32), shape((16, 128), f32)),
        in_specs=[SMEM] * 3 + [ANY] * 5,
        out_specs=(ANY, VMEM),
        scratch_shapes=[
            pltpu.VMEM((16, ROWS + 8, 128), f32),
            pltpu.VMEM((LEV, OWN, WIDE), f32),
            pltpu.VMEM((TILES, WIN + 8, 128), f32),
            pltpu.VMEM((2, HALO, 128), f32),
            dma((8,)),
        ],
        name="pack",
    )(rows, offs, left, so2, east, north, diff, nest)
    got_tile = lax.all_to_all(send, "tile", 0, 0)
    send = pl.pallas_call(
        merge_kernel,
        out_shape=shape((GROUPS, WIN + 8, 128), f32),
        in_specs=[SMEM] * 2 + [ANY, VMEM],
        out_specs=ANY,
        scratch_shapes=[pltpu.VMEM((WIN, 128), f32), pltpu.VMEM((WIN, 128), f32), dma((5,))],
        name="merge",
    )(rows, left, got_tile, edges)
    got_grp = lax.all_to_all(send, "grp", 0, 0)
    field = functools.partial(pltpu.VMEM, dtype=f32)
    nest_next, back, stepped = pl.pallas_call(
        fine_kernel,
        out_shape=(
            shape((1, LEV, OWN, WIDE), f32),
            shape((GROUPS * TILES, 4, 128), f32),
            shape((LEV, ROWS, COLS), f32),
        ),
        in_specs=[SMEM] * 4 + [ANY] * 7,
        out_specs=(VMEM, ANY, VMEM),
        scratch_shapes=[
            field((WIN, 128)),
            field((2, HALO, 128)),
            field((LEV, OWN, WIDE)),
            field((2, 8, 128)),
            field((2, 8, 128)),
            field((8, ROWS + 16, 128)),
            field((8, ROWS, 128)),
            field((16, 3, 8, 128)),
            field((2, LEV, 3, 80, 128)),
            field((LEV, 3, 80, 128)),
            field((LEV, 3, 80, 128)),
            field((LEV - 1, 3, 64, 128)),
            field((LEV, 3, 80, 128)),
            field((LEV, 3, 64, 128)),
            field((LEV, 3, 64, 128)),
            field((LEV, 3, 64, 128)),
            field((LEV, 3, 64, 128)),
            field((LEV, 3, 64, 128)),
            field((3, 16, 128)),
            field((4, 128)),
            dma((14,)),
        ],
        name="fine",
    )(rows, left, height, width, got_tile, got_grp, nest, so2, east, north, diff)
    got = lax.all_to_all(back, ("grp", "tile"), 0, 0)
    got = got.reshape(GROUPS, FR, 128)
    parent_next = pl.pallas_call(
        place_kernel,
        out_shape=shape((LEV, ROWS, COLS), f32),
        in_specs=[SMEM] * 5 + [ANY, ANY],
        out_specs=ANY,
        scratch_shapes=[field((LEV, 40, 128)), field((FR, 128)), dma((3,))],
        input_output_aliases={5: 0},
        name="place",
    )(rows, offs, left, height, width, stepped, got)
    return parent_next, nest_next


def solution(mesh):
    in_specs = (
        P(None, "grp", "tile"),
        P(None, "grp", "tile"),
        P(None, "grp", "tile"),
        P(None, "grp", "tile"),
        P("grp", None, "tile", None),
        P(),
        P(),
        P(),
        P(),
        P(),
    )
    out_specs = (P(None, "grp", "tile"), P("grp", None, "tile", None))
    return jax.shard_map(shards, mesh=mesh, in_specs=in_specs, out_specs=out_specs, check_vma=False)
```

```python
import functools
import jax
import jax.numpy as jnp
from jax import lax
from jax.experimental import pallas as pl
from jax.experimental.pallas import tpu as pltpu
from jax.sharding import PartitionSpec as P

RATIO = 10
FR = 32
LEV = 4
ROWS = 64
COLS = 128
OWN = 40
WIDE = 320
GROUPS = 16
TILES = 8
SPAN = FR + 2
WIN = 40
HALO = 120
MIX = 0.02

SMEM = pl.BlockSpec(memory_space=pltpu.SMEM)
ANY = pl.BlockSpec(memory_space=pl.ANY)
VMEM = pl.BlockSpec(memory_space=pltpu.VMEM)


def width_of(chunk):
    return min(128, WIDE - 128 * chunk)


def nest_over(rows, group):
    found = jnp.int32(0)
    for i in range(GROUPS):
        found = jnp.where(rows[i] == group, jnp.int32(i), found)
    return found


def lanes(shape):
    return lax.broadcasted_iota(jnp.int32, shape, 1)


def pack_kernel(rows, offs, left, so2, east, north, diff, nest, send, edges, x, nx, sems):
    t = lax.axis_index("tile")
    g = lax.axis_index("grp")
    loads = [
        pltpu.make_async_copy(f, x.at[pl.ds(4 * i, 4), pl.ds(0, ROWS), :], sems.at[i])
        for i, f in enumerate((so2, east, north, diff))
    ]
    loads.append(pltpu.make_async_copy(nest.at[0], nx, sems.at[4]))
    for c in loads:
        c.start()
    n = nest_over(rows, g)
    top = offs[n] - 1
    base = 128 * t + 1 - left[n] + 1024
    x[:, ROWS : ROWS + 8, :] = jnp.zeros((16, 8, 128), jnp.float32)
    lane = lanes((8, 128))
    before = jnp.where(t > 0, t - 1, t + 2)
    after = jnp.where(t < TILES - 1, t + 1, t - 2)
    loads[4].wait()
    for l in range(LEV):
        for m in range(3):
            w = width_of(m)
            at = 10 * (3 * l + m)
            rows_at = pl.ds(WIN + 8 + at, 10)
            send[before, rows_at, 0:w] = nx[l, 0:10, 128 * m : 128 * m + w]
            send[after, rows_at, 0:w] = nx[l, OWN - 10 : OWN, 128 * m : 128 * m + w]
    for c in loads[:4]:
        c.wait()
    for l in range(LEV):
        edges[l : l + 1, :] = x[l, 0:1, :]
        edges[4 + l : 5 + l, :] = x[4 + l, 0:1, :]
        edges[8 + l : 9 + l, :] = x[l, ROWS - 1 : ROWS, :]
        edges[12 + l : 13 + l, :] = x[4 + l, ROWS - 1 : ROWS, :]
    first = jnp.zeros((8, 128), jnp.float32)
    last = jnp.zeros((8, 128), jnp.float32)
    for p in range(8):
        plane = p if p < 4 else p + 4
        for b in range(8):
            k = 8 * p + b
            v = x[plane, 8 * b : 8 * b + 8, :]
            first = jnp.where(lane == k, pltpu.roll(v, k, 1), first)
            last = jnp.where(lane == k, pltpu.roll(v, k + 1, 1), last)
    shifts = [lax.rem(base + SPAN * f, 128) for f in range(3)]
    kshifts = [lax.rem(base + 32 * l - 1, 128) for l in range(LEV)]
    for d in range(TILES):
        for l in range(LEV):
            part = [
                pltpu.roll(x[4 * f + l, pl.ds(top + 4 * d, 8), :], shifts[f], 1) for f in range(3)
            ]
            send[d, 8 * l : 8 * l + 8, :] = jnp.where(
                lane < SPAN, part[0], jnp.where(lane < 2 * SPAN, part[1], part[2])
            )
        part = [pltpu.roll(x[12 + l, pl.ds(top + 4 * d, 8), :], kshifts[l], 1) for l in range(LEV)]
        send[d, 32:40, :] = jnp.where(
            lane < 64,
            jnp.where(lane < 32, part[0], part[1]),
            jnp.where(lane < 96, part[2], part[3]),
        )
        send[d, 40:48, :] = jnp.where(d < t, first, last)


def merge_kernel(rows, left, got, edges, send):
    g = lax.axis_index("grp")
    n = nest_over(rows, g)
    start = left[n] - 1
    first = lax.div(start, COLS)
    second = jnp.minimum(first + 1, TILES - 1)
    send[jnp.where(g > 0, g - 1, g + 2), WIN : WIN + 8, :] = edges[0:8, :]
    send[jnp.where(g < GROUPS - 1, g + 1, g - 2), WIN : WIN + 8, :] = edges[8:16, :]
    room = COLS - (start - COLS * first)
    lane = lanes((8, 128))
    col = lane - jnp.where(lane >= SPAN, SPAN, 0) - jnp.where(lane >= 2 * SPAN, SPAN, 0)
    kcol = (lane & 31) + 1
    for l in range(5):
        q = slice(8 * l, 8 * l + 8)
        here = (col if l < 4 else kcol) < room
        send[n, q, :] = jnp.where(here, got[first, q, :], got[second, q, :])


def from_left(chunks, lane):
    turned = [pltpu.roll(c, 1, 1) for c in chunks]
    return [jnp.where(lane == 0, turned[m - 1], turned[m]) for m in range(3)]


def from_right(chunks, lane):
    turned = [pltpu.roll(c, 127, 1) for c in chunks]
    return [jnp.where(lane == 127, turned[(m + 1) % 3], turned[m]) for m in range(3)]


def pos(v):
    return jnp.maximum(v, 0.0)


def neg(v):
    return jnp.minimum(v, 0.0)


def fine_kernel(
    rows, left, height, width, got_tile, got_grp, nest, so2, east, north, diff,
    fine_out, back, stepped,
    nx, px, vk, e, c, u, v, kz, raw, am, ap, bm, bp, ac, sums, sems,
):
    t = lax.axis_index("tile")
    g = lax.axis_index("grp")
    src = rows[g]
    prev_t = jnp.maximum(t - 1, 0)
    next_t = jnp.minimum(t + 1, TILES - 1)
    prev_g = jnp.maximum(g - 1, 0)
    next_g = jnp.minimum(g + 1, GROUPS - 1)
    copies = [
        (nest.at[0], nx),
        (so2, px.at[pl.ds(0, 4), pl.ds(8, ROWS), :]),
        (east, px.at[pl.ds(4, 4), pl.ds(8, ROWS), :]),
        (north, vk.at[pl.ds(0, 4)]),
        (diff, vk.at[pl.ds(4, 4)]),
    ]
    copies = [pltpu.make_async_copy(s, d, sems.at[i]) for i, (s, d) in enumerate(copies)]
    for copy in copies:
        copy.start()
    lane = lanes((8, 128))
    sub = lax.broadcasted_iota(jnp.int32, (8, 128), 0)
    zero = jnp.zeros((8, 128), jnp.float32)
    for p in range(2):
        for l in range(LEV):
            for m in range(3):
                c[p, l, m, 0:8, :] = zero
                c[p, l, m, 72:80, :] = zero
    for m in range(3):
        fine_col = 128 * m + lane
        under = (fine_col * 6554) >> 16
        pick = jnp.where(fine_col < WIDE, under + 1, jnp.where(fine_col == WIDE, SPAN - 1, 0))
        kpick = jnp.minimum(under, FR - 1)
        for l in range(LEV):
            block = got_grp[src, 8 * l : 8 * l + 8, :]
            for f in range(3):
                e[4 * f + l, m] = jnp.take_along_axis(block, pick + SPAN * f, axis=1)
            e[12 + l, m] = jnp.take_along_axis(got_grp[src, 32:40, :], kpick + 32 * l, axis=1)
    copies[0].wait()
    for l in range(LEV):
        for m in range(3):
            n = width_of(m)
            at = 10 * (3 * l + m)
            raw[l, m, 8:18, :] = got_tile[prev_t, pl.ds(WIN + 8 + at, 10), :]
            raw[l, m, 18:58, 0:n] = nx[l, :, 128 * m : 128 * m + n]
            raw[l, m, 58:68, :] = got_tile[next_t, pl.ds(WIN + 8 + at, 10), :]
    last_row = RATIO * height[g]
    last_col = RATIO * width[g]
    first_row = OWN * t - 10

    def spread(p, m, i):
        lo, hi = (8 * i) // 10, min((8 * i + 7) // 10, 5)
        low = jnp.broadcast_to(e[p, m, lo : lo + 1, :], (8, 128))
        if lo == hi:
            return low
        high = jnp.broadcast_to(e[p, m, hi : hi + 1, :], (8, 128))
        return jnp.where(sub < 10 * hi - 8 * i, low, high)

    for i in range(8):
        r = 8 + 8 * i
        row = first_row + 8 * i + sub
        row_in = (row >= 0) & (row < last_row)
        for m in range(3):
            active = row_in & (128 * m + lane < last_col)
            for l in range(LEV):
                c[0, l, m, r : r + 8, :] = jnp.where(active, raw[l, m, r : r + 8, :], spread(l, m, i))
                u[l, m, r : r + 8, :] = spread(4 + l, m, i)
                v[l, m, r : r + 8, :] = spread(8 + l, m, i)
    for i in range(8):
        r = 8 + 8 * i
        local = 8 * i + sub
        row = first_row + local
        row_in = (row >= 0) & (row < last_row) & (local >= 1) & (local <= 58)
        inside = [row_in & (128 * m + lane < last_col) for m in range(3)]
        faces = []
        for m in range(3):
            ks = [spread(12 + l, m, i) for l in range(LEV)]
            faces.append([(0.05 * (ks[l] + ks[l + 1])) for l in range(LEV - 1)])
            for l in range(LEV - 1):
                kz[l, m, 8 * i : 8 * i + 8, :] = jnp.where(inside[m], faces[m][l], 0.0)
        for l in range(LEV):
            vs = [v[l, m, r : r + 8, :] for m in range(3)]
            before = from_left(vs, lane)
            after = from_right(vs, lane)
            for m in range(3):
                here = u[l, m, r : r + 8, :]
                u_lo = 0.5 * (u[l, m, r - 1 : r + 7, :] + here)
                u_hi = 0.5 * (here + u[l, m, r + 1 : r + 9, :])
                v_lo = 0.5 * (before[m] + vs[m])
                v_hi = 0.5 * (vs[m] + after[m])
                mid = (1.0 - 4.0 * MIX) - pos(u_hi) + neg(u_lo) - pos(v_hi) + neg(v_lo)
                if l > 0:
                    mid = mid - faces[m][l - 1]
                if l < LEV - 1:
                    mid = mid - faces[m][l]
                q = slice(8 * i, 8 * i + 8)
                ac[l, m, q, :] = jnp.where(inside[m], mid, 1.0)
                am[l, m, q, :] = jnp.where(inside[m], MIX + pos(u_lo), 0.0)
                ap[l, m, q, :] = jnp.where(inside[m], MIX - neg(u_hi), 0.0)
                bm[l, m, q, :] = jnp.where(inside[m], MIX + pos(v_lo), 0.0)
                bp[l, m, q, :] = jnp.where(inside[m], MIX - neg(v_hi), 0.0)

    def advance(old, new):
        for i in range(8):
            r = 8 + 8 * i
            q = slice(8 * i, 8 * i + 8)
            now = [[c[old, l, m, r : r + 8, :] for m in range(3)] for l in range(LEV)]
            flow = [[kz[l, m, q, :] for m in range(3)] for l in range(LEV - 1)]
            for l in range(LEV):
                before = from_left(now[l], lane)
                after = from_right(now[l], lane)
                for m in range(3):
                    value = ac[l, m, q, :] * now[l][m]
                    value = value + am[l, m, q, :] * c[old, l, m, r - 1 : r + 7, :]
                    value = value + ap[l, m, q, :] * c[old, l, m, r + 1 : r + 9, :]
                    value = value + bm[l, m, q, :] * before[m]
                    value = value + bp[l, m, q, :] * after[m]
                    if l > 0:
                        value = value + flow[l - 1][m] * now[l - 1][m]
                    if l < LEV - 1:
                        value = value + flow[l][m] * now[l + 1][m]
                    c[new, l, m, r : r + 8, :] = value

    def pair(_, carry):
        advance(0, 1)
        advance(1, 0)
        return carry

    lax.fori_loop(0, RATIO // 2, pair, 0)
    for l in range(LEV):
        for m in range(3):
            n = width_of(m)
            fine_out[0, l, :, 128 * m : 128 * m + n] = c[0, l, m, 18:58, 0:n]
            for a in range(4):
                band = c[0, l, m, 18 + 10 * a : 28 + 10 * a, :]
                sums[m, 4 * l + a : 4 * l + a + 1, :] = jnp.sum(band, axis=0, keepdims=True)
    mean = jnp.zeros((16, 128), jnp.float32)
    for m in range(3):
        k = 128 * m + lax.broadcasted_iota(jnp.int32, (128, 128), 0)
        chosen = ((k * 6554) >> 16) == lanes((128, 128))
        pick = jnp.where(chosen & (k < WIDE), 1.0, 0.0)
        mean = mean + jnp.dot(
            sums[m], pick, precision=lax.Precision.HIGHEST, preferred_element_type=jnp.float32
        )
    mean = mean * (1.0 / (RATIO * RATIO))
    lane4 = lanes((4, 128))
    value = jnp.zeros((4, 128), jnp.float32)
    turned = [mean if l == 0 else pltpu.roll(mean, 32 * l, 1) for l in range(LEV)]
    for l in range(LEV):
        inside = (lane4 >= 32 * l) & (lane4 < 32 * l + 32)
        value = jnp.where(inside, turned[l][4 * l : 4 * l + 4, :], value)
    tile_a = lax.div(left[g], COLS)
    tile_b = jnp.where(tile_a < TILES - 1, tile_a + 1, tile_a - 1)
    back[TILES * src + tile_a] = value
    back[TILES * src + tile_b] = value

    for copy in copies[1:]:
        copy.wait()
    for p in range(8):
        px[p, 7:8, :] = jnp.where(g > 0, got_grp[prev_g, WIN + p : WIN + p + 1, :], 0.0)
        px[p, 72:73, :] = jnp.where(g < GROUPS - 1, got_grp[next_g, WIN + p : WIN + p + 1, :], 0.0)
    edge_l = jnp.where(t > 0, got_tile[prev_t, WIN : WIN + 8, :], 0.0)
    edge_r = jnp.where(t < TILES - 1, got_tile[next_t, WIN : WIN + 8, :], 0.0)
    for b in range(8):
        r = 8 + 8 * b
        q = slice(8 * b, 8 * b + 8)
        now = [px[l, r : r + 8, :] for l in range(LEV)]
        ks = [vk[4 + l, q, :] for l in range(LEV)]
        between = [0.5 * (ks[l] + ks[l + 1]) * (now[l + 1] - now[l]) for l in range(LEV - 1)]
        for l in range(LEV):
            here = now[l]
            k, kv = 8 * l + b, 32 + 8 * l + b
            wind = vk[l, q, :]
            c_w = jnp.where(lane == 0, pltpu.roll(edge_l, (128 - k) % 128, 1), pltpu.roll(here, 1, 1))
            c_e = jnp.where(lane == 127, pltpu.roll(edge_r, 127 - k, 1), pltpu.roll(here, 127, 1))
            v_w = jnp.where(lane == 0, pltpu.roll(edge_l, 128 - kv, 1), pltpu.roll(wind, 1, 1))
            v_e = jnp.where(lane == 127, pltpu.roll(edge_r, 127 - kv, 1), pltpu.roll(wind, 127, 1))
            c_n = px[l, r - 1 : r + 7, :]
            c_s = px[l, r + 1 : r + 9, :]
            flow = px[4 + l, r : r + 8, :]
            u_lo = 0.5 * (px[4 + l, r - 1 : r + 7, :] + flow)
            u_hi = 0.5 * (flow + px[4 + l, r + 1 : r + 9, :])
            v_lo = 0.5 * (v_w + wind)
            v_hi = 0.5 * (wind + v_e)
            value = (
                here
                - ((pos(u_hi) * here + neg(u_hi) * c_s) - (pos(u_lo) * c_n + neg(u_lo) * here))
                - ((pos(v_hi) * here + neg(v_hi) * c_e) - (pos(v_lo) * c_w + neg(v_lo) * here))
                + MIX * (c_n + c_s + c_w + c_e - 4.0 * here)
            )
            if l < LEV - 1:
                value = value + between[l]
            if l > 0:
                value = value - between[l - 1]
            stepped[l, q, :] = value


def place_kernel(rows, offs, left, height, width, stepped, got, out, s, sems):
    t = lax.axis_index("tile")
    g = lax.axis_index("grp")
    n = nest_over(rows, g)
    lf = left[n]
    wd = width[n]

    @pl.when((lf < COLS * t + COLS) & (lf + wd > COLS * t))
    def _():
        off = offs[n]
        base = pl.multiple_of(lax.div(off, 8) * 8, 8)
        load_s = pltpu.make_async_copy(stepped.at[:, pl.ds(base, 40), :], s, sems.at[0])
        load_s.start()
        lane = lanes((FR, 128)) + COLS * t
        row = lax.broadcasted_iota(jnp.int32, (FR, 128), 0)
        covered = (lane >= lf) & (lane < lf + wd) & (row < height[n])
        load_s.wait()
        for l in range(LEV):
            turned = pltpu.roll(got[n], lax.rem(lf - COLS * t - 32 * l + 2048, 128), 1)
            at = pl.ds(off - base, FR)
            s[l, at, :] = jnp.where(covered, turned, s[l, at, :])
        store = pltpu.make_async_copy(s, out.at[:, pl.ds(base, 40), :], sems.at[1])
        store.start()
        store.wait()


def shards(so2, east, north, diff, nest, rows, offs, left, height, width):
    f32 = jnp.float32
    shape = jax.ShapeDtypeStruct
    dma = pltpu.SemaphoreType.DMA
    field = functools.partial(pltpu.VMEM, dtype=f32)
    near = functools.partial(pltpu.with_memory_space_constraint, memory_space=pltpu.VMEM)
    send, edges = pl.pallas_call(
        pack_kernel,
        out_shape=(field((TILES, WIN + 8 + HALO, 128)), field((16, 128))),
        in_specs=[SMEM] * 3 + [ANY] * 5,
        out_specs=(VMEM, VMEM),
        scratch_shapes=[field((16, ROWS + 8, 128)), field((LEV, OWN, WIDE)), dma((5,))],
        name="pack",
    )(rows, offs, left, so2, east, north, diff, nest)
    got_tile = near(lax.all_to_all(send, "tile", 0, 0))
    send = pl.pallas_call(
        merge_kernel,
        out_shape=field((GROUPS, WIN + 8, 128)),
        in_specs=[SMEM] * 2 + [VMEM, VMEM],
        out_specs=VMEM,
        name="merge",
    )(rows, left, got_tile, near(edges))
    got_grp = near(lax.all_to_all(send, "grp", 0, 0))
    nest_next, back, stepped = pl.pallas_call(
        fine_kernel,
        out_shape=(
            shape((1, LEV, OWN, WIDE), f32),
            field((GROUPS * TILES, 4, 128)),
            shape((LEV, ROWS, COLS), f32),
        ),
        in_specs=[SMEM] * 4 + [VMEM] * 2 + [ANY] * 5,
        out_specs=(VMEM, VMEM, VMEM),
        scratch_shapes=[
            field((LEV, OWN, WIDE)),
            field((8, ROWS + 16, 128)),
            field((8, ROWS, 128)),
            field((16, 3, 8, 128)),
            field((2, LEV, 3, 80, 128)),
            field((LEV, 3, 80, 128)),
            field((LEV, 3, 80, 128)),
            field((LEV - 1, 3, 64, 128)),
            field((LEV, 3, 80, 128)),
            field((LEV, 3, 64, 128)),
            field((LEV, 3, 64, 128)),
            field((LEV, 3, 64, 128)),
            field((LEV, 3, 64, 128)),
            field((LEV, 3, 64, 128)),
            field((3, 16, 128)),
            dma((5,)),
        ],
        name="fine",
    )(rows, left, height, width, got_tile, got_grp, nest, so2, east, north, diff)
    got = lax.all_to_all(back, ("grp", "tile"), 0, 0)
    got = near(got.reshape(GROUPS, FR, 128))
    parent_next = pl.pallas_call(
        place_kernel,
        out_shape=shape((LEV, ROWS, COLS), f32),
        in_specs=[SMEM] * 5 + [ANY, VMEM],
        out_specs=ANY,
        scratch_shapes=[field((LEV, 40, 128)), dma((2,))],
        input_output_aliases={5: 0},
        name="place",
    )(rows, offs, left, height, width, stepped, got)
    return parent_next, nest_next


def solution(mesh):
    in_specs = (
        P(None, "grp", "tile"),
        P(None, "grp", "tile"),
        P(None, "grp", "tile"),
        P(None, "grp", "tile"),
        P("grp", None, "tile", None),
        P(),
        P(),
        P(),
        P(),
        P(),
    )
    out_specs = (P(None, "grp", "tile"), P("grp", None, "tile", None))
    return jax.shard_map(shards, mesh=mesh, in_specs=in_specs, out_specs=out_specs, check_vma=False)
```

```python
import functools
import jax
import jax.numpy as jnp
from jax import lax
from jax.experimental import pallas as pl
from jax.experimental.pallas import tpu as pltpu
from jax.sharding import PartitionSpec as P

RATIO = 10
FR = 32
LEV = 4
ROWS = 64
COLS = 128
OWN = 40
WIDE = 320
GROUPS = 16
TILES = 8
SPAN = FR + 2
WIN = 40
HALO = 120
MIX = 0.02

SMEM = pl.BlockSpec(memory_space=pltpu.SMEM)
ANY = pl.BlockSpec(memory_space=pl.ANY)
VMEM = pl.BlockSpec(memory_space=pltpu.VMEM)


def width_of(chunk):
    return min(128, WIDE - 128 * chunk)


def nest_over(rows, group):
    found = jnp.int32(0)
    for i in range(GROUPS):
        found = jnp.where(rows[i] == group, jnp.int32(i), found)
    return found


def lanes(shape):
    return lax.broadcasted_iota(jnp.int32, shape, 1)


def pack_kernel(rows, offs, left, so2, east, north, diff, nest, send, edges, x, nx, sems):
    t = lax.axis_index("tile")
    g = lax.axis_index("grp")
    loads = [
        pltpu.make_async_copy(f, x.at[pl.ds(4 * i, 4), pl.ds(0, ROWS), :], sems.at[i])
        for i, f in enumerate((so2, east, north, diff))
    ]
    loads.append(pltpu.make_async_copy(nest.at[0], nx, sems.at[4]))
    for c in loads:
        c.start()
    n = nest_over(rows, g)
    top = offs[n] - 1
    base = 128 * t + 1 - left[n] + 1024
    x[:, ROWS : ROWS + 8, :] = jnp.zeros((16, 8, 128), jnp.float32)
    lane = lanes((8, 128))
    before = jnp.where(t > 0, t - 1, t + 2)
    after = jnp.where(t < TILES - 1, t + 1, t - 2)
    loads[4].wait()
    for l in range(LEV):
        for m in range(3):
            w = width_of(m)
            at = 10 * (3 * l + m)
            rows_at = pl.ds(WIN + 8 + at, 10)
            send[before, rows_at, 0:w] = nx[l, 0:10, 128 * m : 128 * m + w]
            send[after, rows_at, 0:w] = nx[l, OWN - 10 : OWN, 128 * m : 128 * m + w]
    for c in loads[:4]:
        c.wait()
    for l in range(LEV):
        edges[l : l + 1, :] = x[l, 0:1, :]
        edges[4 + l : 5 + l, :] = x[4 + l, 0:1, :]
        edges[8 + l : 9 + l, :] = x[l, ROWS - 1 : ROWS, :]
        edges[12 + l : 13 + l, :] = x[4 + l, ROWS - 1 : ROWS, :]
    first = jnp.zeros((8, 128), jnp.float32)
    last = jnp.zeros((8, 128), jnp.float32)
    for p in range(8):
        plane = p if p < 4 else p + 4
        for b in range(8):
            k = 8 * p + b
            v = x[plane, 8 * b : 8 * b + 8, :]
            first = jnp.where(lane == k, pltpu.roll(v, k, 1), first)
            last = jnp.where(lane == k, pltpu.roll(v, k + 1, 1), last)
    shifts = [lax.rem(base + SPAN * f, 128) for f in range(3)]
    kshifts = [lax.rem(base + 32 * l - 1, 128) for l in range(LEV)]
    for d in range(TILES):
        for l in range(LEV):
            part = [
                pltpu.roll(x[4 * f + l, pl.ds(top + 4 * d, 8), :], shifts[f], 1) for f in range(3)
            ]
            send[d, 8 * l : 8 * l + 8, :] = jnp.where(
                lane < SPAN, part[0], jnp.where(lane < 2 * SPAN, part[1], part[2])
            )
        part = [pltpu.roll(x[12 + l, pl.ds(top + 4 * d, 8), :], kshifts[l], 1) for l in range(LEV)]
        send[d, 32:40, :] = jnp.where(
            lane < 64,
            jnp.where(lane < 32, part[0], part[1]),
            jnp.where(lane < 96, part[2], part[3]),
        )
        send[d, 40:48, :] = jnp.where(d < t, first, last)


def merge_kernel(rows, left, got, edges, send):
    g = lax.axis_index("grp")
    n = nest_over(rows, g)
    start = left[n] - 1
    first = lax.div(start, COLS)
    second = jnp.minimum(first + 1, TILES - 1)
    send[jnp.where(g > 0, g - 1, g + 2), WIN : WIN + 8, :] = edges[0:8, :]
    send[jnp.where(g < GROUPS - 1, g + 1, g - 2), WIN : WIN + 8, :] = edges[8:16, :]
    room = COLS - (start - COLS * first)
    lane = lanes((8, 128))
    col = lane - jnp.where(lane >= SPAN, SPAN, 0) - jnp.where(lane >= 2 * SPAN, SPAN, 0)
    kcol = (lane & 31) + 1
    for l in range(5):
        q = slice(8 * l, 8 * l + 8)
        here = (col if l < 4 else kcol) < room
        send[n, q, :] = jnp.where(here, got[first, q, :], got[second, q, :])


def from_left(chunks, lane):
    turned = [pltpu.roll(c, 1, 1) for c in chunks]
    return [jnp.where(lane == 0, turned[m - 1], turned[m]) for m in range(3)]


def from_right(chunks, lane):
    turned = [pltpu.roll(c, 127, 1) for c in chunks]
    return [jnp.where(lane == 127, turned[(m + 1) % 3], turned[m]) for m in range(3)]


def pos(v):
    return jnp.maximum(v, 0.0)


def neg(v):
    return jnp.minimum(v, 0.0)


def fine_kernel(
    rows, left, height, width, got_tile, got_grp, nest,
    fine_out, back,
    nx, e, c, u, v, kz, raw, am, ap, bm, bp, ac, sums, sems,
):
    t = lax.axis_index("tile")
    g = lax.axis_index("grp")
    src = rows[g]
    prev_t = jnp.maximum(t - 1, 0)
    next_t = jnp.minimum(t + 1, TILES - 1)
    load = pltpu.make_async_copy(nest.at[0], nx, sems.at[0])
    load.start()
    lane = lanes((8, 128))
    sub = lax.broadcasted_iota(jnp.int32, (8, 128), 0)
    zero = jnp.zeros((8, 128), jnp.float32)
    for p in range(2):
        for l in range(LEV):
            for m in range(3):
                c[p, l, m, 0:8, :] = zero
                c[p, l, m, 72:80, :] = zero
    for m in range(3):
        fine_col = 128 * m + lane
        under = (fine_col * 6554) >> 16
        pick = jnp.where(fine_col < WIDE, under + 1, jnp.where(fine_col == WIDE, SPAN - 1, 0))
        kpick = jnp.minimum(under, FR - 1)
        for l in range(LEV):
            block = got_grp[src, 8 * l : 8 * l + 8, :]
            for f in range(3):
                e[4 * f + l, m] = jnp.take_along_axis(block, pick + SPAN * f, axis=1)
            e[12 + l, m] = jnp.take_along_axis(got_grp[src, 32:40, :], kpick + 32 * l, axis=1)
    load.wait()
    for l in range(LEV):
        for m in range(3):
            n = width_of(m)
            at = 10 * (3 * l + m)
            raw[l, m, 8:18, :] = got_tile[prev_t, pl.ds(WIN + 8 + at, 10), :]
            raw[l, m, 18:58, 0:n] = nx[l, :, 128 * m : 128 * m + n]
            raw[l, m, 58:68, :] = got_tile[next_t, pl.ds(WIN + 8 + at, 10), :]
    last_row = RATIO * height[g]
    last_col = RATIO * width[g]
    first_row = OWN * t - 10

    def spread(p, m, i):
        lo, hi = (8 * i) // 10, min((8 * i + 7) // 10, 5)
        low = jnp.broadcast_to(e[p, m, lo : lo + 1, :], (8, 128))
        if lo == hi:
            return low
        high = jnp.broadcast_to(e[p, m, hi : hi + 1, :], (8, 128))
        return jnp.where(sub < 10 * hi - 8 * i, low, high)

    for i in range(8):
        r = 8 + 8 * i
        row = first_row + 8 * i + sub
        row_in = (row >= 0) & (row < last_row)
        for m in range(3):
            active = row_in & (128 * m + lane < last_col)
            for l in range(LEV):
                c[0, l, m, r : r + 8, :] = jnp.where(active, raw[l, m, r : r + 8, :], spread(l, m, i))
                u[l, m, r : r + 8, :] = spread(4 + l, m, i)
                v[l, m, r : r + 8, :] = spread(8 + l, m, i)
    for i in range(8):
        r = 8 + 8 * i
        local = 8 * i + sub
        row = first_row + local
        row_in = (row >= 0) & (row < last_row) & (local >= 1) & (local <= 58)
        inside = [row_in & (128 * m + lane < last_col) for m in range(3)]
        faces = []
        for m in range(3):
            ks = [spread(12 + l, m, i) for l in range(LEV)]
            faces.append([(0.05 * (ks[l] + ks[l + 1])) for l in range(LEV - 1)])
            for l in range(LEV - 1):
                kz[l, m, 8 * i : 8 * i + 8, :] = jnp.where(inside[m], faces[m][l], 0.0)
        for l in range(LEV):
            vs = [v[l, m, r : r + 8, :] for m in range(3)]
            before = from_left(vs, lane)
            after = from_right(vs, lane)
            for m in range(3):
                here = u[l, m, r : r + 8, :]
                u_lo = 0.5 * (u[l, m, r - 1 : r + 7, :] + here)
                u_hi = 0.5 * (here + u[l, m, r + 1 : r + 9, :])
                v_lo = 0.5 * (before[m] + vs[m])
                v_hi = 0.5 * (vs[m] + after[m])
                mid = (1.0 - 4.0 * MIX) - pos(u_hi) + neg(u_lo) - pos(v_hi) + neg(v_lo)
                if l > 0:
                    mid = mid - faces[m][l - 1]
                if l < LEV - 1:
                    mid = mid - faces[m][l]
                q = slice(8 * i, 8 * i + 8)
                ac[l, m, q, :] = jnp.where(inside[m], mid, 1.0)
                am[l, m, q, :] = jnp.where(inside[m], MIX + pos(u_lo), 0.0)
                ap[l, m, q, :] = jnp.where(inside[m], MIX - neg(u_hi), 0.0)
                bm[l, m, q, :] = jnp.where(inside[m], MIX + pos(v_lo), 0.0)
                bp[l, m, q, :] = jnp.where(inside[m], MIX - neg(v_hi), 0.0)

    def advance(old, new):
        for i in range(8):
            r = 8 + 8 * i
            q = slice(8 * i, 8 * i + 8)
            now = [[c[old, l, m, r : r + 8, :] for m in range(3)] for l in range(LEV)]
            flow = [[kz[l, m, q, :] for m in range(3)] for l in range(LEV - 1)]
            for l in range(LEV):
                before = from_left(now[l], lane)
                after = from_right(now[l], lane)
                for m in range(3):
                    value = ac[l, m, q, :] * now[l][m]
                    value = value + am[l, m, q, :] * c[old, l, m, r - 1 : r + 7, :]
                    value = value + ap[l, m, q, :] * c[old, l, m, r + 1 : r + 9, :]
                    value = value + bm[l, m, q, :] * before[m]
                    value = value + bp[l, m, q, :] * after[m]
                    if l > 0:
                        value = value + flow[l - 1][m] * now[l - 1][m]
                    if l < LEV - 1:
                        value = value + flow[l][m] * now[l + 1][m]
                    c[new, l, m, r : r + 8, :] = value

    def pair(_, carry):
        advance(0, 1)
        advance(1, 0)
        return carry

    lax.fori_loop(0, RATIO // 2, pair, 0)
    for l in range(LEV):
        for m in range(3):
            n = width_of(m)
            fine_out[0, l, :, 128 * m : 128 * m + n] = c[0, l, m, 18:58, 0:n]
            for a in range(4):
                band = c[0, l, m, 18 + 10 * a : 28 + 10 * a, :]
                sums[m, 4 * l + a : 4 * l + a + 1, :] = jnp.sum(band, axis=0, keepdims=True)
    mean = jnp.zeros((16, 128), jnp.float32)
    for m in range(3):
        k = 128 * m + lax.broadcasted_iota(jnp.int32, (128, 128), 0)
        chosen = ((k * 6554) >> 16) == lanes((128, 128))
        pick = jnp.where(chosen & (k < WIDE), 1.0, 0.0)
        mean = mean + jnp.dot(
            sums[m], pick, precision=lax.Precision.HIGHEST, preferred_element_type=jnp.float32
        )
    mean = mean * (1.0 / (RATIO * RATIO))
    lane4 = lanes((4, 128))
    value = jnp.zeros((4, 128), jnp.float32)
    turned = [mean if l == 0 else pltpu.roll(mean, 32 * l, 1) for l in range(LEV)]
    for l in range(LEV):
        inside = (lane4 >= 32 * l) & (lane4 < 32 * l + 32)
        value = jnp.where(inside, turned[l][4 * l : 4 * l + 4, :], value)
    tile_a = lax.div(left[g], COLS)
    tile_b = jnp.where(tile_a < TILES - 1, tile_a + 1, tile_a - 1)
    back[TILES * src + tile_a] = value
    back[TILES * src + tile_b] = value


def step_kernel(got_tile, got_grp, so2, east, north, diff, stepped, px, vk, sems):
    t = lax.axis_index("tile")
    g = lax.axis_index("grp")
    prev_t = jnp.maximum(t - 1, 0)
    next_t = jnp.minimum(t + 1, TILES - 1)
    prev_g = jnp.maximum(g - 1, 0)
    next_g = jnp.minimum(g + 1, GROUPS - 1)
    copies = [
        (so2, px.at[pl.ds(0, 4), pl.ds(8, ROWS), :]),
        (east, px.at[pl.ds(4, 4), pl.ds(8, ROWS), :]),
        (north, vk.at[pl.ds(0, 4)]),
        (diff, vk.at[pl.ds(4, 4)]),
    ]
    copies = [pltpu.make_async_copy(s, d, sems.at[i]) for i, (s, d) in enumerate(copies)]
    for copy in copies:
        copy.start()
    lane = lanes((8, 128))
    for copy in copies:
        copy.wait()
    for p in range(8):
        px[p, 7:8, :] = jnp.where(g > 0, got_grp[prev_g, WIN + p : WIN + p + 1, :], 0.0)
        px[p, 72:73, :] = jnp.where(g < GROUPS - 1, got_grp[next_g, WIN + p : WIN + p + 1, :], 0.0)
    edge_l = jnp.where(t > 0, got_tile[prev_t, WIN : WIN + 8, :], 0.0)
    edge_r = jnp.where(t < TILES - 1, got_tile[next_t, WIN : WIN + 8, :], 0.0)
    for b in range(8):
        r = 8 + 8 * b
        q = slice(8 * b, 8 * b + 8)
        now = [px[l, r : r + 8, :] for l in range(LEV)]
        ks = [vk[4 + l, q, :] for l in range(LEV)]
        between = [0.5 * (ks[l] + ks[l + 1]) * (now[l + 1] - now[l]) for l in range(LEV - 1)]
        for l in range(LEV):
            here = now[l]
            k, kv = 8 * l + b, 32 + 8 * l + b
            wind = vk[l, q, :]
            c_w = jnp.where(lane == 0, pltpu.roll(edge_l, (128 - k) % 128, 1), pltpu.roll(here, 1, 1))
            c_e = jnp.where(lane == 127, pltpu.roll(edge_r, 127 - k, 1), pltpu.roll(here, 127, 1))
            v_w = jnp.where(lane == 0, pltpu.roll(edge_l, 128 - kv, 1), pltpu.roll(wind, 1, 1))
            v_e = jnp.where(lane == 127, pltpu.roll(edge_r, 127 - kv, 1), pltpu.roll(wind, 127, 1))
            c_n = px[l, r - 1 : r + 7, :]
            c_s = px[l, r + 1 : r + 9, :]
            flow = px[4 + l, r : r + 8, :]
            u_lo = 0.5 * (px[4 + l, r - 1 : r + 7, :] + flow)
            u_hi = 0.5 * (flow + px[4 + l, r + 1 : r + 9, :])
            v_lo = 0.5 * (v_w + wind)
            v_hi = 0.5 * (wind + v_e)
            value = (
                here
                - ((pos(u_hi) * here + neg(u_hi) * c_s) - (pos(u_lo) * c_n + neg(u_lo) * here))
                - ((pos(v_hi) * here + neg(v_hi) * c_e) - (pos(v_lo) * c_w + neg(v_lo) * here))
                + MIX * (c_n + c_s + c_w + c_e - 4.0 * here)
            )
            if l < LEV - 1:
                value = value + between[l]
            if l > 0:
                value = value - between[l - 1]
            stepped[l, q, :] = value


def place_kernel(rows, offs, left, height, width, stepped, got, out, s, sems):
    t = lax.axis_index("tile")
    g = lax.axis_index("grp")
    n = nest_over(rows, g)
    lf = left[n]
    wd = width[n]

    @pl.when((lf < COLS * t + COLS) & (lf + wd > COLS * t))
    def _():
        off = offs[n]
        base = pl.multiple_of(lax.div(off, 8) * 8, 8)
        load_s = pltpu.make_async_copy(stepped.at[:, pl.ds(base, 40), :], s, sems.at[0])
        load_s.start()
        lane = lanes((FR, 128)) + COLS * t
        row = lax.broadcasted_iota(jnp.int32, (FR, 128), 0)
        covered = (lane >= lf) & (lane < lf + wd) & (row < height[n])
        load_s.wait()
        for l in range(LEV):
            turned = pltpu.roll(got[n], lax.rem(lf - COLS * t - 32 * l + 2048, 128), 1)
            at = pl.ds(off - base, FR)
            s[l, at, :] = jnp.where(covered, turned, s[l, at, :])
        store = pltpu.make_async_copy(s, out.at[:, pl.ds(base, 40), :], sems.at[1])
        store.start()
        store.wait()


def shards(so2, east, north, diff, nest, rows, offs, left, height, width):
    f32 = jnp.float32
    shape = jax.ShapeDtypeStruct
    dma = pltpu.SemaphoreType.DMA
    field = functools.partial(pltpu.VMEM, dtype=f32)
    near = functools.partial(pltpu.with_memory_space_constraint, memory_space=pltpu.VMEM)
    send, edges = pl.pallas_call(
        pack_kernel,
        out_shape=(field((TILES, WIN + 8 + HALO, 128)), field((16, 128))),
        in_specs=[SMEM] * 3 + [ANY] * 5,
        out_specs=(VMEM, VMEM),
        scratch_shapes=[field((16, ROWS + 8, 128)), field((LEV, OWN, WIDE)), dma((5,))],
        name="pack",
    )(rows, offs, left, so2, east, north, diff, nest)
    got_tile = near(lax.all_to_all(send, "tile", 0, 0))
    send = pl.pallas_call(
        merge_kernel,
        out_shape=field((GROUPS, WIN + 8, 128)),
        in_specs=[SMEM] * 2 + [VMEM, VMEM],
        out_specs=VMEM,
        name="merge",
    )(rows, left, got_tile, near(edges))
    got_grp = near(lax.all_to_all(send, "grp", 0, 0))
    nest_next, back = pl.pallas_call(
        fine_kernel,
        out_shape=(
            shape((1, LEV, OWN, WIDE), f32),
            field((GROUPS * TILES, 4, 128)),
        ),
        in_specs=[SMEM] * 4 + [VMEM] * 2 + [ANY],
        out_specs=(VMEM, VMEM),
        scratch_shapes=[
            field((LEV, OWN, WIDE)),
            field((16, 3, 8, 128)),
            field((2, LEV, 3, 80, 128)),
            field((LEV, 3, 80, 128)),
            field((LEV, 3, 80, 128)),
            field((LEV - 1, 3, 64, 128)),
            field((LEV, 3, 80, 128)),
            field((LEV, 3, 64, 128)),
            field((LEV, 3, 64, 128)),
            field((LEV, 3, 64, 128)),
            field((LEV, 3, 64, 128)),
            field((LEV, 3, 64, 128)),
            field((3, 16, 128)),
            dma((1,)),
        ],
        name="fine",
    )(rows, left, height, width, got_tile, got_grp, nest)
    stepped = pl.pallas_call(
        step_kernel,
        out_shape=shape((LEV, ROWS, COLS), f32),
        in_specs=[VMEM] * 2 + [ANY] * 4,
        out_specs=VMEM,
        scratch_shapes=[field((8, ROWS + 16, 128)), field((8, ROWS, 128)), dma((4,))],
        name="step",
    )(got_tile, got_grp, so2, east, north, diff)
    got = lax.all_to_all(back, ("grp", "tile"), 0, 0)
    got = near(got.reshape(GROUPS, FR, 128))
    parent_next = pl.pallas_call(
        place_kernel,
        out_shape=shape((LEV, ROWS, COLS), f32),
        in_specs=[SMEM] * 5 + [ANY, VMEM],
        out_specs=ANY,
        scratch_shapes=[field((LEV, 40, 128)), dma((2,))],
        input_output_aliases={5: 0},
        name="place",
    )(rows, offs, left, height, width, stepped, got)
    return parent_next, nest_next


def solution(mesh):
    in_specs = (
        P(None, "grp", "tile"),
        P(None, "grp", "tile"),
        P(None, "grp", "tile"),
        P(None, "grp", "tile"),
        P("grp", None, "tile", None),
        P(),
        P(),
        P(),
        P(),
        P(),
    )
    out_specs = (P(None, "grp", "tile"), P("grp", None, "tile", None))
    return jax.shard_map(shards, mesh=mesh, in_specs=in_specs, out_specs=out_specs, check_vma=False)
```

```python
import functools
import jax
import jax.numpy as jnp
from jax import lax
from jax.experimental import pallas as pl
from jax.experimental.pallas import tpu as pltpu
from jax.sharding import PartitionSpec as P

RATIO = 10
FR = 32
LEV = 4
ROWS = 64
COLS = 128
OWN = 40
WIDE = 320
GROUPS = 16
TILES = 8
SPAN = FR + 2
WIN = 30
EDGE = 34
SLOT = 136
GSLOT = 40
STARTS = (-1, 107, 215)
TAKEN = (0, 117, 225, 320)
MIX = 0.02

SMEM = pl.BlockSpec(memory_space=pltpu.SMEM)
ANY = pl.BlockSpec(memory_space=pl.ANY)
VMEM = pl.BlockSpec(memory_space=pltpu.VMEM)


def nest_over(rows, group):
    found = jnp.int32(0)
    for i in range(GROUPS):
        found = jnp.where(rows[i] == group, jnp.int32(i), found)
    return found


def lanes(shape):
    return lax.broadcasted_iota(jnp.int32, shape, 1)


def pack_kernel(rows, offs, left, so2, east, north, diff, nest, send, edges, x, nx, sems):
    t = lax.axis_index("tile")
    g = lax.axis_index("grp")
    loads = [
        pltpu.make_async_copy(f, x.at[pl.ds(4 * i, 4), pl.ds(0, ROWS), :], sems.at[i])
        for i, f in enumerate((so2, east, north, diff))
    ]
    loads.append(pltpu.make_async_copy(nest.at[0], nx, sems.at[4]))
    for c in loads:
        c.start()
    n = nest_over(rows, g)
    top = offs[n] - 1
    base = 128 * t + 1 - left[n] + 1024
    x[:, ROWS : ROWS + 8, :] = jnp.zeros((16, 8, 128), jnp.float32)
    lane = lanes((8, 128))
    before = jnp.where(t > 0, t - 1, t + 2)
    after = jnp.where(t < TILES - 1, t + 1, t - 2)
    loads[4].wait()
    for at, source in ((before, 0), (after, OWN - 10)):
        q = slice(source, source + 10)
        for l in range(LEV):
            for m in range(2):
                send[at, pl.ds(EDGE + 10 * (2 * l + m), 10), :] = nx[l, q, 128 * m : 128 * m + 128]
            side = 64 * (l % 2)
            send[at, pl.ds(EDGE + 80 + 10 * (l // 2), 10), side : side + 64] = nx[l, q, 256:320]
    for c in loads[:4]:
        c.wait()
    for l in range(LEV):
        edges[l : l + 1, :] = x[l, 0:1, :]
        edges[4 + l : 5 + l, :] = x[4 + l, 0:1, :]
        edges[8 + l : 9 + l, :] = x[l, ROWS - 1 : ROWS, :]
        edges[12 + l : 13 + l, :] = x[4 + l, ROWS - 1 : ROWS, :]
    first = jnp.zeros((8, 128), jnp.float32)
    last = jnp.zeros((8, 128), jnp.float32)
    for p in range(8):
        plane = p if p < 4 else p + 4
        for b in range(8):
            k = 8 * p + b
            v = x[plane, 8 * b : 8 * b + 8, :]
            first = jnp.where(lane == k, pltpu.roll(v, k, 1), first)
            last = jnp.where(lane == k, pltpu.roll(v, k + 1, 1), last)
    first = jnp.where(lane[0:4] < 64, first[0:4], pltpu.roll(first, 64, 1)[4:8])
    last = jnp.where(lane[0:4] < 64, last[0:4], pltpu.roll(last, 64, 1)[4:8])
    shifts = [lax.rem(base + SPAN * f, 128) for f in range(3)]
    kshifts = [lax.rem(base + 32 * l - 1, 128) for l in range(LEV)]
    for d in range(TILES):
        for l in range(LEV):
            part = [
                pltpu.roll(x[4 * f + l, pl.ds(top + 4 * d, 8), :], shifts[f], 1) for f in range(3)
            ]
            piece = jnp.where(lane < SPAN, part[0], jnp.where(lane < 2 * SPAN, part[1], part[2]))
            send[d, 6 * l : 6 * l + 6, :] = piece[0:6]
        part = [pltpu.roll(x[12 + l, pl.ds(top + 4 * d, 8), :], kshifts[l], 1) for l in range(LEV)]
        piece = jnp.where(
            lane < 64,
            jnp.where(lane < 32, part[0], part[1]),
            jnp.where(lane < 96, part[2], part[3]),
        )
        send[d, 24:WIN, :] = piece[0:6]
        send[d, WIN:EDGE, :] = jnp.where(d < t, first, last)


def merge_kernel(rows, left, got, edges, send):
    g = lax.axis_index("grp")
    n = nest_over(rows, g)
    start = left[n] - 1
    first = lax.div(start, COLS)
    second = jnp.minimum(first + 1, TILES - 1)
    send[jnp.where(g > 0, g - 1, g + 2), WIN : WIN + 8, :] = edges[0:8, :]
    send[jnp.where(g < GROUPS - 1, g + 1, g - 2), WIN : WIN + 8, :] = edges[8:16, :]
    room = COLS - (start - COLS * first)
    lane = lanes((8, 128))
    col = lane - jnp.where(lane >= SPAN, SPAN, 0) - jnp.where(lane >= 2 * SPAN, SPAN, 0)
    kcol = (lane & 31) + 1
    for l in range(3):
        q = slice(8 * l, 8 * l + 8)
        send[n, q, :] = jnp.where(col < room, got[first, q, :], got[second, q, :])
    q = slice(24, WIN)
    send[n, q, :] = jnp.where(kcol[0:6] < room, got[first, q, :], got[second, q, :])


def pos(v):
    return jnp.maximum(v, 0.0)


def neg(v):
    return jnp.minimum(v, 0.0)


def fine_kernel(
    rows, left, height, width, got_tile, got_grp, nest,
    c, back,
    nx, third, e, raw, am, ap, bm, bp, ac, kz, sums, sems,
):
    t = lax.axis_index("tile")
    g = lax.axis_index("grp")
    src = rows[g]
    prev_t = jnp.maximum(t - 1, 0)
    next_t = jnp.minimum(t + 1, TILES - 1)
    load = pltpu.make_async_copy(nest.at[0], nx, sems.at[0])
    load.start()
    lane = lanes((8, 128))
    sub = lax.broadcasted_iota(jnp.int32, (8, 128), 0)
    zero = jnp.zeros((8, 128), jnp.float32)
    for l in range(LEV):
        for m in range(3):
            raw[l, m, 56:64, :] = zero
            for p in range(2):
                c[p, l, m, 0:8, :] = zero
                c[p, l, m, 72:80, :] = zero

    above = OWN // RATIO * t - 1 + sub
    row_in = (above >= 0) & (above < height[g])
    coarse = {}
    for m in range(3):
        col = STARTS[m] + lane
        under = (jnp.maximum(col, 0) * 6554) >> 16
        pick = jnp.where(col < 0, 0, jnp.where(col < WIDE, under + 1, SPAN - 1))
        kpick = jnp.minimum(under, FR - 1)
        inside = row_in & (col >= 0) & (col < RATIO * width[g])
        block = got_grp[src, 24:32, :]
        ks = [jnp.take_along_axis(block, kpick + 32 * l, axis=1) for l in range(LEV)]
        faces = [0.05 * (ks[l] + ks[l + 1]) for l in range(LEV - 1)]
        for l in range(LEV - 1):
            e[10 * LEV + l, m] = jnp.where(inside, faces[l], 0.0)
        for l in range(LEV):
            block = got_grp[src, 6 * l : 6 * l + 8, :]
            e[l, m] = jnp.take_along_axis(block, pick, axis=1)
            u = jnp.take_along_axis(block, pick + SPAN, axis=1)
            v = jnp.take_along_axis(block, pick + 2 * SPAN, axis=1)
            u_lo = 0.5 * (pltpu.roll(u, 1, 0) + u)
            u_hi = 0.5 * (u + pltpu.roll(u, 7, 0))
            v_lo = 0.5 * (pltpu.roll(v, 1, 1) + v)
            v_hi = 0.5 * (v + pltpu.roll(v, 127, 1))
            rest = (1.0 - 4.0 * MIX) - pos(v_hi) + neg(v_lo)
            if l > 0:
                rest = rest - faces[l - 1]
            if l < LEV - 1:
                rest = rest - faces[l]
            values = (
                rest - pos(u) + neg(u),
                rest - pos(u) + neg(u_lo),
                rest - pos(u_hi) + neg(u),
                MIX + pos(u),
                MIX + pos(u_lo),
                MIX - neg(u),
                MIX - neg(u_hi),
                MIX + pos(v_lo),
                MIX - neg(v_hi),
            )
            for k, value in enumerate(values):
                e[LEV * (k + 1) + l, m] = jnp.where(inside, value, 1.0 if k < 3 else 0.0)

    def spread(p, m, i):
        lo, hi = (8 * i) // 10, min((8 * i + 7) // 10, 5)
        low = jnp.broadcast_to(e[p, m, lo : lo + 1, :], (8, 128))
        if lo == hi:
            return low
        high = jnp.broadcast_to(e[p, m, hi : hi + 1, :], (8, 128))
        return jnp.where(sub < 10 * hi - 8 * i, low, high)

    def at_row(value, p, m, i, last):
        for k in range(6):
            at = 10 * k + (9 if last else 0) - 8 * i
            if 0 <= at < 8:
                value = jnp.where(sub == at, jnp.broadcast_to(e[p, m, k : k + 1, :], (8, 128)), value)
        return value

    for i in range(8):
        q = slice(8 * i, 8 * i + 8)
        for m in range(3):
            for l in range(LEV - 1):
                kz[l, m, q, :] = spread(10 * LEV + l, m, i)
            for l in range(LEV):
                mid = at_row(spread(LEV + l, m, i), 2 * LEV + l, m, i, False)
                ac[l, m, q, :] = at_row(mid, 3 * LEV + l, m, i, True)
                am[l, m, q, :] = at_row(spread(4 * LEV + l, m, i), 5 * LEV + l, m, i, False)
                ap[l, m, q, :] = at_row(spread(6 * LEV + l, m, i), 7 * LEV + l, m, i, True)
                bm[l, m, q, :] = spread(8 * LEV + l, m, i)
                bp[l, m, q, :] = spread(9 * LEV + l, m, i)

    load.wait()

    def lay(l, at, n, parts, turn):
        wide = lanes((n, 128))
        raw[l, 0, at : at + n, :] = pltpu.roll(parts[0], 1, 1)
        raw[l, 1, at : at + n, :] = jnp.where(
            wide < 21, pltpu.roll(parts[0], 21, 1), pltpu.roll(parts[1], 21, 1)
        )
        raw[l, 2, at : at + n, :] = jnp.where(
            wide < 41, pltpu.roll(parts[1], 41, 1), pltpu.roll(parts[2], turn, 1)
        )

    for l in range(LEV):
        third[l, :, 0:64] = nx[l, :, 256:320]
        lay(l, 10, OWN, (nx[l, :, 0:128], nx[l, :, 128:256], third[l]), 41)
        turn = 41 if l % 2 == 0 else 105
        for tile, at in ((prev_t, 0), (next_t, OWN + 10)):
            spots = (EDGE + 20 * l, EDGE + 20 * l + 10, EDGE + 80 + 10 * (l // 2))
            lay(l, at, 10, [got_tile[tile, k : k + 10, :] for k in spots], turn)
    last_row = RATIO * height[g]
    first_row = OWN * t - 10
    for i in range(8):
        r = 8 + 8 * i
        row = first_row + 8 * i + sub
        row_in = (row >= 0) & (row < last_row)
        for m in range(3):
            col = STARTS[m] + lane
            active = row_in & (col >= 0) & (col < RATIO * width[g])
            for l in range(LEV):
                c[0, l, m, r : r + 8, :] = jnp.where(active, raw[l, m, r - 8 : r, :], spread(l, m, i))

    def advance(old, new, tiles):
        for m in range(3):
            for i in tiles:
                r = 8 + 8 * i
                q = slice(8 * i, 8 * i + 8)
                now = [c[old, l, m, r : r + 8, :] for l in range(LEV)]
                flow = [kz[l, m, q, :] for l in range(LEV - 1)]
                for l in range(LEV):
                    value = ac[l, m, q, :] * now[l]
                    value = value + am[l, m, q, :] * c[old, l, m, r - 1 : r + 7, :]
                    value = value + ap[l, m, q, :] * c[old, l, m, r + 1 : r + 9, :]
                    value = value + bm[l, m, q, :] * pltpu.roll(now[l], 1, 1)
                    value = value + bp[l, m, q, :] * pltpu.roll(now[l], 127, 1)
                    if l > 0:
                        value = value + flow[l - 1] * now[l - 1]
                    if l < LEV - 1:
                        value = value + flow[l] * now[l + 1]
                    c[new, l, m, r : r + 8, :] = value

    def steps(first, last, tiles):
        def body(k, carry):
            old = lax.rem(k, 2)
            advance(old, 1 - old, tiles)
            return carry

        lax.fori_loop(first, last, body, 0)

    steps(0, 3, range(8))
    steps(3, 7, range(7))
    steps(7, RATIO, range(1, 7))
    for l in range(LEV):
        for m in range(3):
            for a in range(4):
                band = c[0, l, m, 18 + 10 * a : 28 + 10 * a, :]
                sums[m, 4 * l + a : 4 * l + a + 1, :] = jnp.sum(band, axis=0, keepdims=True)
    mean = jnp.zeros((16, 128), jnp.float32)
    for m in range(3):
        col = STARTS[m] + lax.broadcasted_iota(jnp.int32, (128, 128), 0)
        chosen = ((jnp.maximum(col, 0) * 6554) >> 16) == lanes((128, 128))
        chosen = chosen & (col >= TAKEN[m]) & (col < TAKEN[m + 1])
        pick = jnp.where(chosen, 1.0, 0.0)
        mean = mean + jnp.dot(
            sums[m], pick, precision=lax.Precision.HIGHEST, preferred_element_type=jnp.float32
        )
    mean = mean * (1.0 / (RATIO * RATIO))
    lane4 = lanes((4, 128))
    value = jnp.zeros((4, 128), jnp.float32)
    turned = [mean if l == 0 else pltpu.roll(mean, 32 * l, 1) for l in range(LEV)]
    for l in range(LEV):
        inside = (lane4 >= 32 * l) & (lane4 < 32 * l + 32)
        value = jnp.where(inside, turned[l][4 * l : 4 * l + 4, :], value)
    tile_a = lax.div(left[g], COLS)
    tile_b = jnp.where(tile_a < TILES - 1, tile_a + 1, tile_a - 1)
    back[TILES * src + tile_a] = value
    back[TILES * src + tile_b] = value


def finish_kernel(got_tile, got_grp, c, so2, east, north, diff, stepped, fine_out, px, vk, ed, sems):
    t = lax.axis_index("tile")
    g = lax.axis_index("grp")
    prev_t = jnp.maximum(t - 1, 0)
    next_t = jnp.minimum(t + 1, TILES - 1)
    prev_g = jnp.maximum(g - 1, 0)
    next_g = jnp.minimum(g + 1, GROUPS - 1)
    copies = [
        (so2, px.at[pl.ds(0, 4), pl.ds(8, ROWS), :]),
        (east, px.at[pl.ds(4, 4), pl.ds(8, ROWS), :]),
        (north, vk.at[pl.ds(0, 4)]),
        (diff, vk.at[pl.ds(4, 4)]),
    ]
    copies = [pltpu.make_async_copy(s, d, sems.at[i]) for i, (s, d) in enumerate(copies)]
    for copy in copies:
        copy.start()
    lane = lanes((8, 128))
    wide = lanes((OWN, 128))
    for l in range(LEV):
        turned = [pltpu.roll(c[0, l, m, 18:58, :], by, 1) for m, by in enumerate((127, 107, 87))]
        fine_out[0, l, :, 0:128] = jnp.where(wide < 117, turned[0], turned[1])
        fine_out[0, l, :, 128:256] = jnp.where(wide < 97, turned[1], turned[2])
        fine_out[0, l, :, 256:320] = turned[2][:, 0:64]
    for copy in copies:
        copy.wait()
    for p in range(8):
        px[p, 7:8, :] = jnp.where(g > 0, got_grp[prev_g, WIN + p : WIN + p + 1, :], 0.0)
        px[p, 72:73, :] = jnp.where(g < GROUPS - 1, got_grp[next_g, WIN + p : WIN + p + 1, :], 0.0)
    for k, tile in enumerate((prev_t, next_t)):
        packed = got_tile[tile, WIN : WIN + 8, :]
        ed[k, 0:4, :] = packed[0:4]
        ed[k, 4:8, :] = pltpu.roll(packed, 64, 1)[0:4]
    edge_l = jnp.where(t > 0, ed[0], 0.0)
    edge_r = jnp.where(t < TILES - 1, ed[1], 0.0)
    for b in range(8):
        r = 8 + 8 * b
        q = slice(8 * b, 8 * b + 8)
        now = [px[l, r : r + 8, :] for l in range(LEV)]
        ks = [vk[4 + l, q, :] for l in range(LEV)]
        between = [0.5 * (ks[l] + ks[l + 1]) * (now[l + 1] - now[l]) for l in range(LEV - 1)]
        for l in range(LEV):
            here = now[l]
            k, kv = 8 * l + b, 32 + 8 * l + b
            wind = vk[l, q, :]
            c_w = jnp.where(lane == 0, pltpu.roll(edge_l, (128 - k) % 128, 1), pltpu.roll(here, 1, 1))
            c_e = jnp.where(lane == 127, pltpu.roll(edge_r, 127 - k, 1), pltpu.roll(here, 127, 1))
            v_w = jnp.where(lane == 0, pltpu.roll(edge_l, 128 - kv, 1), pltpu.roll(wind, 1, 1))
            v_e = jnp.where(lane == 127, pltpu.roll(edge_r, 127 - kv, 1), pltpu.roll(wind, 127, 1))
            c_n = px[l, r - 1 : r + 7, :]
            c_s = px[l, r + 1 : r + 9, :]
            flow = px[4 + l, r : r + 8, :]
            u_lo = 0.5 * (px[4 + l, r - 1 : r + 7, :] + flow)
            u_hi = 0.5 * (flow + px[4 + l, r + 1 : r + 9, :])
            v_lo = 0.5 * (v_w + wind)
            v_hi = 0.5 * (wind + v_e)
            value = (
                here
                - ((pos(u_hi) * here + neg(u_hi) * c_s) - (pos(u_lo) * c_n + neg(u_lo) * here))
                - ((pos(v_hi) * here + neg(v_hi) * c_e) - (pos(v_lo) * c_w + neg(v_lo) * here))
                + MIX * (c_n + c_s + c_w + c_e - 4.0 * here)
            )
            if l < LEV - 1:
                value = value + between[l]
            if l > 0:
                value = value - between[l - 1]
            stepped[l, q, :] = value


def place_kernel(rows, offs, left, height, width, stepped, got, out, s, sems):
    t = lax.axis_index("tile")
    g = lax.axis_index("grp")
    n = nest_over(rows, g)
    lf = left[n]
    wd = width[n]

    @pl.when((lf < COLS * t + COLS) & (lf + wd > COLS * t))
    def _():
        off = offs[n]
        base = pl.multiple_of(lax.div(off, 8) * 8, 8)
        load_s = pltpu.make_async_copy(stepped.at[:, pl.ds(base, 40), :], s, sems.at[0])
        load_s.start()
        lane = lanes((FR, 128)) + COLS * t
        row = lax.broadcasted_iota(jnp.int32, (FR, 128), 0)
        covered = (lane >= lf) & (lane < lf + wd) & (row < height[n])
        load_s.wait()
        for l in range(LEV):
            turned = pltpu.roll(got[n], lax.rem(lf - COLS * t - 32 * l + 2048, 128), 1)
            at = pl.ds(off - base, FR)
            s[l, at, :] = jnp.where(covered, turned, s[l, at, :])
        store = pltpu.make_async_copy(s, out.at[:, pl.ds(base, 40), :], sems.at[1])
        store.start()
        store.wait()


def shards(so2, east, north, diff, nest, rows, offs, left, height, width):
    f32 = jnp.float32
    shape = jax.ShapeDtypeStruct
    dma = pltpu.SemaphoreType.DMA
    field = functools.partial(pltpu.VMEM, dtype=f32)
    near = functools.partial(pltpu.with_memory_space_constraint, memory_space=pltpu.VMEM)
    send, edges = pl.pallas_call(
        pack_kernel,
        out_shape=(field((TILES, SLOT, 128)), field((16, 128))),
        in_specs=[SMEM] * 3 + [ANY] * 5,
        out_specs=(VMEM, VMEM),
        scratch_shapes=[field((16, ROWS + 8, 128)), field((LEV, OWN, WIDE)), dma((5,))],
        name="pack",
    )(rows, offs, left, so2, east, north, diff, nest)
    got_tile = near(lax.all_to_all(send, "tile", 0, 0))
    send = pl.pallas_call(
        merge_kernel,
        out_shape=field((GROUPS, GSLOT, 128)),
        in_specs=[SMEM] * 2 + [VMEM, VMEM],
        out_specs=VMEM,
        name="merge",
    )(rows, left, got_tile, near(edges))
    got_grp = near(lax.all_to_all(send, "grp", 0, 0))
    c, back = pl.pallas_call(
        fine_kernel,
        out_shape=(field((2, LEV, 3, 80, 128)), field((GROUPS * TILES, 4, 128))),
        in_specs=[SMEM] * 4 + [VMEM] * 2 + [ANY],
        out_specs=(VMEM, VMEM),
        scratch_shapes=[
            field((LEV, OWN, WIDE)),
            field((LEV, OWN, 128)),
            field((11 * LEV - 1, 3, 8, 128)),
            field((LEV, 3, 64, 128)),
            field((LEV, 3, 64, 128)),
            field((LEV, 3, 64, 128)),
            field((LEV, 3, 64, 128)),
            field((LEV, 3, 64, 128)),
            field((LEV, 3, 64, 128)),
            field((LEV - 1, 3, 64, 128)),
            field((3, 16, 128)),
            dma((1,)),
        ],
        name="fine",
    )(rows, left, height, width, got_tile, got_grp, nest)
    stepped, nest_next = pl.pallas_call(
        finish_kernel,
        out_shape=(shape((LEV, ROWS, COLS), f32), shape((1, LEV, OWN, WIDE), f32)),
        in_specs=[VMEM] * 3 + [ANY] * 4,
        out_specs=(VMEM, VMEM),
        scratch_shapes=[
            field((8, ROWS + 16, 128)),
            field((8, ROWS, 128)),
            field((2, 8, 128)),
            dma((4,)),
        ],
        name="finish",
    )(got_tile, got_grp, near(c), so2, east, north, diff)
    got = lax.all_to_all(back, ("grp", "tile"), 0, 0)
    got = near(got.reshape(GROUPS, FR, 128))
    parent_next = pl.pallas_call(
        place_kernel,
        out_shape=shape((LEV, ROWS, COLS), f32),
        in_specs=[SMEM] * 5 + [ANY, VMEM],
        out_specs=ANY,
        scratch_shapes=[field((LEV, 40, 128)), dma((2,))],
        input_output_aliases={5: 0},
        name="place",
    )(rows, offs, left, height, width, stepped, got)
    return parent_next, nest_next


def solution(mesh):
    in_specs = (
        P(None, "grp", "tile"),
        P(None, "grp", "tile"),
        P(None, "grp", "tile"),
        P(None, "grp", "tile"),
        P("grp", None, "tile", None),
        P(),
        P(),
        P(),
        P(),
        P(),
    )
    out_specs = (P(None, "grp", "tile"), P("grp", None, "tile", None))
    return jax.shard_map(shards, mesh=mesh, in_specs=in_specs, out_specs=out_specs, check_vma=False)
```

```python
import functools
import jax
import jax.numpy as jnp
from jax import lax
from jax.experimental import pallas as pl
from jax.experimental.pallas import tpu as pltpu
from jax.sharding import PartitionSpec as P

RATIO = 10
FR = 32
LEV = 4
ROWS = 64
COLS = 128
OWN = 40
WIDE = 320
GROUPS = 16
TILES = 8
SPAN = FR + 2
WIN = 30
EDGE = 34
SLOT = 136
GSLOT = 40
STARTS = (0, 96, 192)
TAKEN = (0, 117, 203, 320)
MIX = 0.02

SMEM = pl.BlockSpec(memory_space=pltpu.SMEM)
ANY = pl.BlockSpec(memory_space=pl.ANY)
VMEM = pl.BlockSpec(memory_space=pltpu.VMEM)


def nest_over(rows, group):
    found = jnp.int32(0)
    for i in range(GROUPS):
        found = jnp.where(rows[i] == group, jnp.int32(i), found)
    return found


def lanes(shape):
    return lax.broadcasted_iota(jnp.int32, shape, 1)


def pack_kernel(rows, offs, left, so2, east, north, diff, nest, send, edges, x, nx, cut, sems):
    t = lax.axis_index("tile")
    g = lax.axis_index("grp")
    loads = [
        pltpu.make_async_copy(f, x.at[pl.ds(4 * i, 4), pl.ds(0, ROWS), :], sems.at[i])
        for i, f in enumerate((so2, east, north, diff))
    ]
    loads.append(pltpu.make_async_copy(nest.at[0], nx, sems.at[4]))
    for c in loads:
        c.start()
    n = nest_over(rows, g)
    top = offs[n] - 1
    base = 128 * t + 1 - left[n] + 1024
    x[:, ROWS : ROWS + 8, :] = jnp.zeros((16, 8, 128), jnp.float32)
    lane = lanes((8, 128))
    before = jnp.where(t > 0, t - 1, t + 2)
    after = jnp.where(t < TILES - 1, t + 1, t - 2)
    loads[4].wait()
    for at, source in ((before, 0), (after, OWN - 10)):
        q = slice(source, source + 10)
        for l in range(LEV):
            for m in range(2):
                send[at, pl.ds(EDGE + 10 * (2 * l + m), 10), :] = nx[l, q, 128 * m : 128 * m + 128]
            side = 64 * (l % 2)
            send[at, pl.ds(EDGE + 80 + 10 * (l // 2), 10), side : side + 64] = nx[l, q, 256:320]
    for c in loads[:4]:
        c.wait()
    for l in range(LEV):
        edges[l : l + 1, :] = x[l, 0:1, :]
        edges[4 + l : 5 + l, :] = x[4 + l, 0:1, :]
        edges[8 + l : 9 + l, :] = x[l, ROWS - 1 : ROWS, :]
        edges[12 + l : 13 + l, :] = x[4 + l, ROWS - 1 : ROWS, :]
    shifts = [lax.rem(base + SPAN * f, 128) for f in range(3)]
    kshifts = [lax.rem(base + 32 * l - 1, 128) for l in range(LEV)]
    for b in range(5):
        at = pl.ds(top + 8 * b, 8)
        q = slice(8 * b, 8 * b + 8)
        for l in range(LEV):
            part = [pltpu.roll(x[4 * f + l, at, :], shifts[f], 1) for f in range(3)]
            cut[l, q, :] = jnp.where(lane < SPAN, part[0], jnp.where(lane < 2 * SPAN, part[1], part[2]))
        part = [pltpu.roll(x[12 + l, at, :], kshifts[l], 1) for l in range(LEV)]
        cut[4, q, :] = jnp.where(
            lane < 64,
            jnp.where(lane < 32, part[0], part[1]),
            jnp.where(lane < 96, part[2], part[3]),
        )
    sub = lax.broadcasted_iota(jnp.int32, (8, 128), 0)
    ends = jnp.where(((sub == 0) & (lane == 0)) | ((sub == 1) & (lane == 127)), 1.0, 0.0)
    planes = [x[p if p < 4 else p + 4, 0:ROWS, :] for p in range(8)]
    sides = lax.dot_general(
        ends,
        jnp.concatenate(planes, axis=0),
        (((1,), (1,)), ((), ())),
        precision=lax.Precision.HIGHEST,
        preferred_element_type=jnp.float32,
    )
    for d in range(TILES):
        for l in range(5):
            send[d, 6 * l : 6 * l + 6, :] = cut[l, 4 * d : 4 * d + 6, :]
        for k in range(4):
            pair = sides[0:2, 128 * k : 128 * k + 128]
            send[d, WIN + k : WIN + k + 1, :] = jnp.where(d < t, pair[0:1], pair[1:2])


def merge_kernel(rows, left, got, edges, send):
    g = lax.axis_index("grp")
    n = nest_over(rows, g)
    start = left[n] - 1
    first = lax.div(start, COLS)
    second = jnp.minimum(first + 1, TILES - 1)
    send[jnp.where(g > 0, g - 1, g + 2), WIN : WIN + 8, :] = edges[0:8, :]
    send[jnp.where(g < GROUPS - 1, g + 1, g - 2), WIN : WIN + 8, :] = edges[8:16, :]
    room = COLS - (start - COLS * first)
    lane = lanes((8, 128))
    col = lane - jnp.where(lane >= SPAN, SPAN, 0) - jnp.where(lane >= 2 * SPAN, SPAN, 0)
    kcol = (lane & 31) + 1
    for l in range(3):
        q = slice(8 * l, 8 * l + 8)
        send[n, q, :] = jnp.where(col < room, got[first, q, :], got[second, q, :])
    q = slice(24, WIN)
    send[n, q, :] = jnp.where(kcol[0:6] < room, got[first, q, :], got[second, q, :])


def columns(chunk, lane):
    col = STARTS[chunk] + lane
    if chunk == 0:
        return jnp.where(lane == 127, -1, col)
    if chunk == 2:
        return jnp.where(lane == 0, WIDE, col)
    return col


def pos(v):
    return jnp.maximum(v, 0.0)


def neg(v):
    return jnp.minimum(v, 0.0)


def fine_kernel(
    rows, left, height, width, got_tile, got_grp, nest,
    c, back,
    slot, nx, last_part, e, raw, am, ap, bm, bp, ac, kz, sums, sems,
):
    t = lax.axis_index("tile")
    g = lax.axis_index("grp")
    src = rows[g]
    prev_t = jnp.maximum(t - 1, 0)
    next_t = jnp.minimum(t + 1, TILES - 1)
    load = pltpu.make_async_copy(nest.at[0], nx, sems.at[0])
    load.start()
    lane = lanes((8, 128))
    sub = lax.broadcasted_iota(jnp.int32, (8, 128), 0)
    zero = jnp.zeros((8, 128), jnp.float32)
    for l in range(LEV):
        for m in range(3):
            raw[l, m, 56:64, :] = zero
            for p in range(2):
                c[p, l, m, 0:8, :] = zero
                c[p, l, m, 72:80, :] = zero

    above = OWN // RATIO * t - 1 + sub
    row_in = (above >= 0) & (above < height[g])
    coarse = {}
    for m in range(3):
        col = columns(m, lane)
        under = (jnp.maximum(col, 0) * 6554) >> 16
        pick = jnp.where(col < 0, 0, jnp.where(col < WIDE, under + 1, SPAN - 1))
        kpick = jnp.minimum(under, FR - 1)
        inside = row_in & (col >= 0) & (col < RATIO * width[g])
        block = got_grp[src, 24:32, :]
        ks = [jnp.take_along_axis(block, kpick + 32 * l, axis=1) for l in range(LEV)]
        faces = [0.05 * (ks[l] + ks[l + 1]) for l in range(LEV - 1)]
        for l in range(LEV - 1):
            e[10 * LEV + l, m] = jnp.where(inside, faces[l], 0.0)
        for l in range(LEV):
            block = got_grp[src, 6 * l : 6 * l + 8, :]
            e[l, m] = jnp.take_along_axis(block, pick, axis=1)
            u = jnp.take_along_axis(block, pick + SPAN, axis=1)
            v = jnp.take_along_axis(block, pick + 2 * SPAN, axis=1)
            u_lo = 0.5 * (pltpu.roll(u, 1, 0) + u)
            u_hi = 0.5 * (u + pltpu.roll(u, 7, 0))
            v_lo = 0.5 * (pltpu.roll(v, 1, 1) + v)
            v_hi = 0.5 * (v + pltpu.roll(v, 127, 1))
            rest = (1.0 - 4.0 * MIX) - pos(v_hi) + neg(v_lo)
            if l > 0:
                rest = rest - faces[l - 1]
            if l < LEV - 1:
                rest = rest - faces[l]
            values = (
                rest - pos(u) + neg(u),
                rest - pos(u) + neg(u_lo),
                rest - pos(u_hi) + neg(u),
                MIX + pos(u),
                MIX + pos(u_lo),
                MIX - neg(u),
                MIX - neg(u_hi),
                MIX + pos(v_lo),
                MIX - neg(v_hi),
            )
            for k, value in enumerate(values):
                e[LEV * (k + 1) + l, m] = jnp.where(inside, value, 1.0 if k < 3 else 0.0)

    def spread(p, m, i):
        lo, hi = (8 * i) // 10, min((8 * i + 7) // 10, 5)
        low = jnp.broadcast_to(e[p, m, lo : lo + 1, :], (8, 128))
        if lo == hi:
            return low
        high = jnp.broadcast_to(e[p, m, hi : hi + 1, :], (8, 128))
        return jnp.where(sub < 10 * hi - 8 * i, low, high)

    def at_row(value, p, m, i, last):
        for k in range(6):
            at = 10 * k + (9 if last else 0) - 8 * i
            if 0 <= at < 8:
                value = jnp.where(sub == at, jnp.broadcast_to(e[p, m, k : k + 1, :], (8, 128)), value)
        return value

    for i in range(8):
        q = slice(8 * i, 8 * i + 8)
        for m in range(3):
            for l in range(LEV - 1):
                kz[l, m, q, :] = spread(10 * LEV + l, m, i)
            for l in range(LEV):
                mid = at_row(spread(LEV + l, m, i), 2 * LEV + l, m, i, False)
                ac[l, m, q, :] = at_row(mid, 3 * LEV + l, m, i, True)
                am[l, m, q, :] = at_row(spread(4 * LEV + l, m, i), 5 * LEV + l, m, i, False)
                ap[l, m, q, :] = at_row(spread(6 * LEV + l, m, i), 7 * LEV + l, m, i, True)
                bm[l, m, q, :] = spread(8 * LEV + l, m, i)
                bp[l, m, q, :] = spread(9 * LEV + l, m, i)

    load.wait()

    def lay(l, at, n, parts, turn):
        wide = lanes((n, 128))
        q = slice(at, at + n)
        raw[l, 0, q, :] = parts[0]
        raw[l, 1, q, :] = jnp.where(wide < 32, pltpu.roll(parts[0], 32, 1), pltpu.roll(parts[1], 32, 1))
        third = pltpu.roll(parts[2], 64, 1) if turn else parts[2]
        raw[l, 2, q, :] = jnp.where(wide < 64, pltpu.roll(parts[1], 64, 1), third)

    for l in range(LEV):
        last_part[l, :, 64:128] = nx[l, :, 256:320]
        lay(l, 10, OWN, (nx[l, :, 0:128], nx[l, :, 128:256], last_part[l]), False)
        for tile, at in ((prev_t, 0), (next_t, OWN + 10)):
            spots = (EDGE + 20 * l, EDGE + 20 * l + 10, EDGE + 80 + 10 * (l // 2))
            lay(l, at, 10, [got_tile[tile, k : k + 10, :] for k in spots], l % 2 == 0)
    last_row = RATIO * height[g]
    first_row = OWN * t - 10
    for i in range(8):
        r = 8 + 8 * i
        row = first_row + 8 * i + sub
        row_in = (row >= 0) & (row < last_row)
        for m in range(3):
            col = columns(m, lane)
            active = row_in & (col >= 0) & (col < RATIO * width[g])
            for l in range(LEV):
                c[0, l, m, r : r + 8, :] = jnp.where(active, raw[l, m, r - 8 : r, :], spread(l, m, i))

    def advance(old, new, tiles):
        for m in range(3):
            for i in tiles:
                r = 8 + 8 * i
                q = slice(8 * i, 8 * i + 8)
                now = [c[old, l, m, r : r + 8, :] for l in range(LEV)]
                flow = [kz[l, m, q, :] for l in range(LEV - 1)]
                for l in range(LEV):
                    value = ac[l, m, q, :] * now[l]
                    value = value + am[l, m, q, :] * c[old, l, m, r - 1 : r + 7, :]
                    value = value + ap[l, m, q, :] * c[old, l, m, r + 1 : r + 9, :]
                    value = value + bm[l, m, q, :] * pltpu.roll(now[l], 1, 1)
                    value = value + bp[l, m, q, :] * pltpu.roll(now[l], 127, 1)
                    if l > 0:
                        value = value + flow[l - 1] * now[l - 1]
                    if l < LEV - 1:
                        value = value + flow[l] * now[l + 1]
                    c[new, l, m, r : r + 8, :] = value

    def steps(count, tiles):
        def body(_, carry):
            advance(0, 1, tiles)
            advance(1, 0, tiles)
            return carry

        lax.fori_loop(0, count, body, 0)

    steps(2, range(8))
    steps(2, range(7))
    steps(1, range(1, 7))
    mean = jnp.zeros((48, 128), jnp.float32)
    wide = lanes((16, 128))
    for m in range(3):
        for l in range(LEV):
            total = c[0, l, m, pl.ds(18, 4, stride=10), :]
            for k in range(1, RATIO):
                total = total + c[0, l, m, pl.ds(18 + k, 4, stride=10), :]
            sums[m, 4 * l : 4 * l + 4, :] = total
        taken = (wide >= TAKEN[m] - STARTS[m]) & (wide < TAKEN[m + 1] - STARTS[m])
        value = jnp.where(taken, sums[m], 0.0)
        high = value.astype(jnp.bfloat16)
        value = value - high.astype(jnp.float32)
        middle = value.astype(jnp.bfloat16)
        low = (value - middle.astype(jnp.float32)).astype(jnp.bfloat16)
        away = lax.broadcasted_iota(jnp.int32, (128, 128), 0) + STARTS[m] - RATIO * lanes((128, 128))
        pick = jnp.where((away >= 0) & (away < RATIO), 1.0, 0.0).astype(jnp.bfloat16)
        parts = jnp.concatenate([high, middle, low], axis=0)
        mean = mean + jnp.dot(parts, pick, preferred_element_type=jnp.float32)
    mean = mean[0:16] + (mean[16:32] + mean[32:48])
    mean = mean * (1.0 / (RATIO * RATIO))
    lane4 = lanes((4, 128))
    value = jnp.zeros((4, 128), jnp.float32)
    turned = [mean if l == 0 else pltpu.roll(mean, 32 * l, 1) for l in range(LEV)]
    for l in range(LEV):
        inside = (lane4 >= 32 * l) & (lane4 < 32 * l + 32)
        value = jnp.where(inside, turned[l][4 * l : 4 * l + 4, :], value)
    tile_a = lax.div(left[g], COLS)
    tile_b = jnp.where(tile_a < TILES - 1, tile_a + 1, tile_a - 1)
    slot[...] = value
    stores = [
        pltpu.make_async_copy(slot, back.at[TILES * src + tile], sems.at[1 + k])
        for k, tile in enumerate((tile_a, tile_b))
    ]
    for store in stores:
        store.start()
    for store in stores:
        store.wait()


def finish_kernel(
    rows, offs, got_tile, got_grp, c, so2, east, north, diff, stepped, fine_out, keep, px, vk, side, sems
):
    t = lax.axis_index("tile")
    g = lax.axis_index("grp")
    prev_t = jnp.maximum(t - 1, 0)
    next_t = jnp.minimum(t + 1, TILES - 1)
    prev_g = jnp.maximum(g - 1, 0)
    next_g = jnp.minimum(g + 1, GROUPS - 1)
    copies = [
        (so2, px.at[pl.ds(0, 4), pl.ds(8, ROWS), :]),
        (east, px.at[pl.ds(4, 4), pl.ds(8, ROWS), :]),
        (north, vk.at[pl.ds(0, 4)]),
        (diff, vk.at[pl.ds(4, 4)]),
    ]
    copies = [pltpu.make_async_copy(s, d, sems.at[i]) for i, (s, d) in enumerate(copies)]
    for copy in copies:
        copy.start()
    lane = lanes((8, 128))
    wide = lanes((OWN, 128))
    for l in range(LEV):
        middle = pltpu.roll(c[0, l, 1, 18:58, :], 96, 1)
        last = pltpu.roll(c[0, l, 2, 18:58, :], 64, 1)
        fine_out[0, l, :, 0:128] = jnp.where(wide < 117, c[0, l, 0, 18:58, :], middle)
        fine_out[0, l, :, 128:256] = jnp.where(wide < 75, middle, last)
        fine_out[0, l, :, 256:320] = last[:, 0:64]
    for copy in copies:
        copy.wait()
    for p in range(8):
        px[p, 7:8, :] = jnp.where(g > 0, got_grp[prev_g, WIN + p : WIN + p + 1, :], 0.0)
        px[p, 72:73, :] = jnp.where(g < GROUPS - 1, got_grp[next_g, WIN + p : WIN + p + 1, :], 0.0)
    here = lax.broadcasted_iota(jnp.int32, (8, 128), 0) == 0
    for k, (tile, there, at) in enumerate(((prev_t, t > 0, 0), (next_t, t < TILES - 1, 127))):
        put = jnp.where(here & (lane == at), 1.0, 0.0)
        for p in range(4):
            row = jnp.where(there, got_tile[tile, WIN + p : WIN + p + 1, :], 0.0)
            side[k, 128 * p : 128 * p + 128, :] = lax.dot_general(
                jnp.broadcast_to(row, (8, 128)),
                put,
                (((0,), (0,)), ((), ())),
                precision=lax.Precision.HIGHEST,
                preferred_element_type=jnp.float32,
            )
    for b in range(8):
        r = 8 + 8 * b
        q = slice(8 * b, 8 * b + 8)
        now = [px[l, r : r + 8, :] for l in range(LEV)]
        ks = [vk[4 + l, q, :] for l in range(LEV)]
        between = [0.5 * (ks[l] + ks[l + 1]) * (now[l + 1] - now[l]) for l in range(LEV - 1)]
        for l in range(LEV):
            here = now[l]
            at, vat = 64 * l + 8 * b, 256 + 64 * l + 8 * b
            wind = vk[l, q, :]
            c_w = jnp.where(lane == 0, side[0, at : at + 8, :], pltpu.roll(here, 1, 1))
            c_e = jnp.where(lane == 127, side[1, at : at + 8, :], pltpu.roll(here, 127, 1))
            v_w = jnp.where(lane == 0, side[0, vat : vat + 8, :], pltpu.roll(wind, 1, 1))
            v_e = jnp.where(lane == 127, side[1, vat : vat + 8, :], pltpu.roll(wind, 127, 1))
            c_n = px[l, r - 1 : r + 7, :]
            c_s = px[l, r + 1 : r + 9, :]
            flow = px[4 + l, r : r + 8, :]
            u_lo = 0.5 * (px[4 + l, r - 1 : r + 7, :] + flow)
            u_hi = 0.5 * (flow + px[4 + l, r + 1 : r + 9, :])
            v_lo = 0.5 * (v_w + wind)
            v_hi = 0.5 * (wind + v_e)
            value = (
                here
                - ((pos(u_hi) * here + neg(u_hi) * c_s) - (pos(u_lo) * c_n + neg(u_lo) * here))
                - ((pos(v_hi) * here + neg(v_hi) * c_e) - (pos(v_lo) * c_w + neg(v_lo) * here))
                + MIX * (c_n + c_s + c_w + c_e - 4.0 * here)
            )
            if l < LEV - 1:
                value = value + between[l]
            if l > 0:
                value = value - between[l - 1]
            stepped[l, q, :] = value
    off = offs[nest_over(rows, g)]
    base = pl.multiple_of(lax.div(off, 8) * 8, 8)
    for l in range(LEV):
        keep[l] = stepped[l, pl.ds(base, 40), :]


def place_kernel(rows, offs, left, height, width, stepped, keep, got, out, s, sems):
    t = lax.axis_index("tile")
    g = lax.axis_index("grp")
    n = nest_over(rows, g)
    lf = left[n]
    wd = width[n]

    @pl.when((lf < COLS * t + COLS) & (lf + wd > COLS * t))
    def _():
        off = offs[n]
        base = pl.multiple_of(lax.div(off, 8) * 8, 8)
        lane = lanes((FR, 128)) + COLS * t
        row = lax.broadcasted_iota(jnp.int32, (FR, 128), 0)
        covered = (lane >= lf) & (lane < lf + wd) & (row < height[n])
        at = pl.ds(off - base, FR)
        for l in range(LEV):
            turned = pltpu.roll(got[n], lax.rem(lf - COLS * t - 32 * l + 2048, 128), 1)
            s[l] = keep[l]
            s[l, at, :] = jnp.where(covered, turned, keep[l, at, :])
        store = pltpu.make_async_copy(s, out.at[:, pl.ds(base, 40), :], sems.at[0])
        store.start()
        store.wait()


def shards(so2, east, north, diff, nest, rows, offs, left, height, width):
    f32 = jnp.float32
    shape = jax.ShapeDtypeStruct
    dma = pltpu.SemaphoreType.DMA
    field = functools.partial(pltpu.VMEM, dtype=f32)
    near = functools.partial(pltpu.with_memory_space_constraint, memory_space=pltpu.VMEM)
    send, edges = pl.pallas_call(
        pack_kernel,
        out_shape=(field((TILES, SLOT, 128)), field((16, 128))),
        in_specs=[SMEM] * 3 + [ANY] * 5,
        out_specs=(VMEM, VMEM),
        scratch_shapes=[
            field((16, ROWS + 8, 128)),
            field((LEV, OWN, WIDE)),
            field((5, 40, 128)),
            dma((5,)),
        ],
        name="pack",
    )(rows, offs, left, so2, east, north, diff, nest)
    got_tile = near(lax.all_to_all(send, "tile", 0, 0))
    send = pl.pallas_call(
        merge_kernel,
        out_shape=field((GROUPS, GSLOT, 128)),
        in_specs=[SMEM] * 2 + [VMEM, VMEM],
        out_specs=VMEM,
        name="merge",
    )(rows, left, got_tile, near(edges))
    got_grp = near(lax.all_to_all(send, "grp", 0, 0))
    c, back = pl.pallas_call(
        fine_kernel,
        out_shape=(field((2, LEV, 3, 80, 128)), shape((GROUPS * TILES, 4, 128), f32)),
        in_specs=[SMEM] * 4 + [VMEM] * 2 + [ANY],
        out_specs=(VMEM, ANY),
        scratch_shapes=[
            field((4, 128)),
            field((LEV, OWN, WIDE)),
            field((LEV, OWN, 128)),
            field((11 * LEV - 1, 3, 8, 128)),
            field((LEV, 3, 64, 128)),
            field((LEV, 3, 64, 128)),
            field((LEV, 3, 64, 128)),
            field((LEV, 3, 64, 128)),
            field((LEV, 3, 64, 128)),
            field((LEV, 3, 64, 128)),
            field((LEV - 1, 3, 64, 128)),
            field((3, 16, 128)),
            dma((3,)),
        ],
        name="fine",
    )(rows, left, height, width, got_tile, got_grp, nest)
    stepped, nest_next, keep = pl.pallas_call(
        finish_kernel,
        out_shape=(
            shape((LEV, ROWS, COLS), f32),
            shape((1, LEV, OWN, WIDE), f32),
            field((LEV, 40, 128)),
        ),
        in_specs=[SMEM] * 2 + [VMEM] * 3 + [ANY] * 4,
        out_specs=(VMEM, VMEM, VMEM),
        scratch_shapes=[
            field((8, ROWS + 16, 128)),
            field((8, ROWS, 128)),
            field((2, 512, 128)),
            dma((4,)),
        ],
        name="finish",
    )(rows, offs, got_tile, got_grp, near(c), so2, east, north, diff)
    got = lax.all_to_all(back, ("grp", "tile"), 0, 0)
    got = near(got.reshape(GROUPS, FR, 128))
    parent_next = pl.pallas_call(
        place_kernel,
        out_shape=shape((LEV, ROWS, COLS), f32),
        in_specs=[SMEM] * 5 + [ANY, VMEM, VMEM],
        out_specs=ANY,
        scratch_shapes=[field((LEV, 40, 128)), dma((1,))],
        input_output_aliases={5: 0},
        name="place",
    )(rows, offs, left, height, width, stepped, near(keep), got)
    return parent_next, nest_next


def solution(mesh):
    in_specs = (
        P(None, "grp", "tile"),
        P(None, "grp", "tile"),
        P(None, "grp", "tile"),
        P(None, "grp", "tile"),
        P("grp", None, "tile", None),
        P(),
        P(),
        P(),
        P(),
        P(),
    )
    out_specs = (P(None, "grp", "tile"), P("grp", None, "tile", None))
    return jax.shard_map(shards, mesh=mesh, in_specs=in_specs, out_specs=out_specs, check_vma=False)
```

```python
import functools
import jax
import jax.numpy as jnp
from jax import lax
from jax.experimental import pallas as pl
from jax.experimental.pallas import tpu as pltpu
from jax.sharding import PartitionSpec as P

RATIO = 10
FR = 32
LEV = 4
ROWS = 64
COLS = 128
OWN = 40
WIDE = 320
GROUPS = 16
TILES = 8
SPAN = FR + 2
WIN = 30
EDGE = 34
SLOT = 136
GSLOT = 40
STARTS = (0, 96, 192)
TAKEN = (0, 117, 203, 320)
MIX = 0.02

SMEM = pl.BlockSpec(memory_space=pltpu.SMEM)
ANY = pl.BlockSpec(memory_space=pl.ANY)
VMEM = pl.BlockSpec(memory_space=pltpu.VMEM)


def nest_over(rows, group):
    found = jnp.int32(0)
    for i in range(GROUPS):
        found = jnp.where(rows[i] == group, jnp.int32(i), found)
    return found


def lanes(shape):
    return lax.broadcasted_iota(jnp.int32, shape, 1)


def pack_kernel(
    rows, offs, left, height, width, so2, east, north, diff, nest, send, edges, facts, x, nx, cut, sems
):
    t = lax.axis_index("tile")
    g = lax.axis_index("grp")
    loads = [
        pltpu.make_async_copy(f, x.at[pl.ds(4 * i, 4), pl.ds(0, ROWS), :], sems.at[i])
        for i, f in enumerate((so2, east, north, diff))
    ]
    loads.append(pltpu.make_async_copy(nest.at[0], nx, sems.at[4]))
    for c in loads:
        c.start()
    n = nest_over(rows, g)
    facts[0] = n
    facts[1] = left[n]
    facts[2] = offs[n]
    facts[3] = height[n]
    facts[4] = width[n]
    facts[5] = rows[g]
    facts[6] = left[g]
    facts[7] = height[g]
    facts[8] = width[g]
    top = offs[n] - 1
    base = 128 * t + 1 - left[n] + 1024
    x[:, ROWS : ROWS + 8, :] = jnp.zeros((16, 8, 128), jnp.float32)
    lane = lanes((8, 128))
    before = jnp.where(t > 0, t - 1, t + 2)
    after = jnp.where(t < TILES - 1, t + 1, t - 2)
    loads[4].wait()
    for at, source in ((before, 0), (after, OWN - 10)):
        q = slice(source, source + 10)
        for l in range(LEV):
            for m in range(2):
                send[at, pl.ds(EDGE + 10 * (2 * l + m), 10), :] = nx[l, q, 128 * m : 128 * m + 128]
            side = 64 * (l % 2)
            send[at, pl.ds(EDGE + 80 + 10 * (l // 2), 10), side : side + 64] = nx[l, q, 256:320]
    for c in loads[:4]:
        c.wait()
    for l in range(LEV):
        edges[l : l + 1, :] = x[l, 0:1, :]
        edges[4 + l : 5 + l, :] = x[4 + l, 0:1, :]
        edges[8 + l : 9 + l, :] = x[l, ROWS - 1 : ROWS, :]
        edges[12 + l : 13 + l, :] = x[4 + l, ROWS - 1 : ROWS, :]
    shifts = [lax.rem(base + SPAN * f, 128) for f in range(3)]
    kshifts = [lax.rem(base + 32 * l - 1, 128) for l in range(LEV)]
    for b in range(5):
        at = pl.ds(top + 8 * b, 8)
        q = slice(8 * b, 8 * b + 8)
        for l in range(LEV):
            part = [pltpu.roll(x[4 * f + l, at, :], shifts[f], 1) for f in range(3)]
            cut[l, q, :] = jnp.where(lane < SPAN, part[0], jnp.where(lane < 2 * SPAN, part[1], part[2]))
        part = [pltpu.roll(x[12 + l, at, :], kshifts[l], 1) for l in range(LEV)]
        cut[4, q, :] = jnp.where(
            lane < 64,
            jnp.where(lane < 32, part[0], part[1]),
            jnp.where(lane < 96, part[2], part[3]),
        )
    sub = lax.broadcasted_iota(jnp.int32, (8, 128), 0)
    ends = jnp.where(((sub == 0) & (lane == 0)) | ((sub == 1) & (lane == 127)), 1.0, 0.0)
    planes = [x[p if p < 4 else p + 4, 0:ROWS, :] for p in range(8)]
    sides = lax.dot_general(
        ends,
        jnp.concatenate(planes, axis=0),
        (((1,), (1,)), ((), ())),
        precision=lax.Precision.HIGHEST,
        preferred_element_type=jnp.float32,
    )
    for d in range(TILES):
        for l in range(5):
            send[d, 6 * l : 6 * l + 6, :] = cut[l, 4 * d : 4 * d + 6, :]
        for k in range(4):
            pair = sides[0:2, 128 * k : 128 * k + 128]
            send[d, WIN + k : WIN + k + 1, :] = jnp.where(d < t, pair[0:1], pair[1:2])


def merge_kernel(facts, got, edges, send):
    g = lax.axis_index("grp")
    n = facts[0]
    start = facts[1] - 1
    first = lax.div(start, COLS)
    second = jnp.minimum(first + 1, TILES - 1)
    send[jnp.where(g > 0, g - 1, g + 2), WIN : WIN + 8, :] = edges[0:8, :]
    send[jnp.where(g < GROUPS - 1, g + 1, g - 2), WIN : WIN + 8, :] = edges[8:16, :]
    room = COLS - (start - COLS * first)
    lane = lanes((8, 128))
    col = lane - jnp.where(lane >= SPAN, SPAN, 0) - jnp.where(lane >= 2 * SPAN, SPAN, 0)
    kcol = (lane & 31) + 1
    for l in range(3):
        q = slice(8 * l, 8 * l + 8)
        send[n, q, :] = jnp.where(col < room, got[first, q, :], got[second, q, :])
    q = slice(24, WIN)
    send[n, q, :] = jnp.where(kcol[0:6] < room, got[first, q, :], got[second, q, :])


def columns(chunk, lane):
    col = STARTS[chunk] + lane
    if chunk == 0:
        return jnp.where(lane == 127, -1, col)
    if chunk == 2:
        return jnp.where(lane == 0, WIDE, col)
    return col


def pos(v):
    return jnp.maximum(v, 0.0)


def neg(v):
    return jnp.minimum(v, 0.0)


def fine_kernel(
    facts, got_tile, got_grp, nest,
    c, back,
    slot, nx, last_part, e, raw, am, ap, bm, bp, ac, kz, sums, sems,
):
    t = lax.axis_index("tile")
    g = lax.axis_index("grp")
    src = facts[5]
    prev_t = jnp.maximum(t - 1, 0)
    next_t = jnp.minimum(t + 1, TILES - 1)
    load = pltpu.make_async_copy(nest.at[0], nx, sems.at[0])
    load.start()
    lane = lanes((8, 128))
    sub = lax.broadcasted_iota(jnp.int32, (8, 128), 0)
    zero = jnp.zeros((8, 128), jnp.float32)
    for l in range(LEV):
        for m in range(3):
            raw[l, m, 56:64, :] = zero
            for p in range(2):
                c[p, l, m, 0:8, :] = zero
                c[p, l, m, 72:80, :] = zero

    above = OWN // RATIO * t - 1 + sub
    row_in = (above >= 0) & (above < facts[7])
    coarse = {}
    for m in range(3):
        col = columns(m, lane)
        under = (jnp.maximum(col, 0) * 6554) >> 16
        pick = jnp.where(col < 0, 0, jnp.where(col < WIDE, under + 1, SPAN - 1))
        kpick = jnp.minimum(under, FR - 1)
        inside = row_in & (col >= 0) & (col < RATIO * facts[8])
        block = got_grp[src, 24:32, :]
        ks = [jnp.take_along_axis(block, kpick + 32 * l, axis=1) for l in range(LEV)]
        faces = [0.05 * (ks[l] + ks[l + 1]) for l in range(LEV - 1)]
        for l in range(LEV - 1):
            e[10 * LEV + l, m] = jnp.where(inside, faces[l], 0.0)
        for l in range(LEV):
            block = got_grp[src, 6 * l : 6 * l + 8, :]
            e[l, m] = jnp.take_along_axis(block, pick, axis=1)
            u = jnp.take_along_axis(block, pick + SPAN, axis=1)
            v = jnp.take_along_axis(block, pick + 2 * SPAN, axis=1)
            u_lo = 0.5 * (pltpu.roll(u, 1, 0) + u)
            u_hi = 0.5 * (u + pltpu.roll(u, 7, 0))
            v_lo = 0.5 * (pltpu.roll(v, 1, 1) + v)
            v_hi = 0.5 * (v + pltpu.roll(v, 127, 1))
            rest = (1.0 - 4.0 * MIX) - pos(v_hi) + neg(v_lo)
            if l > 0:
                rest = rest - faces[l - 1]
            if l < LEV - 1:
                rest = rest - faces[l]
            values = (
                rest - pos(u) + neg(u),
                rest - pos(u) + neg(u_lo),
                rest - pos(u_hi) + neg(u),
                MIX + pos(u),
                MIX + pos(u_lo),
                MIX - neg(u),
                MIX - neg(u_hi),
                MIX + pos(v_lo),
                MIX - neg(v_hi),
            )
            for k, value in enumerate(values):
                e[LEV * (k + 1) + l, m] = jnp.where(inside, value, 1.0 if k < 3 else 0.0)

    def spread(p, m, i):
        lo, hi = (8 * i) // 10, min((8 * i + 7) // 10, 5)
        low = jnp.broadcast_to(e[p, m, lo : lo + 1, :], (8, 128))
        if lo == hi:
            return low
        high = jnp.broadcast_to(e[p, m, hi : hi + 1, :], (8, 128))
        return jnp.where(sub < 10 * hi - 8 * i, low, high)

    def at_row(value, p, m, i, last):
        for k in range(6):
            at = 10 * k + (9 if last else 0) - 8 * i
            if 0 <= at < 8:
                value = jnp.where(sub == at, jnp.broadcast_to(e[p, m, k : k + 1, :], (8, 128)), value)
        return value

    for i in range(8):
        q = slice(8 * i, 8 * i + 8)
        for m in range(3):
            for l in range(LEV - 1):
                kz[l, m, q, :] = spread(10 * LEV + l, m, i)
            for l in range(LEV):
                mid = at_row(spread(LEV + l, m, i), 2 * LEV + l, m, i, False)
                ac[l, m, q, :] = at_row(mid, 3 * LEV + l, m, i, True)
                am[l, m, q, :] = at_row(spread(4 * LEV + l, m, i), 5 * LEV + l, m, i, False)
                ap[l, m, q, :] = at_row(spread(6 * LEV + l, m, i), 7 * LEV + l, m, i, True)
                bm[l, m, q, :] = spread(8 * LEV + l, m, i)
                bp[l, m, q, :] = spread(9 * LEV + l, m, i)

    load.wait()

    def lay(l, at, n, parts, turn):
        wide = lanes((n, 128))
        q = slice(at, at + n)
        raw[l, 0, q, :] = parts[0]
        raw[l, 1, q, :] = jnp.where(wide < 32, pltpu.roll(parts[0], 32, 1), pltpu.roll(parts[1], 32, 1))
        third = pltpu.roll(parts[2], 64, 1) if turn else parts[2]
        raw[l, 2, q, :] = jnp.where(wide < 64, pltpu.roll(parts[1], 64, 1), third)

    for l in range(LEV):
        last_part[l, :, 64:128] = nx[l, :, 256:320]
        lay(l, 10, OWN, (nx[l, :, 0:128], nx[l, :, 128:256], last_part[l]), False)
        for tile, at in ((prev_t, 0), (next_t, OWN + 10)):
            spots = (EDGE + 20 * l, EDGE + 20 * l + 10, EDGE + 80 + 10 * (l // 2))
            lay(l, at, 10, [got_tile[tile, k : k + 10, :] for k in spots], l % 2 == 0)
    last_row = RATIO * facts[7]
    first_row = OWN * t - 10
    for i in range(8):
        r = 8 + 8 * i
        row = first_row + 8 * i + sub
        row_in = (row >= 0) & (row < last_row)
        for m in range(3):
            col = columns(m, lane)
            active = row_in & (col >= 0) & (col < RATIO * facts[8])
            for l in range(LEV):
                c[0, l, m, r : r + 8, :] = jnp.where(active, raw[l, m, r - 8 : r, :], spread(l, m, i))

    def advance(old, new, tiles):
        for m in range(3):
            for i in tiles:
                r = 8 + 8 * i
                q = slice(8 * i, 8 * i + 8)
                now = [c[old, l, m, r : r + 8, :] for l in range(LEV)]
                flow = [kz[l, m, q, :] for l in range(LEV - 1)]
                for l in range(LEV):
                    value = ac[l, m, q, :] * now[l]
                    value = value + am[l, m, q, :] * c[old, l, m, r - 1 : r + 7, :]
                    value = value + ap[l, m, q, :] * c[old, l, m, r + 1 : r + 9, :]
                    value = value + bm[l, m, q, :] * pltpu.roll(now[l], 1, 1)
                    value = value + bp[l, m, q, :] * pltpu.roll(now[l], 127, 1)
                    if l > 0:
                        value = value + flow[l - 1] * now[l - 1]
                    if l < LEV - 1:
                        value = value + flow[l] * now[l + 1]
                    c[new, l, m, r : r + 8, :] = value

    def steps(count, tiles):
        def body(_, carry):
            advance(0, 1, tiles)
            advance(1, 0, tiles)
            return carry

        lax.fori_loop(0, count, body, 0)

    steps(2, range(8))
    steps(2, range(7))
    steps(1, range(1, 7))
    mean = jnp.zeros((48, 128), jnp.float32)
    wide = lanes((16, 128))
    for m in range(3):
        for l in range(LEV):
            total = c[0, l, m, pl.ds(18, 4, stride=10), :]
            for k in range(1, RATIO):
                total = total + c[0, l, m, pl.ds(18 + k, 4, stride=10), :]
            sums[m, 4 * l : 4 * l + 4, :] = total
        taken = (wide >= TAKEN[m] - STARTS[m]) & (wide < TAKEN[m + 1] - STARTS[m])
        value = jnp.where(taken, sums[m], 0.0)
        high = value.astype(jnp.bfloat16)
        value = value - high.astype(jnp.float32)
        middle = value.astype(jnp.bfloat16)
        low = (value - middle.astype(jnp.float32)).astype(jnp.bfloat16)
        away = lax.broadcasted_iota(jnp.int32, (128, 128), 0) + STARTS[m] - RATIO * lanes((128, 128))
        pick = jnp.where((away >= 0) & (away < RATIO), 1.0, 0.0).astype(jnp.bfloat16)
        parts = jnp.concatenate([high, middle, low], axis=0)
        mean = mean + jnp.dot(parts, pick, preferred_element_type=jnp.float32)
    mean = mean[0:16] + (mean[16:32] + mean[32:48])
    mean = mean * (1.0 / (RATIO * RATIO))
    lane4 = lanes((4, 128))
    value = jnp.zeros((4, 128), jnp.float32)
    turned = [mean if l == 0 else pltpu.roll(mean, 32 * l, 1) for l in range(LEV)]
    for l in range(LEV):
        inside = (lane4 >= 32 * l) & (lane4 < 32 * l + 32)
        value = jnp.where(inside, turned[l][4 * l : 4 * l + 4, :], value)
    tile_a = lax.div(facts[6], COLS)
    tile_b = jnp.where(tile_a < TILES - 1, tile_a + 1, tile_a - 1)
    slot[...] = value
    stores = [
        pltpu.make_async_copy(slot, back.at[TILES * src + tile], sems.at[1 + k])
        for k, tile in enumerate((tile_a, tile_b))
    ]
    for store in stores:
        store.start()
    for store in stores:
        store.wait()


def finish_kernel(
    facts, got_tile, got_grp, c, so2, east, north, diff, stepped, fine_out, keep, px, vk, side, sems
):
    t = lax.axis_index("tile")
    g = lax.axis_index("grp")
    prev_t = jnp.maximum(t - 1, 0)
    next_t = jnp.minimum(t + 1, TILES - 1)
    prev_g = jnp.maximum(g - 1, 0)
    next_g = jnp.minimum(g + 1, GROUPS - 1)
    copies = [
        (so2, px.at[pl.ds(0, 4), pl.ds(8, ROWS), :]),
        (east, px.at[pl.ds(4, 4), pl.ds(8, ROWS), :]),
        (north, vk.at[pl.ds(0, 4)]),
        (diff, vk.at[pl.ds(4, 4)]),
    ]
    copies = [pltpu.make_async_copy(s, d, sems.at[i]) for i, (s, d) in enumerate(copies)]
    for copy in copies:
        copy.start()
    lane = lanes((8, 128))
    wide = lanes((OWN, 128))
    for l in range(LEV):
        middle = pltpu.roll(c[0, l, 1, 18:58, :], 96, 1)
        last = pltpu.roll(c[0, l, 2, 18:58, :], 64, 1)
        fine_out[0, l, :, 0:128] = jnp.where(wide < 117, c[0, l, 0, 18:58, :], middle)
        fine_out[0, l, :, 128:256] = jnp.where(wide < 75, middle, last)
        fine_out[0, l, :, 256:320] = last[:, 0:64]
    for copy in copies:
        copy.wait()
    for p in range(8):
        px[p, 7:8, :] = jnp.where(g > 0, got_grp[prev_g, WIN + p : WIN + p + 1, :], 0.0)
        px[p, 72:73, :] = jnp.where(g < GROUPS - 1, got_grp[next_g, WIN + p : WIN + p + 1, :], 0.0)
    here = lax.broadcasted_iota(jnp.int32, (8, 128), 0) == 0
    for k, (tile, there, at) in enumerate(((prev_t, t > 0, 0), (next_t, t < TILES - 1, 127))):
        put = jnp.where(here & (lane == at), 1.0, 0.0)
        for p in range(4):
            row = jnp.where(there, got_tile[tile, WIN + p : WIN + p + 1, :], 0.0)
            side[k, 128 * p : 128 * p + 128, :] = lax.dot_general(
                jnp.broadcast_to(row, (8, 128)),
                put,
                (((0,), (0,)), ((), ())),
                precision=lax.Precision.HIGHEST,
                preferred_element_type=jnp.float32,
            )
    for b in range(8):
        r = 8 + 8 * b
        q = slice(8 * b, 8 * b + 8)
        now = [px[l, r : r + 8, :] for l in range(LEV)]
        ks = [vk[4 + l, q, :] for l in range(LEV)]
        between = [0.5 * (ks[l] + ks[l + 1]) * (now[l + 1] - now[l]) for l in range(LEV - 1)]
        for l in range(LEV):
            here = now[l]
            at, vat = 64 * l + 8 * b, 256 + 64 * l + 8 * b
            wind = vk[l, q, :]
            c_w = jnp.where(lane == 0, side[0, at : at + 8, :], pltpu.roll(here, 1, 1))
            c_e = jnp.where(lane == 127, side[1, at : at + 8, :], pltpu.roll(here, 127, 1))
            v_w = jnp.where(lane == 0, side[0, vat : vat + 8, :], pltpu.roll(wind, 1, 1))
            v_e = jnp.where(lane == 127, side[1, vat : vat + 8, :], pltpu.roll(wind, 127, 1))
            c_n = px[l, r - 1 : r + 7, :]
            c_s = px[l, r + 1 : r + 9, :]
            flow = px[4 + l, r : r + 8, :]
            u_lo = 0.5 * (px[4 + l, r - 1 : r + 7, :] + flow)
            u_hi = 0.5 * (flow + px[4 + l, r + 1 : r + 9, :])
            v_lo = 0.5 * (v_w + wind)
            v_hi = 0.5 * (wind + v_e)
            value = (
                here
                - ((pos(u_hi) * here + neg(u_hi) * c_s) - (pos(u_lo) * c_n + neg(u_lo) * here))
                - ((pos(v_hi) * here + neg(v_hi) * c_e) - (pos(v_lo) * c_w + neg(v_lo) * here))
                + MIX * (c_n + c_s + c_w + c_e - 4.0 * here)
            )
            if l < LEV - 1:
                value = value + between[l]
            if l > 0:
                value = value - between[l - 1]
            stepped[l, q, :] = value
    off = facts[2]
    base = pl.multiple_of(lax.div(off, 8) * 8, 8)
    for l in range(LEV):
        keep[l] = stepped[l, pl.ds(base, 40), :]


def place_kernel(facts, stepped, keep, got, out, s, sems):
    t = lax.axis_index("tile")
    n, lf, wd = facts[0], facts[1], facts[4]

    @pl.when((lf < COLS * t + COLS) & (lf + wd > COLS * t))
    def _():
        off = facts[2]
        base = pl.multiple_of(lax.div(off, 8) * 8, 8)
        lane = lanes((FR, 128)) + COLS * t
        row = lax.broadcasted_iota(jnp.int32, (FR, 128), 0)
        covered = (lane >= lf) & (lane < lf + wd) & (row < facts[3])
        at = pl.ds(off - base, FR)
        for l in range(LEV):
            turned = pltpu.roll(got[n], lax.rem(lf - COLS * t - 32 * l + 2048, 128), 1)
            s[l] = keep[l]
            s[l, at, :] = jnp.where(covered, turned, keep[l, at, :])
        store = pltpu.make_async_copy(s, out.at[:, pl.ds(base, 40), :], sems.at[0])
        store.start()
        store.wait()


def shards(so2, east, north, diff, nest, rows, offs, left, height, width):
    f32 = jnp.float32
    shape = jax.ShapeDtypeStruct
    dma = pltpu.SemaphoreType.DMA
    field = functools.partial(pltpu.VMEM, dtype=f32)
    near = functools.partial(pltpu.with_memory_space_constraint, memory_space=pltpu.VMEM)
    scalar = functools.partial(pltpu.with_memory_space_constraint, memory_space=pltpu.SMEM)
    send, edges, facts = pl.pallas_call(
        pack_kernel,
        out_shape=(
            field((TILES, SLOT, 128)),
            field((16, 128)),
            pltpu.SMEM((16,), jnp.int32),
        ),
        in_specs=[SMEM] * 5 + [ANY] * 5,
        out_specs=(VMEM, VMEM, SMEM),
        scratch_shapes=[
            field((16, ROWS + 8, 128)),
            field((LEV, OWN, WIDE)),
            field((5, 40, 128)),
            dma((5,)),
        ],
        name="pack",
    )(rows, offs, left, height, width, so2, east, north, diff, nest)
    facts = scalar(facts)
    got_tile = near(lax.all_to_all(send, "tile", 0, 0))
    send = pl.pallas_call(
        merge_kernel,
        out_shape=field((GROUPS, GSLOT, 128)),
        in_specs=[SMEM, VMEM, VMEM],
        out_specs=VMEM,
        name="merge",
    )(facts, got_tile, near(edges))
    got_grp = near(lax.all_to_all(send, "grp", 0, 0))
    c, back = pl.pallas_call(
        fine_kernel,
        out_shape=(field((2, LEV, 3, 80, 128)), shape((GROUPS * TILES, 4, 128), f32)),
        in_specs=[SMEM] + [VMEM] * 2 + [ANY],
        out_specs=(VMEM, ANY),
        scratch_shapes=[
            field((4, 128)),
            field((LEV, OWN, WIDE)),
            field((LEV, OWN, 128)),
            field((11 * LEV - 1, 3, 8, 128)),
            field((LEV, 3, 64, 128)),
            field((LEV, 3, 64, 128)),
            field((LEV, 3, 64, 128)),
            field((LEV, 3, 64, 128)),
            field((LEV, 3, 64, 128)),
            field((LEV, 3, 64, 128)),
            field((LEV - 1, 3, 64, 128)),
            field((3, 16, 128)),
            dma((3,)),
        ],
        name="fine",
    )(facts, got_tile, got_grp, nest)
    stepped, nest_next, keep = pl.pallas_call(
        finish_kernel,
        out_shape=(
            shape((LEV, ROWS, COLS), f32),
            shape((1, LEV, OWN, WIDE), f32),
            field((LEV, 40, 128)),
        ),
        in_specs=[SMEM] + [VMEM] * 3 + [ANY] * 4,
        out_specs=(VMEM, VMEM, VMEM),
        scratch_shapes=[
            field((8, ROWS + 16, 128)),
            field((8, ROWS, 128)),
            field((2, 512, 128)),
            dma((4,)),
        ],
        name="finish",
    )(facts, got_tile, got_grp, near(c), so2, east, north, diff)
    got = lax.all_to_all(back, ("grp", "tile"), 0, 0)
    got = near(got.reshape(GROUPS, FR, 128))
    parent_next = pl.pallas_call(
        place_kernel,
        out_shape=shape((LEV, ROWS, COLS), f32),
        in_specs=[SMEM, ANY, VMEM, VMEM],
        out_specs=ANY,
        scratch_shapes=[field((LEV, 40, 128)), dma((1,))],
        input_output_aliases={1: 0},
        name="place",
    )(facts, stepped, near(keep), got)
    return parent_next, nest_next


def solution(mesh):
    in_specs = (
        P(None, "grp", "tile"),
        P(None, "grp", "tile"),
        P(None, "grp", "tile"),
        P(None, "grp", "tile"),
        P("grp", None, "tile", None),
        P(),
        P(),
        P(),
        P(),
        P(),
    )
    out_specs = (P(None, "grp", "tile"), P("grp", None, "tile", None))
    return jax.shard_map(shards, mesh=mesh, in_specs=in_specs, out_specs=out_specs, check_vma=False)
```

```python
import functools
import jax
import jax.numpy as jnp
from jax import lax
from jax.experimental import pallas as pl
from jax.experimental.pallas import tpu as pltpu
from jax.sharding import PartitionSpec as P

RATIO = 10
FR = 32
LEV = 4
ROWS = 64
COLS = 128
OWN = 40
WIDE = 320
GROUPS = 16
TILES = 8
SPAN = FR + 2
WIN = 30
EDGE = 34
SLOT = 136
GSLOT = 40
STARTS = (0, 96, 192)
TAKEN = (0, 117, 203, 320)
MIX = 0.02

SMEM = pl.BlockSpec(memory_space=pltpu.SMEM)
ANY = pl.BlockSpec(memory_space=pl.ANY)
VMEM = pl.BlockSpec(memory_space=pltpu.VMEM)


def nest_over(rows, group):
    found = jnp.int32(0)
    for i in range(GROUPS):
        found = jnp.where(rows[i] == group, jnp.int32(i), found)
    return found


def lanes(shape):
    return lax.broadcasted_iota(jnp.int32, shape, 1)


def pack_kernel(
    rows_at, offs_at, left_at, height_at, width_at, so2, east, north, diff, nest,
    send, edges, facts, nx,
    rows, offs, left, height, width, x, cut, sems,
):
    t = lax.axis_index("tile")
    g = lax.axis_index("grp")
    numbers = [
        pltpu.make_async_copy(s, d, sems.at[5 + i])
        for i, (s, d) in enumerate(
            ((rows_at, rows), (offs_at, offs), (left_at, left), (height_at, height), (width_at, width))
        )
    ]
    for c in numbers:
        c.start()
    loads = [
        pltpu.make_async_copy(f, x.at[pl.ds(4 * i, 4), pl.ds(0, ROWS), :], sems.at[i])
        for i, f in enumerate((so2, east, north, diff))
    ]
    loads.append(pltpu.make_async_copy(nest.at[0], nx, sems.at[4]))
    for c in loads:
        c.start()
    for c in numbers:
        c.wait()
    n = nest_over(rows, g)
    facts[0] = n
    facts[1] = left[n]
    facts[2] = offs[n]
    facts[3] = height[n]
    facts[4] = width[n]
    facts[5] = rows[g]
    facts[6] = left[g]
    facts[7] = height[g]
    facts[8] = width[g]
    top = offs[n] - 1
    base = 128 * t + 1 - left[n] + 1024
    x[:, ROWS : ROWS + 8, :] = jnp.zeros((16, 8, 128), jnp.float32)
    lane = lanes((8, 128))
    before = jnp.where(t > 0, t - 1, t + 2)
    after = jnp.where(t < TILES - 1, t + 1, t - 2)
    loads[4].wait()
    for at, source in ((before, 0), (after, OWN - 10)):
        q = slice(source, source + 10)
        for l in range(LEV):
            for m in range(2):
                send[at, pl.ds(EDGE + 10 * (2 * l + m), 10), :] = nx[l, q, 128 * m : 128 * m + 128]
            side = 64 * (l % 2)
            send[at, pl.ds(EDGE + 80 + 10 * (l // 2), 10), side : side + 64] = nx[l, q, 256:320]
    for c in loads[:4]:
        c.wait()
    for l in range(LEV):
        edges[l : l + 1, :] = x[l, 0:1, :]
        edges[4 + l : 5 + l, :] = x[4 + l, 0:1, :]
        edges[8 + l : 9 + l, :] = x[l, ROWS - 1 : ROWS, :]
        edges[12 + l : 13 + l, :] = x[4 + l, ROWS - 1 : ROWS, :]
    shifts = [lax.rem(base + SPAN * f, 128) for f in range(3)]
    kshifts = [lax.rem(base + 32 * l - 1, 128) for l in range(LEV)]
    for b in range(5):
        at = pl.ds(top + 8 * b, 8)
        q = slice(8 * b, 8 * b + 8)
        for l in range(LEV):
            part = [pltpu.roll(x[4 * f + l, at, :], shifts[f], 1) for f in range(3)]
            cut[l, q, :] = jnp.where(lane < SPAN, part[0], jnp.where(lane < 2 * SPAN, part[1], part[2]))
        part = [pltpu.roll(x[12 + l, at, :], kshifts[l], 1) for l in range(LEV)]
        cut[4, q, :] = jnp.where(
            lane < 64,
            jnp.where(lane < 32, part[0], part[1]),
            jnp.where(lane < 96, part[2], part[3]),
        )
    sub = lax.broadcasted_iota(jnp.int32, (8, 128), 0)
    ends = jnp.where(((sub == 0) & (lane == 0)) | ((sub == 1) & (lane == 127)), 1.0, 0.0)
    planes = [x[p if p < 4 else p + 4, 0:ROWS, :] for p in range(8)]
    sides = lax.dot_general(
        ends,
        jnp.concatenate(planes, axis=0),
        (((1,), (1,)), ((), ())),
        precision=lax.Precision.HIGHEST,
        preferred_element_type=jnp.float32,
    )
    for d in range(TILES):
        for l in range(5):
            send[d, 6 * l : 6 * l + 6, :] = cut[l, 4 * d : 4 * d + 6, :]
        for k in range(4):
            pair = sides[0:2, 128 * k : 128 * k + 128]
            send[d, WIN + k : WIN + k + 1, :] = jnp.where(d < t, pair[0:1], pair[1:2])


def merge_kernel(facts, got, edges, send):
    g = lax.axis_index("grp")
    n = facts[0]
    start = facts[1] - 1
    first = lax.div(start, COLS)
    second = jnp.minimum(first + 1, TILES - 1)
    send[jnp.where(g > 0, g - 1, g + 2), WIN : WIN + 8, :] = edges[0:8, :]
    send[jnp.where(g < GROUPS - 1, g + 1, g - 2), WIN : WIN + 8, :] = edges[8:16, :]
    room = COLS - (start - COLS * first)
    lane = lanes((8, 128))
    col = lane - jnp.where(lane >= SPAN, SPAN, 0) - jnp.where(lane >= 2 * SPAN, SPAN, 0)
    kcol = (lane & 31) + 1
    for l in range(3):
        q = slice(8 * l, 8 * l + 8)
        send[n, q, :] = jnp.where(col < room, got[first, q, :], got[second, q, :])
    q = slice(24, WIN)
    send[n, q, :] = jnp.where(kcol[0:6] < room, got[first, q, :], got[second, q, :])


def columns(chunk, lane):
    col = STARTS[chunk] + lane
    if chunk == 0:
        return jnp.where(lane == 127, -1, col)
    if chunk == 2:
        return jnp.where(lane == 0, WIDE, col)
    return col


def pos(v):
    return jnp.maximum(v, 0.0)


def neg(v):
    return jnp.minimum(v, 0.0)


def fine_kernel(
    facts, got_tile, got_grp, nx,
    c, back,
    slot, last_part, e, raw, am, ap, bm, bp, ac, kz, sums, sems,
):
    t = lax.axis_index("tile")
    g = lax.axis_index("grp")
    src = facts[5]
    prev_t = jnp.maximum(t - 1, 0)
    next_t = jnp.minimum(t + 1, TILES - 1)
    lane = lanes((8, 128))
    sub = lax.broadcasted_iota(jnp.int32, (8, 128), 0)
    zero = jnp.zeros((8, 128), jnp.float32)
    for l in range(LEV):
        for m in range(3):
            raw[l, m, 56:64, :] = zero
            for p in range(2):
                c[p, l, m, 0:8, :] = zero
                c[p, l, m, 72:80, :] = zero

    above = OWN // RATIO * t - 1 + sub
    row_in = (above >= 0) & (above < facts[7])
    coarse = {}
    for m in range(3):
        col = columns(m, lane)
        under = (jnp.maximum(col, 0) * 6554) >> 16
        pick = jnp.where(col < 0, 0, jnp.where(col < WIDE, under + 1, SPAN - 1))
        kpick = jnp.minimum(under, FR - 1)
        inside = row_in & (col >= 0) & (col < RATIO * facts[8])
        block = got_grp[src, 24:32, :]
        ks = [jnp.take_along_axis(block, kpick + 32 * l, axis=1) for l in range(LEV)]
        faces = [0.05 * (ks[l] + ks[l + 1]) for l in range(LEV - 1)]
        for l in range(LEV - 1):
            e[10 * LEV + l, m] = jnp.where(inside, faces[l], 0.0)
        for l in range(LEV):
            block = got_grp[src, 6 * l : 6 * l + 8, :]
            e[l, m] = jnp.take_along_axis(block, pick, axis=1)
            u = jnp.take_along_axis(block, pick + SPAN, axis=1)
            v = jnp.take_along_axis(block, pick + 2 * SPAN, axis=1)
            u_lo = 0.5 * (pltpu.roll(u, 1, 0) + u)
            u_hi = 0.5 * (u + pltpu.roll(u, 7, 0))
            v_lo = 0.5 * (pltpu.roll(v, 1, 1) + v)
            v_hi = 0.5 * (v + pltpu.roll(v, 127, 1))
            rest = (1.0 - 4.0 * MIX) - pos(v_hi) + neg(v_lo)
            if l > 0:
                rest = rest - faces[l - 1]
            if l < LEV - 1:
                rest = rest - faces[l]
            values = (
                rest - pos(u) + neg(u),
                rest - pos(u) + neg(u_lo),
                rest - pos(u_hi) + neg(u),
                MIX + pos(u),
                MIX + pos(u_lo),
                MIX - neg(u),
                MIX - neg(u_hi),
                MIX + pos(v_lo),
                MIX - neg(v_hi),
            )
            for k, value in enumerate(values):
                e[LEV * (k + 1) + l, m] = jnp.where(inside, value, 1.0 if k < 3 else 0.0)

    def spread(p, m, i):
        lo, hi = (8 * i) // 10, min((8 * i + 7) // 10, 5)
        low = jnp.broadcast_to(e[p, m, lo : lo + 1, :], (8, 128))
        if lo == hi:
            return low
        high = jnp.broadcast_to(e[p, m, hi : hi + 1, :], (8, 128))
        return jnp.where(sub < 10 * hi - 8 * i, low, high)

    def at_row(value, p, m, i, last):
        for k in range(6):
            at = 10 * k + (9 if last else 0) - 8 * i
            if 0 <= at < 8:
                value = jnp.where(sub == at, jnp.broadcast_to(e[p, m, k : k + 1, :], (8, 128)), value)
        return value

    for i in range(8):
        q = slice(8 * i, 8 * i + 8)
        for m in range(3):
            for l in range(LEV - 1):
                kz[l, m, q, :] = spread(10 * LEV + l, m, i)
            for l in range(LEV):
                mid = at_row(spread(LEV + l, m, i), 2 * LEV + l, m, i, False)
                ac[l, m, q, :] = at_row(mid, 3 * LEV + l, m, i, True)
                am[l, m, q, :] = at_row(spread(4 * LEV + l, m, i), 5 * LEV + l, m, i, False)
                ap[l, m, q, :] = at_row(spread(6 * LEV + l, m, i), 7 * LEV + l, m, i, True)
                bm[l, m, q, :] = spread(8 * LEV + l, m, i)
                bp[l, m, q, :] = spread(9 * LEV + l, m, i)


    def lay(l, at, n, parts, turn):
        wide = lanes((n, 128))
        q = slice(at, at + n)
        raw[l, 0, q, :] = parts[0]
        raw[l, 1, q, :] = jnp.where(wide < 32, pltpu.roll(parts[0], 32, 1), pltpu.roll(parts[1], 32, 1))
        third = pltpu.roll(parts[2], 64, 1) if turn else parts[2]
        raw[l, 2, q, :] = jnp.where(wide < 64, pltpu.roll(parts[1], 64, 1), third)

    for l in range(LEV):
        last_part[l, :, 64:128] = nx[l, :, 256:320]
        lay(l, 10, OWN, (nx[l, :, 0:128], nx[l, :, 128:256], last_part[l]), False)
        for tile, at in ((prev_t, 0), (next_t, OWN + 10)):
            spots = (EDGE + 20 * l, EDGE + 20 * l + 10, EDGE + 80 + 10 * (l // 2))
            lay(l, at, 10, [got_tile[tile, k : k + 10, :] for k in spots], l % 2 == 0)
    last_row = RATIO * facts[7]
    first_row = OWN * t - 10
    for i in range(8):
        r = 8 + 8 * i
        row = first_row + 8 * i + sub
        row_in = (row >= 0) & (row < last_row)
        for m in range(3):
            col = columns(m, lane)
            active = row_in & (col >= 0) & (col < RATIO * facts[8])
            for l in range(LEV):
                c[0, l, m, r : r + 8, :] = jnp.where(active, raw[l, m, r - 8 : r, :], spread(l, m, i))

    def advance(old, new, tiles):
        for m in range(3):
            for i in tiles:
                r = 8 + 8 * i
                q = slice(8 * i, 8 * i + 8)
                now = [c[old, l, m, r : r + 8, :] for l in range(LEV)]
                flow = [kz[l, m, q, :] for l in range(LEV - 1)]
                for l in range(LEV):
                    value = ac[l, m, q, :] * now[l]
                    value = value + am[l, m, q, :] * c[old, l, m, r - 1 : r + 7, :]
                    value = value + ap[l, m, q, :] * c[old, l, m, r + 1 : r + 9, :]
                    value = value + bm[l, m, q, :] * pltpu.roll(now[l], 1, 1)
                    value = value + bp[l, m, q, :] * pltpu.roll(now[l], 127, 1)
                    if l > 0:
                        value = value + flow[l - 1] * now[l - 1]
                    if l < LEV - 1:
                        value = value + flow[l] * now[l + 1]
                    c[new, l, m, r : r + 8, :] = value

    def steps(count, tiles):
        def body(_, carry):
            advance(0, 1, tiles)
            advance(1, 0, tiles)
            return carry

        lax.fori_loop(0, count, body, 0)

    steps(2, range(8))
    steps(2, range(7))
    steps(1, range(1, 7))
    mean = jnp.zeros((48, 128), jnp.float32)
    wide = lanes((16, 128))
    for m in range(3):
        for l in range(LEV):
            total = c[0, l, m, pl.ds(18, 4, stride=10), :]
            for k in range(1, RATIO):
                total = total + c[0, l, m, pl.ds(18 + k, 4, stride=10), :]
            sums[m, 4 * l : 4 * l + 4, :] = total
        taken = (wide >= TAKEN[m] - STARTS[m]) & (wide < TAKEN[m + 1] - STARTS[m])
        value = jnp.where(taken, sums[m], 0.0)
        high = value.astype(jnp.bfloat16)
        value = value - high.astype(jnp.float32)
        middle = value.astype(jnp.bfloat16)
        low = (value - middle.astype(jnp.float32)).astype(jnp.bfloat16)
        away = lax.broadcasted_iota(jnp.int32, (128, 128), 0) + STARTS[m] - RATIO * lanes((128, 128))
        pick = jnp.where((away >= 0) & (away < RATIO), 1.0, 0.0).astype(jnp.bfloat16)
        parts = jnp.concatenate([high, middle, low], axis=0)
        mean = mean + jnp.dot(parts, pick, preferred_element_type=jnp.float32)
    mean = mean[0:16] + (mean[16:32] + mean[32:48])
    mean = mean * (1.0 / (RATIO * RATIO))
    lane4 = lanes((4, 128))
    value = jnp.zeros((4, 128), jnp.float32)
    turned = [mean if l == 0 else pltpu.roll(mean, 32 * l, 1) for l in range(LEV)]
    for l in range(LEV):
        inside = (lane4 >= 32 * l) & (lane4 < 32 * l + 32)
        value = jnp.where(inside, turned[l][4 * l : 4 * l + 4, :], value)
    tile_a = lax.div(facts[6], COLS)
    tile_b = jnp.where(tile_a < TILES - 1, tile_a + 1, tile_a - 1)
    slot[...] = value
    stores = [
        pltpu.make_async_copy(slot, back.at[TILES * src + tile], sems.at[k])
        for k, tile in enumerate((tile_a, tile_b))
    ]
    for store in stores:
        store.start()
    for store in stores:
        store.wait()


def finish_kernel(
    facts, got_tile, got_grp, c, so2, east, north, diff, stepped, fine_out, keep, px, vk, side, sems
):
    t = lax.axis_index("tile")
    g = lax.axis_index("grp")
    prev_t = jnp.maximum(t - 1, 0)
    next_t = jnp.minimum(t + 1, TILES - 1)
    prev_g = jnp.maximum(g - 1, 0)
    next_g = jnp.minimum(g + 1, GROUPS - 1)
    copies = [
        (so2, px.at[pl.ds(0, 4), pl.ds(8, ROWS), :]),
        (east, px.at[pl.ds(4, 4), pl.ds(8, ROWS), :]),
        (north, vk.at[pl.ds(0, 4)]),
        (diff, vk.at[pl.ds(4, 4)]),
    ]
    copies = [pltpu.make_async_copy(s, d, sems.at[i]) for i, (s, d) in enumerate(copies)]
    for copy in copies:
        copy.start()
    lane = lanes((8, 128))
    wide = lanes((OWN, 128))
    for l in range(LEV):
        middle = pltpu.roll(c[0, l, 1, 18:58, :], 96, 1)
        last = pltpu.roll(c[0, l, 2, 18:58, :], 64, 1)
        fine_out[0, l, :, 0:128] = jnp.where(wide < 117, c[0, l, 0, 18:58, :], middle)
        fine_out[0, l, :, 128:256] = jnp.where(wide < 75, middle, last)
        fine_out[0, l, :, 256:320] = last[:, 0:64]
    for copy in copies:
        copy.wait()
    for p in range(8):
        px[p, 7:8, :] = jnp.where(g > 0, got_grp[prev_g, WIN + p : WIN + p + 1, :], 0.0)
        px[p, 72:73, :] = jnp.where(g < GROUPS - 1, got_grp[next_g, WIN + p : WIN + p + 1, :], 0.0)
    here = lax.broadcasted_iota(jnp.int32, (8, 128), 0) == 0
    for k, (tile, there, at) in enumerate(((prev_t, t > 0, 0), (next_t, t < TILES - 1, 127))):
        put = jnp.where(here & (lane == at), 1.0, 0.0)
        for p in range(4):
            row = jnp.where(there, got_tile[tile, WIN + p : WIN + p + 1, :], 0.0)
            side[k, 128 * p : 128 * p + 128, :] = lax.dot_general(
                jnp.broadcast_to(row, (8, 128)),
                put,
                (((0,), (0,)), ((), ())),
                precision=lax.Precision.HIGHEST,
                preferred_element_type=jnp.float32,
            )
    for b in range(8):
        r = 8 + 8 * b
        q = slice(8 * b, 8 * b + 8)
        now = [px[l, r : r + 8, :] for l in range(LEV)]
        ks = [vk[4 + l, q, :] for l in range(LEV)]
        between = [0.5 * (ks[l] + ks[l + 1]) * (now[l + 1] - now[l]) for l in range(LEV - 1)]
        for l in range(LEV):
            here = now[l]
            at, vat = 64 * l + 8 * b, 256 + 64 * l + 8 * b
            wind = vk[l, q, :]
            c_w = jnp.where(lane == 0, side[0, at : at + 8, :], pltpu.roll(here, 1, 1))
            c_e = jnp.where(lane == 127, side[1, at : at + 8, :], pltpu.roll(here, 127, 1))
            v_w = jnp.where(lane == 0, side[0, vat : vat + 8, :], pltpu.roll(wind, 1, 1))
            v_e = jnp.where(lane == 127, side[1, vat : vat + 8, :], pltpu.roll(wind, 127, 1))
            c_n = px[l, r - 1 : r + 7, :]
            c_s = px[l, r + 1 : r + 9, :]
            flow = px[4 + l, r : r + 8, :]
            u_lo = 0.5 * (px[4 + l, r - 1 : r + 7, :] + flow)
            u_hi = 0.5 * (flow + px[4 + l, r + 1 : r + 9, :])
            v_lo = 0.5 * (v_w + wind)
            v_hi = 0.5 * (wind + v_e)
            value = (
                here
                - ((pos(u_hi) * here + neg(u_hi) * c_s) - (pos(u_lo) * c_n + neg(u_lo) * here))
                - ((pos(v_hi) * here + neg(v_hi) * c_e) - (pos(v_lo) * c_w + neg(v_lo) * here))
                + MIX * (c_n + c_s + c_w + c_e - 4.0 * here)
            )
            if l < LEV - 1:
                value = value + between[l]
            if l > 0:
                value = value - between[l - 1]
            stepped[l, q, :] = value
    off = facts[2]
    base = pl.multiple_of(lax.div(off, 8) * 8, 8)
    for l in range(LEV):
        keep[l] = stepped[l, pl.ds(base, 40), :]


def place_kernel(facts, stepped, keep, got, out, s, sems):
    t = lax.axis_index("tile")
    n, lf, wd = facts[0], facts[1], facts[4]

    @pl.when((lf < COLS * t + COLS) & (lf + wd > COLS * t))
    def _():
        off = facts[2]
        base = pl.multiple_of(lax.div(off, 8) * 8, 8)
        lane = lanes((FR, 128)) + COLS * t
        row = lax.broadcasted_iota(jnp.int32, (FR, 128), 0)
        covered = (lane >= lf) & (lane < lf + wd) & (row < facts[3])
        at = pl.ds(off - base, FR)
        for l in range(LEV):
            turned = pltpu.roll(got[n], lax.rem(lf - COLS * t - 32 * l + 2048, 128), 1)
            s[l] = keep[l]
            s[l, at, :] = jnp.where(covered, turned, keep[l, at, :])
        store = pltpu.make_async_copy(s, out.at[:, pl.ds(base, 40), :], sems.at[0])
        store.start()
        store.wait()


def shards(so2, east, north, diff, nest, rows, offs, left, height, width):
    f32 = jnp.float32
    shape = jax.ShapeDtypeStruct
    dma = pltpu.SemaphoreType.DMA
    field = functools.partial(pltpu.VMEM, dtype=f32)
    near = functools.partial(pltpu.with_memory_space_constraint, memory_space=pltpu.VMEM)
    scalar = functools.partial(pltpu.with_memory_space_constraint, memory_space=pltpu.SMEM)
    send, edges, facts, own = pl.pallas_call(
        pack_kernel,
        out_shape=(
            field((TILES, SLOT, 128)),
            field((16, 128)),
            pltpu.SMEM((16,), jnp.int32),
            field((LEV, OWN, WIDE)),
        ),
        in_specs=[ANY] * 10,
        out_specs=(VMEM, VMEM, SMEM, VMEM),
        scratch_shapes=[pltpu.SMEM((16,), jnp.int32)] * 5
        + [
            field((16, ROWS + 8, 128)),
            field((5, 40, 128)),
            dma((10,)),
        ],
        name="pack",
    )(rows, offs, left, height, width, so2, east, north, diff, nest)
    facts = scalar(facts)
    got_tile = near(lax.all_to_all(send, "tile", 0, 0))
    send = pl.pallas_call(
        merge_kernel,
        out_shape=field((GROUPS, GSLOT, 128)),
        in_specs=[SMEM, VMEM, VMEM],
        out_specs=VMEM,
        name="merge",
    )(facts, got_tile, near(edges))
    got_grp = near(lax.all_to_all(send, "grp", 0, 0))
    c, back = pl.pallas_call(
        fine_kernel,
        out_shape=(field((2, LEV, 3, 80, 128)), shape((GROUPS * TILES, 4, 128), f32)),
        in_specs=[SMEM] + [VMEM] * 3,
        out_specs=(VMEM, ANY),
        scratch_shapes=[
            field((4, 128)),
            field((LEV, OWN, 128)),
            field((11 * LEV - 1, 3, 8, 128)),
            field((LEV, 3, 64, 128)),
            field((LEV, 3, 64, 128)),
            field((LEV, 3, 64, 128)),
            field((LEV, 3, 64, 128)),
            field((LEV, 3, 64, 128)),
            field((LEV, 3, 64, 128)),
            field((LEV - 1, 3, 64, 128)),
            field((3, 16, 128)),
            dma((2,)),
        ],
        name="fine",
    )(facts, got_tile, got_grp, near(own))
    stepped, nest_next, keep = pl.pallas_call(
        finish_kernel,
        out_shape=(
            shape((LEV, ROWS, COLS), f32),
            shape((1, LEV, OWN, WIDE), f32),
            field((LEV, 40, 128)),
        ),
        in_specs=[SMEM] + [VMEM] * 3 + [ANY] * 4,
        out_specs=(VMEM, VMEM, VMEM),
        scratch_shapes=[
            field((8, ROWS + 16, 128)),
            field((8, ROWS, 128)),
            field((2, 512, 128)),
            dma((4,)),
        ],
        name="finish",
    )(facts, got_tile, got_grp, near(c), so2, east, north, diff)
    got = lax.all_to_all(back, ("grp", "tile"), 0, 0)
    got = near(got.reshape(GROUPS, FR, 128))
    parent_next = pl.pallas_call(
        place_kernel,
        out_shape=shape((LEV, ROWS, COLS), f32),
        in_specs=[SMEM, ANY, VMEM, VMEM],
        out_specs=ANY,
        scratch_shapes=[field((LEV, 40, 128)), dma((1,))],
        input_output_aliases={1: 0},
        name="place",
    )(facts, stepped, near(keep), got)
    return parent_next, nest_next


def solution(mesh):
    in_specs = (
        P(None, "grp", "tile"),
        P(None, "grp", "tile"),
        P(None, "grp", "tile"),
        P(None, "grp", "tile"),
        P("grp", None, "tile", None),
        P(),
        P(),
        P(),
        P(),
        P(),
    )
    out_specs = (P(None, "grp", "tile"), P("grp", None, "tile", None))
    return jax.shard_map(shards, mesh=mesh, in_specs=in_specs, out_specs=out_specs, check_vma=False)
```

```python
import functools
import jax
import jax.numpy as jnp
from jax import lax
from jax.experimental import pallas as pl
from jax.experimental.pallas import tpu as pltpu
from jax.sharding import PartitionSpec as P

RATIO = 10
FR = 32
LEV = 4
ROWS = 64
COLS = 128
OWN = 40
WIDE = 320
GROUPS = 16
TILES = 8
SPAN = FR + 2
WIN = 30
EDGE = 34
SLOT = 136
GSLOT = 40
STARTS = (0, 96, 192)
TAKEN = (0, 117, 203, 320)
MIX = 0.02

SMEM = pl.BlockSpec(memory_space=pltpu.SMEM)
ANY = pl.BlockSpec(memory_space=pl.ANY)
VMEM = pl.BlockSpec(memory_space=pltpu.VMEM)


def nest_over(rows, group):
    found = jnp.int32(0)
    for i in range(GROUPS):
        found = jnp.where(rows[i] == group, jnp.int32(i), found)
    return found


def lanes(shape):
    return lax.broadcasted_iota(jnp.int32, shape, 1)


def pack_kernel(
    rows_at, offs_at, left_at, height_at, width_at, so2, east, north, diff, nest,
    send, edges, facts, nx, picks,
    rows, offs, left, height, width, x, cut, sems,
):
    t = lax.axis_index("tile")
    g = lax.axis_index("grp")
    numbers = [
        pltpu.make_async_copy(s, d, sems.at[5 + i])
        for i, (s, d) in enumerate(
            ((rows_at, rows), (offs_at, offs), (left_at, left), (height_at, height), (width_at, width))
        )
    ]
    for c in numbers:
        c.start()
    loads = [
        pltpu.make_async_copy(f, x.at[pl.ds(4 * i, 4), pl.ds(0, ROWS), :], sems.at[i])
        for i, f in enumerate((so2, east, north, diff))
    ]
    loads.append(pltpu.make_async_copy(nest.at[0], nx, sems.at[4]))
    for k in (4, 0, 2, 1, 3):
        loads[k].start()
    for m in range(3):
        away = lax.broadcasted_iota(jnp.int32, (128, 128), 0) + STARTS[m] - RATIO * lanes((128, 128))
        picks[m] = jnp.where((away >= 0) & (away < RATIO), 1.0, 0.0).astype(jnp.bfloat16)
    for c in numbers:
        c.wait()
    n = nest_over(rows, g)
    facts[0] = n
    facts[1] = left[n]
    facts[2] = offs[n]
    facts[3] = height[n]
    facts[4] = width[n]
    facts[5] = rows[g]
    facts[6] = left[g]
    facts[7] = height[g]
    facts[8] = width[g]
    top = offs[n] - 1
    base = 128 * t + 1 - left[n] + 1024
    x[:, ROWS : ROWS + 8, :] = jnp.zeros((16, 8, 128), jnp.float32)
    lane = lanes((8, 128))
    before = jnp.where(t > 0, t - 1, t + 2)
    after = jnp.where(t < TILES - 1, t + 1, t - 2)
    loads[4].wait()
    for at, source in ((before, 0), (after, OWN - 10)):
        q = slice(source, source + 10)
        for l in range(LEV):
            for m in range(2):
                send[at, pl.ds(EDGE + 10 * (2 * l + m), 10), :] = nx[l, q, 128 * m : 128 * m + 128]
            side = 64 * (l % 2)
            send[at, pl.ds(EDGE + 80 + 10 * (l // 2), 10), side : side + 64] = nx[l, q, 256:320]
    loads[0].wait()
    loads[2].wait()
    sub = lax.broadcasted_iota(jnp.int32, (8, 128), 0)
    ends = jnp.where(((sub == 0) & (lane == 0)) | ((sub == 1) & (lane == 127)), 1.0, 0.0)
    planes = [x[p if p < 4 else p + 4, 0:ROWS, :] for p in range(8)]
    sides = lax.dot_general(
        ends,
        jnp.concatenate(planes, axis=0),
        (((1,), (1,)), ((), ())),
        precision=lax.Precision.HIGHEST,
        preferred_element_type=jnp.float32,
    )
    loads[1].wait()
    loads[3].wait()
    for l in range(LEV):
        edges[l : l + 1, :] = x[l, 0:1, :]
        edges[4 + l : 5 + l, :] = x[4 + l, 0:1, :]
        edges[8 + l : 9 + l, :] = x[l, ROWS - 1 : ROWS, :]
        edges[12 + l : 13 + l, :] = x[4 + l, ROWS - 1 : ROWS, :]
    shifts = [lax.rem(base + SPAN * f, 128) for f in range(3)]
    kshifts = [lax.rem(base + 32 * l - 1, 128) for l in range(LEV)]
    for b in range(5):
        at = pl.ds(top + 8 * b, 8)
        q = slice(8 * b, 8 * b + 8)
        for l in range(LEV):
            part = [pltpu.roll(x[4 * f + l, at, :], shifts[f], 1) for f in range(3)]
            cut[l, q, :] = jnp.where(lane < SPAN, part[0], jnp.where(lane < 2 * SPAN, part[1], part[2]))
        part = [pltpu.roll(x[12 + l, at, :], kshifts[l], 1) for l in range(LEV)]
        cut[4, q, :] = jnp.where(
            lane < 64,
            jnp.where(lane < 32, part[0], part[1]),
            jnp.where(lane < 96, part[2], part[3]),
        )
    for d in range(TILES):
        for l in range(5):
            send[d, 6 * l : 6 * l + 6, :] = cut[l, 4 * d : 4 * d + 6, :]
        for k in range(4):
            pair = sides[0:2, 128 * k : 128 * k + 128]
            send[d, WIN + k : WIN + k + 1, :] = jnp.where(d < t, pair[0:1], pair[1:2])


def merge_kernel(facts, got, edges, send):
    g = lax.axis_index("grp")
    n = facts[0]
    start = facts[1] - 1
    first = lax.div(start, COLS)
    second = jnp.minimum(first + 1, TILES - 1)
    send[jnp.where(g > 0, g - 1, g + 2), WIN : WIN + 8, :] = edges[0:8, :]
    send[jnp.where(g < GROUPS - 1, g + 1, g - 2), WIN : WIN + 8, :] = edges[8:16, :]
    room = COLS - (start - COLS * first)
    lane = lanes((8, 128))
    col = lane - jnp.where(lane >= SPAN, SPAN, 0) - jnp.where(lane >= 2 * SPAN, SPAN, 0)
    kcol = (lane & 31) + 1
    for l in range(3):
        q = slice(8 * l, 8 * l + 8)
        send[n, q, :] = jnp.where(col < room, got[first, q, :], got[second, q, :])
    q = slice(24, WIN)
    send[n, q, :] = jnp.where(kcol[0:6] < room, got[first, q, :], got[second, q, :])


def columns(chunk, lane):
    col = STARTS[chunk] + lane
    if chunk == 0:
        return jnp.where(lane == 127, -1, col)
    if chunk == 2:
        return jnp.where(lane == 0, WIDE, col)
    return col


def pos(v):
    return jnp.maximum(v, 0.0)


def neg(v):
    return jnp.minimum(v, 0.0)


def fine_kernel(
    facts, got_tile, got_grp, nx, picks,
    c, back,
    slot, last_part, e, raw, am, ap, bm, bp, ac, kz, sums, sems,
):
    t = lax.axis_index("tile")
    g = lax.axis_index("grp")
    src = facts[5]
    prev_t = jnp.maximum(t - 1, 0)
    next_t = jnp.minimum(t + 1, TILES - 1)
    lane = lanes((8, 128))
    sub = lax.broadcasted_iota(jnp.int32, (8, 128), 0)
    zero = jnp.zeros((8, 128), jnp.float32)
    for l in range(LEV):
        for m in range(3):
            raw[l, m, 56:64, :] = zero
            for p in range(2):
                c[p, l, m, 0:8, :] = zero
                c[p, l, m, 72:80, :] = zero

    above = OWN // RATIO * t - 1 + sub
    row_in = (above >= 0) & (above < facts[7])
    coarse = {}
    for m in range(3):
        col = columns(m, lane)
        under = (jnp.maximum(col, 0) * 6554) >> 16
        pick = jnp.where(col < 0, 0, jnp.where(col < WIDE, under + 1, SPAN - 1))
        kpick = jnp.minimum(under, FR - 1)
        inside = row_in & (col >= 0) & (col < RATIO * facts[8])
        block = got_grp[src, 24:32, :]
        ks = [jnp.take_along_axis(block, kpick + 32 * l, axis=1) for l in range(LEV)]
        faces = [0.05 * (ks[l] + ks[l + 1]) for l in range(LEV - 1)]
        for l in range(LEV - 1):
            e[10 * LEV + l, m] = jnp.where(inside, faces[l], 0.0)
        for l in range(LEV):
            block = got_grp[src, 6 * l : 6 * l + 8, :]
            e[l, m] = jnp.take_along_axis(block, pick, axis=1)
            u = jnp.take_along_axis(block, pick + SPAN, axis=1)
            v = jnp.take_along_axis(block, pick + 2 * SPAN, axis=1)
            u_lo = 0.5 * (pltpu.roll(u, 1, 0) + u)
            u_hi = 0.5 * (u + pltpu.roll(u, 7, 0))
            v_lo = 0.5 * (pltpu.roll(v, 1, 1) + v)
            v_hi = 0.5 * (v + pltpu.roll(v, 127, 1))
            rest = (1.0 - 4.0 * MIX) - pos(v_hi) + neg(v_lo)
            if l > 0:
                rest = rest - faces[l - 1]
            if l < LEV - 1:
                rest = rest - faces[l]
            values = (
                rest - pos(u) + neg(u),
                rest - pos(u) + neg(u_lo),
                rest - pos(u_hi) + neg(u),
                MIX + pos(u),
                MIX + pos(u_lo),
                MIX - neg(u),
                MIX - neg(u_hi),
                MIX + pos(v_lo),
                MIX - neg(v_hi),
            )
            for k, value in enumerate(values):
                e[LEV * (k + 1) + l, m] = jnp.where(inside, value, 1.0 if k < 3 else 0.0)

    def spread(p, m, i):
        lo, hi = (8 * i) // 10, min((8 * i + 7) // 10, 5)
        low = jnp.broadcast_to(e[p, m, lo : lo + 1, :], (8, 128))
        if lo == hi:
            return low
        high = jnp.broadcast_to(e[p, m, hi : hi + 1, :], (8, 128))
        return jnp.where(sub < 10 * hi - 8 * i, low, high)

    def at_row(value, p, m, i, last):
        for k in range(6):
            at = 10 * k + (9 if last else 0) - 8 * i
            if 0 <= at < 8:
                value = jnp.where(sub == at, jnp.broadcast_to(e[p, m, k : k + 1, :], (8, 128)), value)
        return value

    for i in range(8):
        q = slice(8 * i, 8 * i + 8)
        for m in range(3):
            for l in range(LEV - 1):
                kz[l, m, q, :] = spread(10 * LEV + l, m, i)
            for l in range(LEV):
                mid = at_row(spread(LEV + l, m, i), 2 * LEV + l, m, i, False)
                ac[l, m, q, :] = at_row(mid, 3 * LEV + l, m, i, True)
                am[l, m, q, :] = at_row(spread(4 * LEV + l, m, i), 5 * LEV + l, m, i, False)
                ap[l, m, q, :] = at_row(spread(6 * LEV + l, m, i), 7 * LEV + l, m, i, True)
                bm[l, m, q, :] = spread(8 * LEV + l, m, i)
                bp[l, m, q, :] = spread(9 * LEV + l, m, i)


    def lay(l, at, n, parts, turn):
        wide = lanes((n, 128))
        q = slice(at, at + n)
        raw[l, 0, q, :] = parts[0]
        raw[l, 1, q, :] = pltpu.roll(jnp.where(wide < 96, parts[1], parts[0]), 32, 1)
        if turn:
            raw[l, 2, q, :] = pltpu.roll(jnp.where(wide < 64, parts[2], parts[1]), 64, 1)
        else:
            raw[l, 2, q, :] = jnp.where(wide < 64, pltpu.roll(parts[1], 64, 1), parts[2])

    for l in range(LEV):
        last_part[l, :, 0:64] = nx[l, :, 256:320]
        lay(l, 10, OWN, (nx[l, :, 0:128], nx[l, :, 128:256], last_part[l]), True)
        for tile, at in ((prev_t, 0), (next_t, OWN + 10)):
            spots = (EDGE + 20 * l, EDGE + 20 * l + 10, EDGE + 80 + 10 * (l // 2))
            lay(l, at, 10, [got_tile[tile, k : k + 10, :] for k in spots], l % 2 == 0)
    last_row = RATIO * facts[7]
    first_row = OWN * t - 10
    for i in range(8):
        r = 8 + 8 * i
        row = first_row + 8 * i + sub
        row_in = (row >= 0) & (row < last_row)
        for m in range(3):
            col = columns(m, lane)
            active = row_in & (col >= 0) & (col < RATIO * facts[8])
            for l in range(LEV):
                c[0, l, m, r : r + 8, :] = jnp.where(active, raw[l, m, r - 8 : r, :], spread(l, m, i))

    def advance(old, new, tiles):
        for m in range(3):
            for i in tiles:
                r = 8 + 8 * i
                q = slice(8 * i, 8 * i + 8)
                now = [c[old, l, m, r : r + 8, :] for l in range(LEV)]
                flow = [kz[l, m, q, :] for l in range(LEV - 1)]
                for l in range(LEV):
                    value = ac[l, m, q, :] * now[l]
                    value = value + am[l, m, q, :] * c[old, l, m, r - 1 : r + 7, :]
                    value = value + ap[l, m, q, :] * c[old, l, m, r + 1 : r + 9, :]
                    value = value + bm[l, m, q, :] * pltpu.roll(now[l], 1, 1)
                    value = value + bp[l, m, q, :] * pltpu.roll(now[l], 127, 1)
                    if l > 0:
                        value = value + flow[l - 1] * now[l - 1]
                    if l < LEV - 1:
                        value = value + flow[l] * now[l + 1]
                    c[new, l, m, r : r + 8, :] = value

    def steps(count, tiles):
        def body(_, carry):
            advance(0, 1, tiles)
            advance(1, 0, tiles)
            return carry

        lax.fori_loop(0, count, body, 0)

    steps(2, range(8))
    steps(2, range(7))
    steps(1, range(1, 7))
    mean = jnp.zeros((48, 128), jnp.float32)
    wide = lanes((16, 128))
    for m in range(3):
        for l in range(LEV):
            total = c[0, l, m, pl.ds(18, 4, stride=10), :]
            for k in range(1, RATIO):
                total = total + c[0, l, m, pl.ds(18 + k, 4, stride=10), :]
            sums[m, 4 * l : 4 * l + 4, :] = total
        taken = (wide >= TAKEN[m] - STARTS[m]) & (wide < TAKEN[m + 1] - STARTS[m])
        value = jnp.where(taken, sums[m], 0.0)
        high = value.astype(jnp.bfloat16)
        value = value - high.astype(jnp.float32)
        middle = value.astype(jnp.bfloat16)
        low = (value - middle.astype(jnp.float32)).astype(jnp.bfloat16)
        parts = jnp.concatenate([high, middle, low], axis=0)
        mean = mean + jnp.dot(parts, picks[m], preferred_element_type=jnp.float32)
    mean = mean[0:16] + (mean[16:32] + mean[32:48])
    mean = mean * (1.0 / (RATIO * RATIO))
    lane4 = lanes((4, 128))
    value = jnp.zeros((4, 128), jnp.float32)
    turned = [mean if l == 0 else pltpu.roll(mean, 32 * l, 1) for l in range(LEV)]
    for l in range(LEV):
        inside = (lane4 >= 32 * l) & (lane4 < 32 * l + 32)
        value = jnp.where(inside, turned[l][4 * l : 4 * l + 4, :], value)
    tile_a = lax.div(facts[6], COLS)
    tile_b = jnp.where(tile_a < TILES - 1, tile_a + 1, tile_a - 1)
    slot[...] = value
    stores = [
        pltpu.make_async_copy(slot, back.at[TILES * src + tile], sems.at[k])
        for k, tile in enumerate((tile_a, tile_b))
    ]
    for store in stores:
        store.start()
    for store in stores:
        store.wait()


def finish_kernel(
    facts, got_tile, got_grp, c, so2, east, north, diff, stepped, fine_out, keep, px, vk, side, sems
):
    t = lax.axis_index("tile")
    g = lax.axis_index("grp")
    prev_t = jnp.maximum(t - 1, 0)
    next_t = jnp.minimum(t + 1, TILES - 1)
    prev_g = jnp.maximum(g - 1, 0)
    next_g = jnp.minimum(g + 1, GROUPS - 1)
    copies = [
        (so2, px.at[pl.ds(0, 4), pl.ds(8, ROWS), :]),
        (east, px.at[pl.ds(4, 4), pl.ds(8, ROWS), :]),
        (north, vk.at[pl.ds(0, 4)]),
        (diff, vk.at[pl.ds(4, 4)]),
    ]
    copies = [pltpu.make_async_copy(s, d, sems.at[i]) for i, (s, d) in enumerate(copies)]
    for copy in copies:
        copy.start()
    lane = lanes((8, 128))
    wide = lanes((OWN, 128))
    for l in range(LEV):
        middle = pltpu.roll(c[0, l, 1, 18:58, :], 96, 1)
        last = pltpu.roll(c[0, l, 2, 18:58, :], 64, 1)
        fine_out[0, l, :, 0:128] = jnp.where(wide < 117, c[0, l, 0, 18:58, :], middle)
        fine_out[0, l, :, 128:256] = jnp.where(wide < 75, middle, last)
        fine_out[0, l, :, 256:320] = last[:, 0:64]
    for copy in copies:
        copy.wait()
    for p in range(8):
        px[p, 7:8, :] = jnp.where(g > 0, got_grp[prev_g, WIN + p : WIN + p + 1, :], 0.0)
        px[p, 72:73, :] = jnp.where(g < GROUPS - 1, got_grp[next_g, WIN + p : WIN + p + 1, :], 0.0)
    here = lax.broadcasted_iota(jnp.int32, (8, 128), 0) == 0
    for k, (tile, there, at) in enumerate(((prev_t, t > 0, 0), (next_t, t < TILES - 1, 127))):
        put = jnp.where(here & (lane == at), 1.0, 0.0)
        for p in range(4):
            row = jnp.where(there, got_tile[tile, WIN + p : WIN + p + 1, :], 0.0)
            side[k, 128 * p : 128 * p + 128, :] = lax.dot_general(
                jnp.broadcast_to(row, (8, 128)),
                put,
                (((0,), (0,)), ((), ())),
                precision=lax.Precision.HIGHEST,
                preferred_element_type=jnp.float32,
            )
    for b in range(8):
        r = 8 + 8 * b
        q = slice(8 * b, 8 * b + 8)
        now = [px[l, r : r + 8, :] for l in range(LEV)]
        ks = [vk[4 + l, q, :] for l in range(LEV)]
        between = [0.5 * (ks[l] + ks[l + 1]) * (now[l + 1] - now[l]) for l in range(LEV - 1)]
        for l in range(LEV):
            here = now[l]
            at, vat = 64 * l + 8 * b, 256 + 64 * l + 8 * b
            wind = vk[l, q, :]
            c_w = jnp.where(lane == 0, side[0, at : at + 8, :], pltpu.roll(here, 1, 1))
            c_e = jnp.where(lane == 127, side[1, at : at + 8, :], pltpu.roll(here, 127, 1))
            v_w = jnp.where(lane == 0, side[0, vat : vat + 8, :], pltpu.roll(wind, 1, 1))
            v_e = jnp.where(lane == 127, side[1, vat : vat + 8, :], pltpu.roll(wind, 127, 1))
            c_n = px[l, r - 1 : r + 7, :]
            c_s = px[l, r + 1 : r + 9, :]
            flow = px[4 + l, r : r + 8, :]
            u_lo = 0.5 * (px[4 + l, r - 1 : r + 7, :] + flow)
            u_hi = 0.5 * (flow + px[4 + l, r + 1 : r + 9, :])
            v_lo = 0.5 * (v_w + wind)
            v_hi = 0.5 * (wind + v_e)
            value = (
                here
                - ((pos(u_hi) * here + neg(u_hi) * c_s) - (pos(u_lo) * c_n + neg(u_lo) * here))
                - ((pos(v_hi) * here + neg(v_hi) * c_e) - (pos(v_lo) * c_w + neg(v_lo) * here))
                + MIX * (c_n + c_s + c_w + c_e - 4.0 * here)
            )
            if l < LEV - 1:
                value = value + between[l]
            if l > 0:
                value = value - between[l - 1]
            stepped[l, q, :] = value
    off = facts[2]
    base = pl.multiple_of(lax.div(off, 8) * 8, 8)
    for l in range(LEV):
        keep[l] = stepped[l, pl.ds(base, 40), :]


def place_kernel(facts, stepped, keep, got, out, s, sems):
    t = lax.axis_index("tile")
    n, lf, wd = facts[0], facts[1], facts[4]

    @pl.when((lf < COLS * t + COLS) & (lf + wd > COLS * t))
    def _():
        off = facts[2]
        base = pl.multiple_of(lax.div(off, 8) * 8, 8)
        lane = lanes((FR, 128)) + COLS * t
        row = lax.broadcasted_iota(jnp.int32, (FR, 128), 0)
        covered = (lane >= lf) & (lane < lf + wd) & (row < facts[3])
        at = pl.ds(off - base, FR)
        for l in range(LEV):
            turned = pltpu.roll(got[n], lax.rem(lf - COLS * t - 32 * l + 2048, 128), 1)
            s[l] = keep[l]
            s[l, at, :] = jnp.where(covered, turned, keep[l, at, :])
        store = pltpu.make_async_copy(s, out.at[:, pl.ds(base, 40), :], sems.at[0])
        store.start()
        store.wait()


def shards(so2, east, north, diff, nest, rows, offs, left, height, width):
    f32 = jnp.float32
    shape = jax.ShapeDtypeStruct
    dma = pltpu.SemaphoreType.DMA
    field = functools.partial(pltpu.VMEM, dtype=f32)
    near = functools.partial(pltpu.with_memory_space_constraint, memory_space=pltpu.VMEM)
    scalar = functools.partial(pltpu.with_memory_space_constraint, memory_space=pltpu.SMEM)
    send, edges, facts, own, picks = pl.pallas_call(
        pack_kernel,
        out_shape=(
            field((TILES, SLOT, 128)),
            field((16, 128)),
            pltpu.SMEM((16,), jnp.int32),
            field((LEV, OWN, WIDE)),
            pltpu.VMEM((3, 128, 128), jnp.bfloat16),
        ),
        in_specs=[ANY] * 10,
        out_specs=(VMEM, VMEM, SMEM, VMEM, VMEM),
        scratch_shapes=[pltpu.SMEM((16,), jnp.int32)] * 5
        + [
            field((16, ROWS + 8, 128)),
            field((5, 40, 128)),
            dma((10,)),
        ],
        name="pack",
    )(rows, offs, left, height, width, so2, east, north, diff, nest)
    facts = scalar(facts)
    got_tile = near(lax.all_to_all(send, "tile", 0, 0))
    send = pl.pallas_call(
        merge_kernel,
        out_shape=field((GROUPS, GSLOT, 128)),
        in_specs=[SMEM, VMEM, VMEM],
        out_specs=VMEM,
        name="merge",
    )(facts, got_tile, near(edges))
    got_grp = near(lax.all_to_all(send, "grp", 0, 0))
    c, back = pl.pallas_call(
        fine_kernel,
        out_shape=(field((2, LEV, 3, 80, 128)), shape((GROUPS * TILES, 4, 128), f32)),
        in_specs=[SMEM] + [VMEM] * 4,
        out_specs=(VMEM, ANY),
        scratch_shapes=[
            field((4, 128)),
            field((LEV, OWN, 128)),
            field((11 * LEV - 1, 3, 8, 128)),
            field((LEV, 3, 64, 128)),
            field((LEV, 3, 64, 128)),
            field((LEV, 3, 64, 128)),
            field((LEV, 3, 64, 128)),
            field((LEV, 3, 64, 128)),
            field((LEV, 3, 64, 128)),
            field((LEV - 1, 3, 64, 128)),
            field((3, 16, 128)),
            dma((2,)),
        ],
        name="fine",
    )(facts, got_tile, got_grp, near(own), near(picks))
    stepped, nest_next, keep = pl.pallas_call(
        finish_kernel,
        out_shape=(
            shape((LEV, ROWS, COLS), f32),
            shape((1, LEV, OWN, WIDE), f32),
            field((LEV, 40, 128)),
        ),
        in_specs=[SMEM] + [VMEM] * 3 + [ANY] * 4,
        out_specs=(VMEM, VMEM, VMEM),
        scratch_shapes=[
            field((8, ROWS + 16, 128)),
            field((8, ROWS, 128)),
            field((2, 512, 128)),
            dma((4,)),
        ],
        name="finish",
    )(facts, got_tile, got_grp, near(c), so2, east, north, diff)
    got = lax.all_to_all(back, ("grp", "tile"), 0, 0)
    got = near(got.reshape(GROUPS, FR, 128))
    parent_next = pl.pallas_call(
        place_kernel,
        out_shape=shape((LEV, ROWS, COLS), f32),
        in_specs=[SMEM, ANY, VMEM, VMEM],
        out_specs=ANY,
        scratch_shapes=[field((LEV, 40, 128)), dma((1,))],
        input_output_aliases={1: 0},
        name="place",
    )(facts, stepped, near(keep), got)
    return parent_next, nest_next


def solution(mesh):
    in_specs = (
        P(None, "grp", "tile"),
        P(None, "grp", "tile"),
        P(None, "grp", "tile"),
        P(None, "grp", "tile"),
        P("grp", None, "tile", None),
        P(),
        P(),
        P(),
        P(),
        P(),
    )
    out_specs = (P(None, "grp", "tile"), P("grp", None, "tile", None))
    return jax.shard_map(shards, mesh=mesh, in_specs=in_specs, out_specs=out_specs, check_vma=False)
```

```python
import functools
import jax
import jax.numpy as jnp
from jax import lax
from jax.experimental import pallas as pl
from jax.experimental.pallas import tpu as pltpu
from jax.sharding import PartitionSpec as P

RATIO = 10
FR = 32
LEV = 4
ROWS = 64
COLS = 128
OWN = 40
WIDE = 320
GROUPS = 16
TILES = 8
SPAN = FR + 2
WIN = 30
EDGE = 34
SLOT = 136
GSLOT = 40
STARTS = (0, 96, 192)
TAKEN = (0, 117, 203, 320)
MIX = 0.02

SMEM = pl.BlockSpec(memory_space=pltpu.SMEM)
ANY = pl.BlockSpec(memory_space=pl.ANY)
VMEM = pl.BlockSpec(memory_space=pltpu.VMEM)


def nest_over(rows, group):
    found = jnp.int32(0)
    for i in range(GROUPS):
        found = jnp.where(rows[i] == group, jnp.int32(i), found)
    return found


def lanes(shape):
    return lax.broadcasted_iota(jnp.int32, shape, 1)


def pack_kernel(
    rows_at, offs_at, left_at, height_at, width_at, so2, east, north, diff, nest,
    send, edges, facts, nx, picks,
    rows, offs, left, height, width, x, cut, sems,
):
    t = lax.axis_index("tile")
    g = lax.axis_index("grp")
    numbers = [
        pltpu.make_async_copy(s, d, sems.at[5 + i])
        for i, (s, d) in enumerate(
            ((rows_at, rows), (offs_at, offs), (left_at, left), (height_at, height), (width_at, width))
        )
    ]
    for c in numbers:
        c.start()
    loads = [
        pltpu.make_async_copy(f, x.at[pl.ds(4 * i, 4), pl.ds(0, ROWS), :], sems.at[i])
        for i, f in enumerate((so2, east, north, diff))
    ]
    loads.append(pltpu.make_async_copy(nest.at[0], nx, sems.at[4]))
    for k in (4, 0, 2, 1, 3):
        loads[k].start()
    for m in range(3):
        away = lax.broadcasted_iota(jnp.int32, (128, 128), 0) + STARTS[m] - RATIO * lanes((128, 128))
        picks[m] = jnp.where((away >= 0) & (away < RATIO), 1.0, 0.0).astype(jnp.bfloat16)
    for c in numbers:
        c.wait()
    n = nest_over(rows, g)
    facts[0] = n
    facts[1] = left[n]
    facts[2] = offs[n]
    facts[3] = height[n]
    facts[4] = width[n]
    facts[5] = rows[g]
    facts[6] = left[g]
    facts[7] = height[g]
    facts[8] = width[g]
    top = offs[n] - 1
    base = 128 * t + 1 - left[n] + 1024
    x[:, ROWS : ROWS + 8, :] = jnp.zeros((16, 8, 128), jnp.float32)
    lane = lanes((8, 128))
    before = jnp.where(t > 0, t - 1, t + 2)
    after = jnp.where(t < TILES - 1, t + 1, t - 2)
    loads[4].wait()
    for at, source in ((before, 0), (after, OWN - 10)):
        q = slice(source, source + 10)
        for l in range(LEV):
            for m in range(2):
                send[at, pl.ds(EDGE + 10 * (2 * l + m), 10), :] = nx[l, q, 128 * m : 128 * m + 128]
            side = 64 * (l % 2)
            send[at, pl.ds(EDGE + 80 + 10 * (l // 2), 10), side : side + 64] = nx[l, q, 256:320]
    loads[0].wait()
    loads[2].wait()
    sub = lax.broadcasted_iota(jnp.int32, (8, 128), 0)
    ends = jnp.where(((sub == 0) & (lane == 0)) | ((sub == 1) & (lane == 127)), 1.0, 0.0)
    planes = [x[p if p < 4 else p + 4, 0:ROWS, :] for p in range(8)]
    sides = lax.dot_general(
        ends,
        jnp.concatenate(planes, axis=0),
        (((1,), (1,)), ((), ())),
        precision=lax.Precision.HIGHEST,
        preferred_element_type=jnp.float32,
    )
    loads[1].wait()
    loads[3].wait()
    for l in range(LEV):
        edges[l : l + 1, :] = x[l, 0:1, :]
        edges[4 + l : 5 + l, :] = x[4 + l, 0:1, :]
        edges[8 + l : 9 + l, :] = x[l, ROWS - 1 : ROWS, :]
        edges[12 + l : 13 + l, :] = x[4 + l, ROWS - 1 : ROWS, :]
    shifts = [lax.rem(base + SPAN * f, 128) for f in range(3)]
    kshifts = [lax.rem(base + 32 * l - 1, 128) for l in range(LEV)]
    for b in range(5):
        at = pl.ds(top + 8 * b, 8)
        q = slice(8 * b, 8 * b + 8)
        for l in range(LEV):
            part = [pltpu.roll(x[4 * f + l, at, :], shifts[f], 1) for f in range(3)]
            cut[l, q, :] = jnp.where(lane < SPAN, part[0], jnp.where(lane < 2 * SPAN, part[1], part[2]))
        part = [pltpu.roll(x[12 + l, at, :], kshifts[l], 1) for l in range(LEV)]
        cut[4, q, :] = jnp.where(
            lane < 64,
            jnp.where(lane < 32, part[0], part[1]),
            jnp.where(lane < 96, part[2], part[3]),
        )
    for d in range(TILES):
        for l in range(5):
            send[d, 6 * l : 6 * l + 6, :] = cut[l, 4 * d : 4 * d + 6, :]
        for k in range(4):
            pair = sides[0:2, 128 * k : 128 * k + 128]
            send[d, WIN + k : WIN + k + 1, :] = jnp.where(d < t, pair[0:1], pair[1:2])


def merge_kernel(facts, got, edges, send):
    g = lax.axis_index("grp")
    n = facts[0]
    start = facts[1] - 1
    first = lax.div(start, COLS)
    second = jnp.minimum(first + 1, TILES - 1)
    send[jnp.where(g > 0, g - 1, g + 2), WIN : WIN + 8, :] = edges[0:8, :]
    send[jnp.where(g < GROUPS - 1, g + 1, g - 2), WIN : WIN + 8, :] = edges[8:16, :]
    room = COLS - (start - COLS * first)
    lane = lanes((8, 128))
    col = lane - jnp.where(lane >= SPAN, SPAN, 0) - jnp.where(lane >= 2 * SPAN, SPAN, 0)
    kcol = (lane & 31) + 1
    for l in range(3):
        q = slice(8 * l, 8 * l + 8)
        send[n, q, :] = jnp.where(col < room, got[first, q, :], got[second, q, :])
    q = slice(24, WIN)
    send[n, q, :] = jnp.where(kcol[0:6] < room, got[first, q, :], got[second, q, :])


def columns(chunk, lane):
    col = STARTS[chunk] + lane
    if chunk == 0:
        return jnp.where(lane == 127, -1, col)
    if chunk == 2:
        return jnp.where(lane == 0, WIDE, col)
    return col


def pos(v):
    return jnp.maximum(v, 0.0)


def neg(v):
    return jnp.minimum(v, 0.0)


def fine_kernel(
    facts, got_tile, got_grp, nx, picks,
    c, back,
    slot, last_part, e, raw, am, ap, bm, bp, ac, kz, sums, sems,
):
    t = lax.axis_index("tile")
    g = lax.axis_index("grp")
    src = facts[5]
    prev_t = jnp.maximum(t - 1, 0)
    next_t = jnp.minimum(t + 1, TILES - 1)
    lane = lanes((8, 128))
    sub = lax.broadcasted_iota(jnp.int32, (8, 128), 0)
    zero = jnp.zeros((8, 128), jnp.float32)
    for l in range(LEV):
        for m in range(3):
            raw[l, m, 56:64, :] = zero
            for p in range(2):
                c[p, l, m, 0:8, :] = zero
                c[p, l, m, 72:80, :] = zero

    above = OWN // RATIO * t - 1 + sub
    row_in = (above >= 0) & (above < facts[7])
    coarse = {}
    for m in range(3):
        col = columns(m, lane)
        under = (jnp.maximum(col, 0) * 6554) >> 16
        pick = jnp.where(col < 0, 0, jnp.where(col < WIDE, under + 1, SPAN - 1))
        kpick = jnp.minimum(under, FR - 1)
        inside = row_in & (col >= 0) & (col < RATIO * facts[8])
        block = got_grp[src, 24:32, :]
        ks = [jnp.take_along_axis(block, kpick + 32 * l, axis=1) for l in range(LEV)]
        faces = [0.05 * (ks[l] + ks[l + 1]) for l in range(LEV - 1)]
        for l in range(LEV - 1):
            e[10 * LEV + l, m] = jnp.where(inside, faces[l], 0.0)
        for l in range(LEV):
            block = got_grp[src, 6 * l : 6 * l + 8, :]
            e[l, m] = jnp.take_along_axis(block, pick, axis=1)
            u = jnp.take_along_axis(block, pick + SPAN, axis=1)
            v = jnp.take_along_axis(block, pick + 2 * SPAN, axis=1)
            u_lo = 0.5 * (pltpu.roll(u, 1, 0) + u)
            u_hi = 0.5 * (u + pltpu.roll(u, 7, 0))
            v_lo = 0.5 * (pltpu.roll(v, 1, 1) + v)
            v_hi = 0.5 * (v + pltpu.roll(v, 127, 1))
            rest = (1.0 - 4.0 * MIX) - pos(v_hi) + neg(v_lo)
            if l > 0:
                rest = rest - faces[l - 1]
            if l < LEV - 1:
                rest = rest - faces[l]
            values = (
                rest - pos(u) + neg(u),
                rest - pos(u) + neg(u_lo),
                rest - pos(u_hi) + neg(u),
                MIX + pos(u),
                MIX + pos(u_lo),
                MIX - neg(u),
                MIX - neg(u_hi),
                MIX + pos(v_lo),
                MIX - neg(v_hi),
            )
            for k, value in enumerate(values):
                e[LEV * (k + 1) + l, m] = jnp.where(inside, value, 1.0 if k < 3 else 0.0)

    def spread(p, m, i):
        lo, hi = (8 * i) // 10, min((8 * i + 7) // 10, 5)
        low = jnp.broadcast_to(e[p, m, lo : lo + 1, :], (8, 128))
        if lo == hi:
            return low
        high = jnp.broadcast_to(e[p, m, hi : hi + 1, :], (8, 128))
        return jnp.where(sub < 10 * hi - 8 * i, low, high)

    def at_row(value, p, m, i, last):
        for k in range(6):
            at = 10 * k + (9 if last else 0) - 8 * i
            if 0 <= at < 8:
                value = jnp.where(sub == at, jnp.broadcast_to(e[p, m, k : k + 1, :], (8, 128)), value)
        return value

    for i in range(8):
        q = slice(8 * i, 8 * i + 8)
        for m in range(3):
            for l in range(LEV - 1):
                kz[l, m, q, :] = spread(10 * LEV + l, m, i)
            for l in range(LEV):
                mid = at_row(spread(LEV + l, m, i), 2 * LEV + l, m, i, False)
                ac[l, m, q, :] = at_row(mid, 3 * LEV + l, m, i, True)
                am[l, m, q, :] = at_row(spread(4 * LEV + l, m, i), 5 * LEV + l, m, i, False)
                ap[l, m, q, :] = at_row(spread(6 * LEV + l, m, i), 7 * LEV + l, m, i, True)
                bm[l, m, q, :] = spread(8 * LEV + l, m, i)
                bp[l, m, q, :] = spread(9 * LEV + l, m, i)


    def lay(l, at, n, parts, turn):
        wide = lanes((n, 128))
        q = slice(at, at + n)
        raw[l, 0, q, :] = parts[0]
        raw[l, 1, q, :] = pltpu.roll(jnp.where(wide < 96, parts[1], parts[0]), 32, 1)
        if turn:
            raw[l, 2, q, :] = pltpu.roll(jnp.where(wide < 64, parts[2], parts[1]), 64, 1)
        else:
            raw[l, 2, q, :] = jnp.where(wide < 64, pltpu.roll(parts[1], 64, 1), parts[2])

    for l in range(LEV):
        last_part[l, :, 0:64] = nx[l, :, 256:320]
        lay(l, 10, OWN, (nx[l, :, 0:128], nx[l, :, 128:256], last_part[l]), True)
        for tile, at in ((prev_t, 0), (next_t, OWN + 10)):
            spots = (EDGE + 20 * l, EDGE + 20 * l + 10, EDGE + 80 + 10 * (l // 2))
            lay(l, at, 10, [got_tile[tile, k : k + 10, :] for k in spots], l % 2 == 0)
    last_row = RATIO * facts[7]
    first_row = OWN * t - 10
    for i in range(8):
        r = 8 + 8 * i
        row = first_row + 8 * i + sub
        row_in = (row >= 0) & (row < last_row)
        for m in range(3):
            col = columns(m, lane)
            active = row_in & (col >= 0) & (col < RATIO * facts[8])
            for l in range(LEV):
                c[0, l, m, r : r + 8, :] = jnp.where(active, raw[l, m, r - 8 : r, :], spread(l, m, i))

    def advance(old, new, tiles):
        for m in range(3):
            for i in tiles:
                r = 8 + 8 * i
                q = slice(8 * i, 8 * i + 8)
                now = [c[old, l, m, r : r + 8, :] for l in range(LEV)]
                flow = [kz[l, m, q, :] for l in range(LEV - 1)]
                for l in range(LEV):
                    value = ac[l, m, q, :] * now[l]
                    value = value + am[l, m, q, :] * c[old, l, m, r - 1 : r + 7, :]
                    value = value + ap[l, m, q, :] * c[old, l, m, r + 1 : r + 9, :]
                    value = value + bm[l, m, q, :] * pltpu.roll(now[l], 1, 1)
                    value = value + bp[l, m, q, :] * pltpu.roll(now[l], 127, 1)
                    if l > 0:
                        value = value + flow[l - 1] * now[l - 1]
                    if l < LEV - 1:
                        value = value + flow[l] * now[l + 1]
                    c[new, l, m, r : r + 8, :] = value

    for k in range(RATIO):
        advance(k % 2, 1 - k % 2, range(0 if k < 7 else 1, 8 if k < 3 else 7))
    mean = jnp.zeros((48, 128), jnp.float32)
    wide = lanes((16, 128))
    for m in range(3):
        for l in range(LEV):
            total = c[0, l, m, pl.ds(18, 4, stride=10), :]
            for k in range(1, RATIO):
                total = total + c[0, l, m, pl.ds(18 + k, 4, stride=10), :]
            sums[m, 4 * l : 4 * l + 4, :] = total
        taken = (wide >= TAKEN[m] - STARTS[m]) & (wide < TAKEN[m + 1] - STARTS[m])
        value = jnp.where(taken, sums[m], 0.0)
        high = value.astype(jnp.bfloat16)
        value = value - high.astype(jnp.float32)
        middle = value.astype(jnp.bfloat16)
        low = (value - middle.astype(jnp.float32)).astype(jnp.bfloat16)
        parts = jnp.concatenate([high, middle, low], axis=0)
        mean = mean + jnp.dot(parts, picks[m], preferred_element_type=jnp.float32)
    mean = mean[0:16] + (mean[16:32] + mean[32:48])
    mean = mean * (1.0 / (RATIO * RATIO))
    lane4 = lanes((4, 128))
    value = jnp.zeros((4, 128), jnp.float32)
    turned = [mean if l == 0 else pltpu.roll(mean, 32 * l, 1) for l in range(LEV)]
    for l in range(LEV):
        inside = (lane4 >= 32 * l) & (lane4 < 32 * l + 32)
        value = jnp.where(inside, turned[l][4 * l : 4 * l + 4, :], value)
    tile_a = lax.div(facts[6], COLS)
    tile_b = jnp.where(tile_a < TILES - 1, tile_a + 1, tile_a - 1)
    slot[...] = value
    stores = [
        pltpu.make_async_copy(slot, back.at[TILES * src + tile], sems.at[k])
        for k, tile in enumerate((tile_a, tile_b))
    ]
    for store in stores:
        store.start()
    for store in stores:
        store.wait()


def finish_kernel(
    facts, got_tile, got_grp, c, so2, east, north, diff, stepped, fine_out, keep, px, vk, side, sems
):
    t = lax.axis_index("tile")
    g = lax.axis_index("grp")
    prev_t = jnp.maximum(t - 1, 0)
    next_t = jnp.minimum(t + 1, TILES - 1)
    prev_g = jnp.maximum(g - 1, 0)
    next_g = jnp.minimum(g + 1, GROUPS - 1)
    copies = [
        (so2, px.at[pl.ds(0, 4), pl.ds(8, ROWS), :]),
        (east, px.at[pl.ds(4, 4), pl.ds(8, ROWS), :]),
        (north, vk.at[pl.ds(0, 4)]),
        (diff, vk.at[pl.ds(4, 4)]),
    ]
    copies = [pltpu.make_async_copy(s, d, sems.at[i]) for i, (s, d) in enumerate(copies)]
    for copy in copies:
        copy.start()
    lane = lanes((8, 128))
    wide = lanes((OWN, 128))
    for l in range(LEV):
        middle = pltpu.roll(c[0, l, 1, 18:58, :], 96, 1)
        last = pltpu.roll(c[0, l, 2, 18:58, :], 64, 1)
        fine_out[0, l, :, 0:128] = jnp.where(wide < 117, c[0, l, 0, 18:58, :], middle)
        fine_out[0, l, :, 128:256] = jnp.where(wide < 75, middle, last)
        fine_out[0, l, :, 256:320] = last[:, 0:64]
    for copy in copies:
        copy.wait()
    for p in range(8):
        px[p, 7:8, :] = jnp.where(g > 0, got_grp[prev_g, WIN + p : WIN + p + 1, :], 0.0)
        px[p, 72:73, :] = jnp.where(g < GROUPS - 1, got_grp[next_g, WIN + p : WIN + p + 1, :], 0.0)
    here = lax.broadcasted_iota(jnp.int32, (8, 128), 0) == 0
    for k, (tile, there, at) in enumerate(((prev_t, t > 0, 0), (next_t, t < TILES - 1, 127))):
        put = jnp.where(here & (lane == at), 1.0, 0.0)
        for p in range(4):
            row = jnp.where(there, got_tile[tile, WIN + p : WIN + p + 1, :], 0.0)
            side[k, 128 * p : 128 * p + 128, :] = lax.dot_general(
                jnp.broadcast_to(row, (8, 128)),
                put,
                (((0,), (0,)), ((), ())),
                precision=lax.Precision.HIGHEST,
                preferred_element_type=jnp.float32,
            )
    for b in range(8):
        r = 8 + 8 * b
        q = slice(8 * b, 8 * b + 8)
        now = [px[l, r : r + 8, :] for l in range(LEV)]
        ks = [vk[4 + l, q, :] for l in range(LEV)]
        between = [0.5 * (ks[l] + ks[l + 1]) * (now[l + 1] - now[l]) for l in range(LEV - 1)]
        for l in range(LEV):
            here = now[l]
            at, vat = 64 * l + 8 * b, 256 + 64 * l + 8 * b
            wind = vk[l, q, :]
            c_w = jnp.where(lane == 0, side[0, at : at + 8, :], pltpu.roll(here, 1, 1))
            c_e = jnp.where(lane == 127, side[1, at : at + 8, :], pltpu.roll(here, 127, 1))
            v_w = jnp.where(lane == 0, side[0, vat : vat + 8, :], pltpu.roll(wind, 1, 1))
            v_e = jnp.where(lane == 127, side[1, vat : vat + 8, :], pltpu.roll(wind, 127, 1))
            c_n = px[l, r - 1 : r + 7, :]
            c_s = px[l, r + 1 : r + 9, :]
            flow = px[4 + l, r : r + 8, :]
            u_lo = 0.5 * (px[4 + l, r - 1 : r + 7, :] + flow)
            u_hi = 0.5 * (flow + px[4 + l, r + 1 : r + 9, :])
            v_lo = 0.5 * (v_w + wind)
            v_hi = 0.5 * (wind + v_e)
            value = (
                here
                - ((pos(u_hi) * here + neg(u_hi) * c_s) - (pos(u_lo) * c_n + neg(u_lo) * here))
                - ((pos(v_hi) * here + neg(v_hi) * c_e) - (pos(v_lo) * c_w + neg(v_lo) * here))
                + MIX * (c_n + c_s + c_w + c_e - 4.0 * here)
            )
            if l < LEV - 1:
                value = value + between[l]
            if l > 0:
                value = value - between[l - 1]
            stepped[l, q, :] = value
    off = facts[2]
    base = pl.multiple_of(lax.div(off, 8) * 8, 8)
    for l in range(LEV):
        keep[l] = stepped[l, pl.ds(base, 40), :]


def place_kernel(facts, stepped, keep, got, out, s, sems):
    t = lax.axis_index("tile")
    n, lf, wd = facts[0], facts[1], facts[4]

    @pl.when((lf < COLS * t + COLS) & (lf + wd > COLS * t))
    def _():
        off = facts[2]
        base = pl.multiple_of(lax.div(off, 8) * 8, 8)
        lane = lanes((FR, 128)) + COLS * t
        row = lax.broadcasted_iota(jnp.int32, (FR, 128), 0)
        covered = (lane >= lf) & (lane < lf + wd) & (row < facts[3])
        at = pl.ds(off - base, FR)
        for l in range(LEV):
            turned = pltpu.roll(got[n], lax.rem(lf - COLS * t - 32 * l + 2048, 128), 1)
            s[l] = keep[l]
            s[l, at, :] = jnp.where(covered, turned, keep[l, at, :])
        store = pltpu.make_async_copy(s, out.at[:, pl.ds(base, 40), :], sems.at[0])
        store.start()
        store.wait()


def shards(so2, east, north, diff, nest, rows, offs, left, height, width):
    f32 = jnp.float32
    shape = jax.ShapeDtypeStruct
    dma = pltpu.SemaphoreType.DMA
    field = functools.partial(pltpu.VMEM, dtype=f32)
    near = functools.partial(pltpu.with_memory_space_constraint, memory_space=pltpu.VMEM)
    scalar = functools.partial(pltpu.with_memory_space_constraint, memory_space=pltpu.SMEM)
    send, edges, facts, own, picks = pl.pallas_call(
        pack_kernel,
        out_shape=(
            field((TILES, SLOT, 128)),
            field((16, 128)),
            pltpu.SMEM((16,), jnp.int32),
            field((LEV, OWN, WIDE)),
            pltpu.VMEM((3, 128, 128), jnp.bfloat16),
        ),
        in_specs=[ANY] * 10,
        out_specs=(VMEM, VMEM, SMEM, VMEM, VMEM),
        scratch_shapes=[pltpu.SMEM((16,), jnp.int32)] * 5
        + [
            field((16, ROWS + 8, 128)),
            field((5, 40, 128)),
            dma((10,)),
        ],
        name="pack",
    )(rows, offs, left, height, width, so2, east, north, diff, nest)
    facts = scalar(facts)
    got_tile = near(lax.all_to_all(send, "tile", 0, 0))
    send = pl.pallas_call(
        merge_kernel,
        out_shape=field((GROUPS, GSLOT, 128)),
        in_specs=[SMEM, VMEM, VMEM],
        out_specs=VMEM,
        name="merge",
    )(facts, got_tile, near(edges))
    got_grp = near(lax.all_to_all(send, "grp", 0, 0))
    c, back = pl.pallas_call(
        fine_kernel,
        out_shape=(field((2, LEV, 3, 80, 128)), shape((GROUPS * TILES, 4, 128), f32)),
        in_specs=[SMEM] + [VMEM] * 4,
        out_specs=(VMEM, ANY),
        scratch_shapes=[
            field((4, 128)),
            field((LEV, OWN, 128)),
            field((11 * LEV - 1, 3, 8, 128)),
            field((LEV, 3, 64, 128)),
            field((LEV, 3, 64, 128)),
            field((LEV, 3, 64, 128)),
            field((LEV, 3, 64, 128)),
            field((LEV, 3, 64, 128)),
            field((LEV, 3, 64, 128)),
            field((LEV - 1, 3, 64, 128)),
            field((3, 16, 128)),
            dma((2,)),
        ],
        name="fine",
    )(facts, got_tile, got_grp, near(own), near(picks))
    stepped, nest_next, keep = pl.pallas_call(
        finish_kernel,
        out_shape=(
            shape((LEV, ROWS, COLS), f32),
            shape((1, LEV, OWN, WIDE), f32),
            field((LEV, 40, 128)),
        ),
        in_specs=[SMEM] + [VMEM] * 3 + [ANY] * 4,
        out_specs=(VMEM, VMEM, VMEM),
        scratch_shapes=[
            field((8, ROWS + 16, 128)),
            field((8, ROWS, 128)),
            field((2, 512, 128)),
            dma((4,)),
        ],
        name="finish",
    )(facts, got_tile, got_grp, near(c), so2, east, north, diff)
    got = lax.all_to_all(back, ("grp", "tile"), 0, 0)
    got = near(got.reshape(GROUPS, FR, 128))
    parent_next = pl.pallas_call(
        place_kernel,
        out_shape=shape((LEV, ROWS, COLS), f32),
        in_specs=[SMEM, ANY, VMEM, VMEM],
        out_specs=ANY,
        scratch_shapes=[field((LEV, 40, 128)), dma((1,))],
        input_output_aliases={1: 0},
        name="place",
    )(facts, stepped, near(keep), got)
    return parent_next, nest_next


def solution(mesh):
    in_specs = (
        P(None, "grp", "tile"),
        P(None, "grp", "tile"),
        P(None, "grp", "tile"),
        P(None, "grp", "tile"),
        P("grp", None, "tile", None),
        P(),
        P(),
        P(),
        P(),
        P(),
    )
    out_specs = (P(None, "grp", "tile"), P("grp", None, "tile", None))
    return jax.shard_map(shards, mesh=mesh, in_specs=in_specs, out_specs=out_specs, check_vma=False)
```
